32 devices in a mesh: grp: 4 (over z), mem: 8 (over y, x, core).
Axes of the slice: x: 2, y: 2, z: 4, core: 2. Of those that a mesh axis runs over, the one named last changes fastest.
Arguments:
- node_memory: bfloat16 [262144, 256], P(('grp', 'mem')), may hold values from -41 to 41
- last_update: int32 [262144], P(('grp', 'mem')), may hold values from 0 to 4095
- evt_src: int32 [65536], P(('grp', 'mem')), may hold values from 0 to 8191
- evt_dst: int32 [65536], P(('grp', 'mem')), may hold values from 0 to 8191
- evt_time: int32 [65536], P(('grp', 'mem')), may hold values from 0 to 4095
- evt_counts: int32 [32, 32], P(('grp', 'mem')), may hold values from 1 to 64, as said below
- time_freq: float32 [128], replicated, may hold values from 0.001 to 0.3
- time_phase: float32 [128], replicated, may hold values from -3.140625 to 3.140625
- msg_weight: bfloat16 [384, 768], replicated, may hold values from -0.25 to 0.25
- mem_weight: bfloat16 [256, 1536], replicated, may hold values from -0.375 to 0.375
- gru_bias: float32 [768], replicated, may hold values from -4 to 4
- qry_rows: int32 [8192], P(('grp', 'mem')), may hold values from 0 to 8191
- qry_time: int32 [8192], P(('grp', 'mem')), may hold values from 0 to 4095
- nbr_time: int32 [8192, 20], P(('grp', 'mem')), may hold values from 0 to 4095
- nbr_slot: int32 [32, 5120], P(('grp', 'mem')), may hold values from 0 to 5119, each once within a row
- req_rows: int32 [163840], P(('grp', 'mem')), may hold values from 0 to 8191
- query_weight: bfloat16 [256, 256], replicated, may hold values from -0.375 to 0.375
- kv_weight: bfloat16 [384, 512], replicated, may hold values from -0.3125 to 0.3125
- out_weight: bfloat16 [512, 256], replicated, may hold values from -0.25 to 0.25
Outputs:
- new_memory: bfloat16 [262144, 256], P(('grp', 'mem'))
- embeddings: bfloat16 [8192, 256], P(('grp', 'mem'))
The draws below stay inside these ranges and needn't reach their ends.
Inputs may be any that keep to these rules, and one draw needn't show every extreme that they name: `evt_counts`: entry [s, o] counts the live slots among the 64 slots that sender s holds for owner o; in every draw one owner receives 64 live slots from every sender.
All inputs are finite; a program needn't handle non-finite values.
Results may differ from the reference program's by a relative error of at most 0.0048.
Values may be sent and summed in bfloat16 or wider, within the bound.
No kernel may reach another device: no remote copies, remote signals or barrier semaphores. Data moves between devices by JAX's collectives and lax.ppermute only.
A program may use at most 128 MiB of HBM per device.

```python
import math
import jax
import jax.numpy as jnp
import numpy as np
from jax import lax

D = 256
TIME_DIM = 128
HEADS = 2
NEIGHBOURS = 20
NODE_DEV = 8192
EVT_DEV = 2048
QRY_DEV = 256
SLOT_CAP = 64
NODES = 262144
EVENTS = 65536
QUERIES = 8192
DEVICES = 32


def draw_evt_counts(key, part):
    key_one, key_two = jax.random.split(jax.random.fold_in(key, 11))
    counts = jax.random.randint(key_one, (DEVICES, DEVICES), 1, SLOT_CAP + 1)
    hottest = jax.random.randint(key_two, (), 0, DEVICES)
    column = jnp.arange(DEVICES)[None, :]
    return jnp.where(column == hottest, SLOT_CAP, counts).astype(jnp.int32)


def draw_node_memory(key, part):
    key_one = jax.random.fold_in(jax.random.fold_in(key, 23), 0)
    array_shape = (NODE_DEV * DEVICES, D)
    return jnp.clip(jax.random.normal(key_one, array_shape, jnp.float32), -4.0, 4.0).astype(jnp.bfloat16)


def plant(result, rng, low, high):
    longest = result.shape.index(max(result.shape))
    spots = []
    for shift in (0, 1):
        where = [jax.random.randint(jax.random.fold_in(rng, axis), (), 0, length) for axis, length in enumerate(result.shape)]
        where[longest] = (where[longest] + shift) % result.shape[longest]
        spots.append(tuple(where))
    return result.at[spots[0]].set(low).at[spots[1]].set(high)


def cumulative_ranks(count, slope):
    weights = [(1 << 20) // math.isqrt(rank ** slope) + 1 for rank in range(1, count + 1)]
    width = 1 + sum(weights) // (1 << 30)
    return np.cumsum(np.array([max(1, weight // width) for weight in weights]))


def ranked(own_key, shape, number_of, slope):
    grid = cumulative_ranks(number_of, slope)
    lot = jax.random.randint(jax.random.fold_in(own_key, 1), shape, 0, int(grid[number_of - 1]))
    rank = jnp.searchsorted(jnp.asarray(grid, jnp.int32), lot, side="right")
    return jax.random.permutation(jax.random.fold_in(own_key, 2), number_of)[rank].astype(jnp.int32)


def bell_draw(key, shape, deviation, reach, kind=jnp.bfloat16):
    return jnp.clip(deviation * jax.random.normal(key, shape, jnp.float32), -reach, reach).astype(kind)


def setup_inputs(seed: int = 0) -> dict:
    splits = jax.random.split(jax.random.key(seed), 20)
    node_memory = draw_node_memory(jax.random.fold_in(splits[19], 71), 0)
    last_update = plant(jax.random.randint(splits[1], (NODES,), 0, 4096), jax.random.fold_in(splits[1], 1), 0, 4095).astype(jnp.int32)
    evt_src = plant(jax.random.randint(splits[2], (EVENTS,), 0, NODE_DEV), jax.random.fold_in(splits[2], 1), 0, NODE_DEV - 1).astype(jnp.int32)
    evt_dst = plant(ranked(splits[3], (EVENTS,), NODE_DEV, 2), jax.random.fold_in(splits[3], 3), 0, NODE_DEV - 1).astype(jnp.int32)
    evt_time = plant(jax.random.randint(splits[4], (EVENTS,), 0, 4096), jax.random.fold_in(splits[4], 1), 0, 4095).astype(jnp.int32)
    evt_counts = draw_evt_counts(jax.random.fold_in(splits[19], 71), 0)
    time_freq = jnp.clip(jnp.exp(jax.random.uniform(splits[6], (TIME_DIM,), jnp.float32, math.log(0.001), math.log(0.3))), 0.001, 0.3)
    time_phase = jnp.clip(jax.random.uniform(splits[7], (TIME_DIM,), jnp.float32, -3.140625, 3.140625), -3.140625, 3.140625)
    msg_weight = bell_draw(splits[8], (D + TIME_DIM, 3 * D), (2 * D + TIME_DIM) ** -0.5, 0.25)
    mem_weight = bell_draw(splits[9], (D, 6 * D), D ** -0.5, 0.375)
    gru_bias = bell_draw(splits[10], (3 * D,), 1.0, 4.0, jnp.float32)
    qry_rows = plant(jax.random.randint(splits[11], (QUERIES,), 0, NODE_DEV), jax.random.fold_in(splits[11], 1), 0, NODE_DEV - 1).astype(jnp.int32)
    qry_time = plant(jax.random.randint(splits[12], (QUERIES,), 0, 4096), jax.random.fold_in(splits[12], 1), 0, 4095).astype(jnp.int32)
    nbr_time = plant(jax.random.randint(splits[13], (QUERIES, NEIGHBOURS), 0, 4096), jax.random.fold_in(splits[13], 1), 0, 4095).astype(jnp.int32)
    nbr_slot = jax.vmap(lambda own: jax.random.permutation(own, QRY_DEV * NEIGHBOURS))(jax.random.split(splits[14], DEVICES)).reshape((DEVICES, QRY_DEV * NEIGHBOURS)).astype(jnp.int32)
    req_rows = plant(jax.random.randint(splits[15], (DEVICES * QRY_DEV * NEIGHBOURS,), 0, NODE_DEV), jax.random.fold_in(splits[15], 1), 0, NODE_DEV - 1).astype(jnp.int32)
    query_weight = bell_draw(splits[16], (D, D), D ** -0.5, 0.375)
    kv_weight = bell_draw(splits[17], (D + TIME_DIM, 2 * D), (D + TIME_DIM) ** -0.5, 0.3125)
    out_weight = bell_draw(splits[18], (2 * D, D), (2 * D) ** -0.5, 0.25)
    return dict(node_memory=node_memory, last_update=last_update, evt_src=evt_src, evt_dst=evt_dst, evt_time=evt_time, evt_counts=evt_counts, time_freq=time_freq, time_phase=time_phase, msg_weight=msg_weight, mem_weight=mem_weight, gru_bias=gru_bias, qry_rows=qry_rows, qry_time=qry_time, nbr_time=nbr_time, nbr_slot=nbr_slot, req_rows=req_rows, query_weight=query_weight, kv_weight=kv_weight, out_weight=out_weight)


def encode(time_delta, time_freq, time_phase):
    return jnp.cos(time_delta[..., None] * time_freq + time_phase)

def gru_rows(aggregate, memory, msg_weight, mem_weight, gru_bias, mem_width):
    input_part = jnp.dot(aggregate, msg_weight, preferred_element_type=jnp.float32) + gru_bias
    joined = jnp.dot(memory, mem_weight, preferred_element_type=jnp.float32)
    input_part = input_part + joined[:, :3 * mem_width]
    hidden_part = joined[:, 3 * mem_width:]
    reset_gate = jax.nn.sigmoid(input_part[:, :mem_width] + hidden_part[:, :mem_width])
    update_gate = jax.nn.sigmoid(input_part[:, mem_width:2 * mem_width] + hidden_part[:, mem_width:2 * mem_width])
    candidate = jnp.tanh(input_part[:, 2 * mem_width:] + reset_gate * hidden_part[:, 2 * mem_width:])
    return (1.0 - update_gate) * candidate + update_gate * memory.astype(jnp.float32)

def attend(query_mem, neighbour_mem, time_delta, time_freq, time_phase, query_weight, kv_weight, out_weight):
    queries, fan_out, mem_width = neighbour_mem.shape
    head_dim = mem_width // HEADS
    encoding = encode(time_delta, time_freq, time_phase).astype(jnp.bfloat16)
    key_input = jnp.concatenate([neighbour_mem, encoding], axis=-1).reshape(queries * fan_out, -1)
    key_value = jnp.dot(key_input, kv_weight, preferred_element_type=jnp.float32)
    key_rows = key_value[:, :mem_width].reshape(queries, fan_out, HEADS, head_dim)
    value_rows = key_value[:, mem_width:].reshape(queries, fan_out, HEADS, head_dim)
    query_vec = jnp.dot(query_mem, query_weight, preferred_element_type=jnp.float32).reshape(queries, HEADS, head_dim)
    scores = jnp.einsum('qhd,qkhd->qhk', query_vec, key_rows, precision=lax.Precision.HIGHEST) / math.sqrt(head_dim)
    weights = jax.nn.softmax(scores, axis=-1)
    attended = jnp.einsum('qhk,qkhd->qhd', weights, value_rows, precision=lax.Precision.HIGHEST)
    attended = attended.reshape(queries, mem_width).astype(jnp.bfloat16)
    joined = jnp.concatenate([attended, query_mem], axis=-1)
    return jnp.dot(joined, out_weight, preferred_element_type=jnp.float32).astype(jnp.bfloat16)

def reference(node_memory, last_update, evt_src, evt_dst, evt_time, evt_counts, time_freq, time_phase, msg_weight, mem_weight, gru_bias, qry_rows, qry_time, nbr_time, nbr_slot, req_rows, query_weight, kv_weight, out_weight):
    devices = DEVICES
    slot_cap = EVT_DEV // devices
    anchor = jnp.arange(devices, dtype=jnp.int32)[:, None] * NODE_DEV
    src_node = anchor + evt_src.reshape(devices, EVT_DEV)
    is_live = jnp.arange(slot_cap, dtype=jnp.int32)[None, None, :] < evt_counts[:, :, None]

    def by_owner(tensor):
        return jnp.swapaxes(tensor.reshape(devices, devices, slot_cap), 0, 1).reshape(devices, devices * slot_cap)

    def update_owner(inputs):
        src_ids, dst_rows, evt_times, alive_mask, memory, last_seen = inputs
        src_rows = node_memory[src_ids].astype(jnp.float32)
        time_delta = (evt_times - last_seen[dst_rows]).astype(jnp.float32)
        encoding = encode(time_delta, time_freq, time_phase)
        weight = alive_mask.astype(jnp.float32)[:, None]
        msg_sums = jax.ops.segment_sum(jnp.concatenate([src_rows, encoding], axis=1) * weight, dst_rows, num_segments=NODE_DEV)
        touches = jax.ops.segment_sum(alive_mask.astype(jnp.int32), dst_rows, num_segments=NODE_DEV)
        aggregate = (msg_sums / jnp.maximum(touches, 1).astype(jnp.float32)[:, None]).astype(jnp.bfloat16)
        updated = gru_rows(aggregate, memory, msg_weight, mem_weight, gru_bias, D)
        return jnp.where(touches[:, None] > 0, updated, memory.astype(jnp.float32)).astype(jnp.bfloat16)
    new_memory = lax.map(update_owner, (by_owner(src_node), by_owner(evt_dst), by_owner(evt_time), by_owner(is_live), node_memory.reshape(devices, NODE_DEV, D), last_update.reshape(devices, NODE_DEV)))
    new_memory = new_memory.reshape(devices * NODE_DEV, D)
    total_slots = QRY_DEV * NEIGHBOURS
    req_cap = total_slots // devices

    def embed_device(inputs):
        device, slot_order, asked_rows, query_rows, query_time, neighbour_time = inputs
        owner = slot_order // req_cap
        nodes = owner * NODE_DEV + asked_rows[slot_order]
        neighbour_mem = new_memory[nodes].reshape(QRY_DEV, NEIGHBOURS, D)
        query_mem = new_memory[device * NODE_DEV + query_rows]
        time_delta = (query_time[:, None] - neighbour_time).astype(jnp.float32)
        return attend(query_mem, neighbour_mem, time_delta, time_freq, time_phase, query_weight, kv_weight, out_weight)
    embeddings = lax.map(embed_device, (jnp.arange(devices, dtype=jnp.int32), nbr_slot, req_rows.reshape(devices, total_slots), qry_rows.reshape(devices, QRY_DEV), qry_time.reshape(devices, QRY_DEV), nbr_time.reshape(devices, QRY_DEV, NEIGHBOURS)))
    return (new_memory, embeddings.reshape(devices * QRY_DEV, D))
```

```python
import functools
import math

import jax
import jax.numpy as jnp
from jax import lax
from jax.experimental import pallas as pl
from jax.experimental.pallas import tpu as pltpu
from jax.sharding import PartitionSpec as P

HEADS = 2
AXES = ("grp", "mem")
LANES = 128
UNROLL = 32
CHUNKS = 8
NEG = -1e30
TIME_BITS = 12
f32 = jnp.float32
bf16 = jnp.bfloat16
i32 = jnp.int32
VM = pl.BlockSpec(memory_space=pltpu.VMEM)
SM = pl.BlockSpec(memory_space=pltpu.SMEM)
ANY = pl.BlockSpec(memory_space=pl.ANY)


def dot(a, b):
    return jnp.dot(a, b, preferred_element_type=f32)


def dot_nt(a, b):
    return lax.dot_general(a, b, (((1,), (1,)), ((), ())), preferred_element_type=f32)


def split(x):
    high = x.astype(bf16)
    return high, (x - high.astype(f32)).astype(bf16)


def cosine(x):
    turns = jnp.round(x * (1.0 / math.pi))
    r = x - turns * 3.140625
    r = r - turns * 9.675025939941406e-4
    r = r - turns * 1.5099579909783764e-7
    s = r * r
    p = -2.755731922398589e-7 + s * 2.08767569878681e-9
    p = 2.48015873015873e-5 + s * p
    p = -1.3888888888888889e-3 + s * p
    p = 4.1666666666666664e-2 + s * p
    p = -0.5 + s * p
    p = 1.0 + s * p
    half = turns * 0.5
    odd = half - jnp.floor(half)
    return p * (1.0 - 4.0 * odd)


def params(mib):
    return pltpu.CompilerParams(vmem_limit_bytes=mib << 20)


def cost(flops, nbytes):
    return pl.CostEstimate(flops=int(flops), bytes_accessed=int(nbytes), transcendentals=0)


def move_rows(count, load, store):
    def body(t, carry):
        base = pl.multiple_of(t * UNROLL, UNROLL)
        for part in range(0, UNROLL, 16):
            rows = [load(base + part + u) for u in range(16)]
            for u in range(16):
                store(base + part + u, rows[u])
        return carry

    lax.fori_loop(0, count // UNROLL, body, 0)


def pack_rows(count, src, src_base, dst, dst_base):
    def body(t, carry):
        r = pl.multiple_of(t * 16, 16)
        for half in range(2):
            dst[pl.ds(dst_base + r, 16), half * LANES : (half + 1) * LANES] = src[
                pl.ds(2 * (src_base + r) + half, 16, stride=2), :
            ].astype(bf16)
        return carry

    lax.fori_loop(0, count // 16, body, 0, unroll=4)


def source_kernel(idx, memory, rows_out, table_out, raw, table, stage, in_sem, out_sem):
    nodes = memory.shape[0]
    step = nodes // CHUNKS
    loads = [
        pltpu.make_async_copy(
            memory.at[pl.ds(c * step, step)], raw.at[pl.ds(c * step, step)], in_sem.at[c]
        )
        for c in range(CHUNKS)
    ]
    saves = [
        pltpu.make_async_copy(
            table.at[pl.ds(2 * c * step, 2 * step)],
            table_out.at[pl.ds(2 * c * step, 2 * step)],
            out_sem.at[c],
        )
        for c in range(CHUNKS)
    ]
    for copy in loads:
        copy.start()
    for c in range(CHUNKS):
        loads[c].wait()

        def widen(t, carry):
            r = pl.multiple_of(c * step + t * 16, 16)
            rows = raw[pl.ds(r, 16), :].astype(f32)
            for half in range(2):
                table[pl.ds(2 * r + half, 16, stride=2), :] = rows[
                    :, half * LANES : (half + 1) * LANES
                ]
            return carry

        lax.fori_loop(0, step // 16, widen, 0, unroll=8)
        saves[c].start()

    def put(k, row):
        stage[pl.ds(2 * k, 2), :] = row

    move_rows(idx.shape[0], lambda k: table[pl.ds(2 * idx[k], 2), :], put)
    pack_rows(idx.shape[0], stage, 0, rows_out, 0)
    for copy in saves:
        copy.wait()


def gather_sources(evt_src, node_memory):
    nodes, width = node_memory.shape
    events = evt_src.shape[0]
    return pl.pallas_call(
        source_kernel,
        out_shape=(
            jax.ShapeDtypeStruct((events, width), bf16),
            jax.ShapeDtypeStruct((2 * nodes, LANES), f32),
        ),
        in_specs=[SM, ANY],
        out_specs=(VM, ANY),
        scratch_shapes=[
            pltpu.VMEM((nodes, width), bf16),
            pltpu.VMEM((2 * nodes, LANES), f32),
            pltpu.VMEM((2 * events, LANES), f32),
            pltpu.SemaphoreType.DMA((CHUNKS,)),
            pltpu.SemaphoreType.DMA((CHUNKS,)),
        ],
        compiler_params=params(24),
        cost_estimate=cost(0, 20e6),
        name="source_rows",
    )(evt_src, node_memory)


def prepare_kernel(
    dst_s,
    seen_s,
    table_hbm,
    dst_row,
    dst_col,
    time_row,
    freq,
    phase,
    msg_weight,
    mem_weight,
    bias,
    pre_out,
    inv_out,
    rows_out,
    table,
    stage,
    seen_pick,
    seen_row,
    codes,
    sem,
):
    events = dst_s.shape[0]
    width = rows_out.shape[1]
    code_width = freq.shape[0]
    load = pltpu.make_async_copy(table_hbm, table, sem.at[0])
    load.start()

    def look(t, carry):
        base = t * 8
        at = [dst_s[base + u] for u in range(8)]
        got = [seen_s[a] for a in at]
        for u in range(8):
            seen_pick[0, base + u] = got[u]
        return carry

    lax.fori_loop(0, events // 8, look, 0)
    across = pltpu.make_async_copy(seen_pick, seen_row, sem.at[1])
    across.start()
    load.wait()

    def put(k, row):
        stage[pl.ds(2 * k, 2), :] = row

    move_rows(events, lambda k: table[pl.ds(2 * dst_s[k], 2), :], put)
    pack_rows(events, stage, 0, rows_out, 0)
    across.wait()
    step = 256
    for t in range(events // step):
        delta = (time_row[:, pl.ds(t * step, step)] - seen_row[:, pl.ds(t * step, step)]).astype(f32)
        codes[pl.ds(0, code_width), pl.ds(t * step, step)] = cosine(
            freq[...] * delta + phase[...]
        ).astype(bf16)
    codes[pl.ds(code_width, LANES), :] = jnp.ones((LANES, events), bf16)

    def block(t, carry):
        r = pl.multiple_of(t * step, step)
        same = jnp.where(dst_col[pl.ds(r, step), :] == dst_row[...], 1.0, 0.0).astype(bf16)
        sums = dot_nt(same, codes[...])
        inv = 1.0 / jnp.maximum(sums[:, code_width:], 1.0)
        code_agg = (sums[:, :code_width] * inv).astype(bf16)
        inv_out[pl.ds(r, step), :] = inv
        memory = rows_out[pl.ds(r, step), :]
        part = dot(code_agg, msg_weight[pl.ds(width, code_width), :]) + bias[...]
        joined = dot(memory, mem_weight[...])
        third = 3 * width
        pre_out[pl.ds(r, step), : 2 * width] = (
            part[:, : 2 * width] + joined[:, : 2 * width] + joined[:, third : third + 2 * width]
        )
        pre_out[pl.ds(r, step), 2 * width : third] = (
            part[:, 2 * width :] + joined[:, 2 * width : third]
        )
        pre_out[pl.ds(r, step), third:] = joined[:, third + 2 * width :]
        return carry

    lax.fori_loop(0, events // step, block, 0)


def prepare(dst, last_update, table, dst_row, dst_col, time_row, freq, phase, msg_weight, mem_weight, bias):
    events = dst.shape[0]
    width = mem_weight.shape[0]
    return pl.pallas_call(
        prepare_kernel,
        out_shape=(
            jax.ShapeDtypeStruct((events, 4 * width), f32),
            jax.ShapeDtypeStruct((events, LANES), f32),
            jax.ShapeDtypeStruct((events, width), bf16),
        ),
        in_specs=[SM, SM, ANY] + [VM] * 8,
        out_specs=(VM, VM, VM),
        scratch_shapes=[
            pltpu.VMEM(table.shape, f32),
            pltpu.VMEM((2 * events, LANES), f32),
            pltpu.SMEM((1, events), i32),
            pltpu.VMEM((1, events), i32),
            pltpu.VMEM((freq.shape[0] + LANES, events), bf16),
            pltpu.SemaphoreType.DMA((2,)),
        ],
        compiler_params=params(40),
        cost_estimate=cost(6e9, 30e6),
        name="prepare",
    )(dst, last_update, table, dst_row, dst_col, time_row, freq, phase, msg_weight, mem_weight, bias)


def update_kernel(
    dst_s,
    req_s,
    qry_s,
    table_hbm,
    got,
    dst_row,
    dst_col,
    pre,
    inv,
    rows,
    msg_weight,
    found_hbm,
    query_out,
    table_out,
    table,
    updated,
    stage,
    packed,
    sem,
    out_sem,
):
    step_id = pl.program_id(0)
    nodes2 = table_hbm.shape[0]
    step, width = rows.shape
    load = pltpu.make_async_copy(table_hbm, table.at[pl.ds(0, nodes2)], sem.at[0])

    @pl.when(step_id == 0)
    def _():
        load.start()

    same = jnp.where(dst_col[...] == dst_row[...], 1.0, 0.0).astype(bf16)
    sums = dot(same, got[...])
    scale = inv[...]
    agg = jnp.concatenate(
        [sums[:, h * LANES : (h + 1) * LANES] * scale for h in range(width // LANES)], axis=1
    ).astype(bf16)
    msg = dot(agg, msg_weight[pl.ds(0, width), :])
    reset = jax.nn.sigmoid(msg[:, :width] + pre[:, :width])
    gate = jax.nn.sigmoid(msg[:, width : 2 * width] + pre[:, width : 2 * width])
    cand = jnp.tanh(msg[:, 2 * width :] + pre[:, 2 * width : 3 * width] + reset * pre[:, 3 * width :])
    new = (1.0 - gate) * cand + gate * rows[...].astype(f32)
    new = new.astype(bf16).astype(f32)
    base = pl.multiple_of(2 * step * step_id, 2 * step)
    for half in range(2):
        updated[pl.ds(base + half, step, stride=2), :] = new[:, half * LANES : (half + 1) * LANES]

    @pl.when(step_id == pl.num_programs(0) - 1)
    def _():
        load.wait()

        def put_table(k, row):
            table[pl.ds(2 * dst_s[k], 2), :] = row

        move_rows(dst_s.shape[0], lambda k: updated[pl.ds(2 * k, 2), :], put_table)
        save = pltpu.make_async_copy(table.at[pl.ds(0, nodes2)], table_out, sem.at[0])
        save.start()

        def put(k, row):
            stage[pl.ds(2 * k, 2), :] = row

        queries = qry_s.shape[0]
        move_rows(queries, lambda k: table[pl.ds(2 * qry_s[k], 2), :], put)
        pack_rows(queries, stage, 0, query_out, 0)
        total = req_s.shape[0]
        chunk = total // 4
        sends = []
        for c in range(4):
            move_rows(chunk, lambda k: table[pl.ds(req_s[c * chunk + k], 2), :], put)
            pack_rows(chunk, stage, 0, packed, c * chunk)
            send = pltpu.make_async_copy(
                packed.at[pl.ds(c * chunk, chunk)],
                found_hbm.at[pl.ds(c * chunk, chunk)],
                out_sem.at[c],
            )
            send.start()
            sends.append(send)
        for send in sends:
            send.wait()
        save.wait()


def update(dst, req2, qry_rows, table, got, dst_row, dst_col, pre, inv, rows, msg_weight):
    events, width = got.shape
    step = 256
    whole = lambda a: pl.BlockSpec(a.shape, lambda t: (0,) * a.ndim, pipeline_mode=pl.Buffered(1))
    block = lambda a: pl.BlockSpec((step, a.shape[1]), lambda t: (t, 0))
    queries = qry_rows.shape[0]
    total = req2.shape[0]
    return pl.pallas_call(
        update_kernel,
        grid=(events // step,),
        out_shape=(
            jax.ShapeDtypeStruct((total, width), bf16),
            jax.ShapeDtypeStruct((queries, width), bf16),
            jax.ShapeDtypeStruct(table.shape, f32),
        ),
        in_specs=[SM, SM, SM, ANY, whole(got), whole(dst_row), block(dst_col), block(pre), block(inv), block(rows), whole(msg_weight)],
        out_specs=(ANY, pl.BlockSpec((queries, width), lambda t: (0, 0)), ANY),
        scratch_shapes=[
            pltpu.VMEM((table.shape[0] + 16, LANES), f32),
            pltpu.VMEM((2 * events, LANES), f32),
            pltpu.VMEM((2 * (total // 4), LANES), f32),
            pltpu.VMEM((total, width), bf16),
            pltpu.SemaphoreType.DMA((1,)),
            pltpu.SemaphoreType.DMA((4,)),
        ],
        compiler_params=params(36),
        cost_estimate=cost(4e9, 40e6),
        name="update",
    )(dst, req2, qry_rows, table, got, dst_row, dst_col, pre, inv, rows, msg_weight)


def narrow_kernel(table, out):
    pack_rows(out.shape[0], table, 0, out, 0)


def narrow(table):
    nodes = table.shape[0] // 2
    step = nodes // 8
    return pl.pallas_call(
        narrow_kernel,
        grid=(8,),
        out_shape=jax.ShapeDtypeStruct((nodes, 2 * LANES), bf16),
        in_specs=[pl.BlockSpec((2 * step, LANES), lambda t: (t, 0))],
        out_specs=pl.BlockSpec((step, 2 * LANES), lambda t: (t, 0)),
        compiler_params=params(16),
        cost_estimate=cost(0, 12e6),
        name="narrow",
    )(table)


def invert_kernel(slot_s, value_s, out_s):
    def body(t, carry):
        base = t * 8
        at = [slot_s[base + u] for u in range(8)]
        value = [value_s[base + u] for u in range(8)]
        for u in range(8):
            out_s[at[u]] = value[u]
        return carry

    lax.fori_loop(0, slot_s.shape[0] // 8, body, 0)


def invert(slots, values):
    return pl.pallas_call(
        invert_kernel,
        out_shape=jax.ShapeDtypeStruct(slots.shape, i32),
        in_specs=[SM, SM],
        out_specs=SM,
        cost_estimate=cost(0, 20e6),
        name="invert",
    )(slots, values)


def project_kernel(shift, query, info, freq, phase, query_weight, kv_weight, qx_out, qe_out, et_out):
    width = query_weight.shape[0]
    head_dim = width // HEADS
    queries = query.shape[0]
    vec = dot(query[...], query_weight[...]) * (1.0 / math.sqrt(head_dim))
    for h in range(HEADS):
        high, low = split(vec[:, h * head_dim : (h + 1) * head_dim])
        keys = kv_weight[:, h * head_dim : (h + 1) * head_dim]
        folded = dot_nt(high, keys) + dot_nt(low, keys)
        parts = split(folded)
        for k in range(2):
            rows = pl.ds((2 * h + k) * queries, queries)
            qx_out[rows, :] = parts[k][:, :width]
            qe_out[rows, :] = parts[k][:, width:]
    step = 256
    slots = info.shape[1]
    for t in range(slots // step):
        delta = ((info[:, pl.ds(t * step, step)] >> shift) - (1 << TIME_BITS)).astype(f32)
        et_out[:, pl.ds(t * step, step)] = cosine(freq[...] * delta + phase[...]).astype(bf16)


def project(shift, query, info, freq, phase, query_weight, kv_weight):
    queries, width = query.shape
    slots = info.shape[1]
    code_width = freq.shape[0]
    return pl.pallas_call(
        functools.partial(project_kernel, shift),
        out_shape=(
            jax.ShapeDtypeStruct((2 * HEADS * queries, width), bf16),
            jax.ShapeDtypeStruct((2 * HEADS * queries, code_width), bf16),
            jax.ShapeDtypeStruct((code_width, slots), bf16),
        ),
        in_specs=[VM] * 6,
        out_specs=(VM, VM, VM),
        compiler_params=params(16),
        cost_estimate=cost(1e9, 5e6),
        name="project",
    )(query, info, freq, phase, query_weight, kv_weight)


def attend_kernel(shift, sub, got, qx, qe, et, info, kv_weight, part_out, lse_out):
    owners, both, width = got.shape
    per_peer = both // 2
    slots = owners * per_peer
    queries = qx.shape[0] // (2 * HEADS)
    head_dim = width // HEADS
    rows = got[:, sub * per_peer : (sub + 1) * per_peer, :].reshape(slots, width)
    codes = et[...]
    who = info[...] & ((1 << shift) - 1)
    mask = lax.broadcasted_iota(i32, (queries, slots), 0) == who
    logs = []
    for h in range(HEADS):
        high = pl.ds(2 * h * queries, queries)
        low = pl.ds((2 * h + 1) * queries, queries)
        scores = dot_nt(qx[high, :], rows) + dot_nt(qx[low, :], rows)
        scores = scores + dot(qe[high, :], codes) + dot(qe[low, :], codes)
        scores = jnp.where(mask, scores, NEG)
        top = jnp.max(scores, axis=1, keepdims=True)
        weights = jnp.where(mask, jnp.exp(scores - top), 0.0).astype(bf16)
        total = jnp.sum(weights.astype(f32), axis=1, keepdims=True)
        some = total > 0.0
        inv = jnp.where(some, 1.0 / jnp.where(some, total, 1.0), 0.0)
        logs.append(jnp.where(some, top + jnp.log(jnp.where(some, total, 1.0)), NEG))
        mem_high, mem_low = split(dot(weights, rows) * inv)
        code_high, code_low = split(dot_nt(weights, codes) * inv)
        lanes = slice(width + h * head_dim, width + (h + 1) * head_dim)
        value_mem = kv_weight[:width, lanes]
        value_code = kv_weight[width:, lanes]
        part = dot(mem_high, value_mem) + dot(mem_low, value_mem)
        part = part + dot(code_high, value_code) + dot(code_low, value_code)
        part_out[:, h * head_dim : (h + 1) * head_dim] = part.astype(part_out.dtype)
    lane = lax.broadcasted_iota(i32, (queries, LANES), 1)
    spread = jnp.where((lane & 7) < 4, logs[0], logs[1])
    lse_out[...] = jnp.transpose(spread)[:8, :]


def attend(shift, sub, got, qx, qe, et, info, kv_weight, kind, name):
    queries = qx.shape[0] // (2 * HEADS)
    width = got.shape[2]
    return pl.pallas_call(
        functools.partial(attend_kernel, shift, sub),
        out_shape=(
            jax.ShapeDtypeStruct((queries, width), kind),
            jax.ShapeDtypeStruct((8, queries), f32),
        ),
        in_specs=[VM] * 6,
        out_specs=(VM, VM),
        compiler_params=params(40),
        cost_estimate=cost(4e9, 5e6),
        name=name,
    )(got, qx, qe, et, info, kv_weight)


def merge_kernel(mine, mine_lse, other, other_lse, query, out_weight, out):
    queries, width = mine.shape
    head_dim = width // HEADS
    pieces = []
    for h in range(HEADS):
        lanes = slice(h * head_dim, (h + 1) * head_dim)
        lse_a = jnp.transpose(jnp.broadcast_to(mine_lse[pl.ds(4 * h, 1), :], (LANES, queries)))
        lse_b = jnp.transpose(jnp.broadcast_to(other_lse[pl.ds(4 * h, 1), :], (LANES, queries)))
        top = jnp.maximum(lse_a, lse_b)
        weight_a = jnp.exp(lse_a - top)
        weight_b = jnp.exp(lse_b - top)
        inv = 1.0 / (weight_a + weight_b)
        pieces.append(
            mine[:, lanes] * (weight_a * inv) + other[:, lanes].astype(f32) * (weight_b * inv)
        )
    attended = jnp.concatenate(pieces, axis=1).astype(bf16)
    result = dot(attended, out_weight[:width, :]) + dot(query[...], out_weight[width:, :])
    out[...] = result.astype(bf16)


def merge(mine, mine_lse, other, other_lse, query, out_weight):
    return pl.pallas_call(
        merge_kernel,
        out_shape=jax.ShapeDtypeStruct(query.shape, bf16),
        in_specs=[VM] * 6,
        out_specs=VM,
        compiler_params=params(8),
        cost_estimate=cost(1e8, 1e6),
        name="merge",
    )(mine, mine_lse, other, other_lse, query, out_weight)


def local(
    group_count,
    mem_count,
    node_memory,
    last_update,
    evt_src,
    evt_dst,
    evt_time,
    evt_counts,
    time_freq,
    time_phase,
    msg_weight,
    mem_weight,
    gru_bias,
    qry_rows,
    qry_time,
    nbr_time,
    nbr_slot,
    req_rows,
    query_weight,
    kv_weight,
    out_weight,
):
    peers = group_count * mem_count
    side_peers = peers // 2
    half_groups = group_count // 2
    nodes, width = node_memory.shape
    events = evt_src.shape[0]
    cap = events // peers
    queries, fan_out = nbr_time.shape
    total_slots = queries * fan_out
    per_peer = total_slots // peers
    side_slots = side_peers * per_peer
    shift = (queries - 1).bit_length()
    side = lax.axis_index("grp") // half_groups
    sides = [list(range(s * side_peers, (s + 1) * side_peers)) for s in range(2)]
    opposite = [(g, (g + half_groups) % group_count) for g in range(group_count)]

    def mine_other(pair):
        return jnp.where(side == 0, pair[0], pair[1]), jnp.where(side == 0, pair[1], pair[0])

    is_live = jnp.arange(cap, dtype=i32)[None, :] < evt_counts[0][:, None]
    target = jnp.where(is_live, evt_dst.reshape(peers, cap), nodes)
    ids = jnp.concatenate(
        [(target << TIME_BITS) + evt_time.reshape(peers, cap), req_rows.reshape(peers, per_peer)],
        axis=1,
    )
    got_ids = lax.all_to_all(ids, AXES, split_axis=0, concat_axis=0, tiled=True)
    sent_rows, table = gather_sources(evt_src, node_memory)
    got_rows = lax.all_to_all(
        sent_rows.reshape(peers, cap, width), AXES, split_axis=0, concat_axis=0, tiled=True
    ).reshape(events, width)

    packed = got_ids[:, :cap].reshape(events)
    dst = packed >> TIME_BITS
    time_row = (packed & ((1 << TIME_BITS) - 1)).reshape(1, events)
    dst_row = jnp.where(dst < nodes, dst, -1).reshape(1, events)
    dst_col = dst.reshape(events, 1)
    mine, other = mine_other(got_ids[:, cap:].reshape(2, side_peers, per_peer))
    req2 = 2 * jnp.concatenate([mine, other], axis=1).reshape(total_slots)
    freq = time_freq.reshape(-1, 1)
    phase = time_phase.reshape(-1, 1)
    bias = gru_bias.reshape(1, -1)
    pre, inv, rows = prepare(
        jnp.minimum(dst, nodes - 1),
        last_update,
        table,
        dst_row,
        dst_col,
        time_row,
        freq,
        phase,
        msg_weight,
        mem_weight,
        bias,
    )
    found, query_mem, new_table = update(
        dst, req2, qry_rows, table, got_rows, dst_row, dst_col, pre, inv, rows, msg_weight
    )
    got = lax.all_to_all(
        found.reshape(side_peers, 2 * per_peer, width),
        AXES,
        split_axis=0,
        concat_axis=0,
        tiled=True,
        axis_index_groups=sides,
    )
    query_other = lax.ppermute(query_mem, "grp", opposite)
    new_memory = narrow(new_table)

    delta = qry_time[:, None] - nbr_time + (1 << TIME_BITS)
    values = (delta << shift) + jnp.arange(queries, dtype=i32)[:, None]
    info = invert(nbr_slot.reshape(total_slots), values.reshape(total_slots))
    info_mine, info_send = mine_other(info.reshape(2, 1, side_slots))
    info_other = lax.ppermute(info_send, "grp", opposite)

    args = (freq, phase, query_weight, kv_weight)
    qx_b, qe_b, et_b = project(shift, query_other, info_other, *args)
    qx_a, qe_a, et_a = project(shift, query_mem, info_mine, *args)
    part_b, lse_b = attend(shift, 1, got, qx_b, qe_b, et_b, info_other, kv_weight, bf16, "attend_other")
    back, back_lse = lax.ppermute(part_b, "grp", opposite), lax.ppermute(lse_b, "grp", opposite)
    part_a, lse_a = attend(shift, 0, got, qx_a, qe_a, et_a, info_mine, kv_weight, f32, "attend_mine")
    embeddings = merge(part_a, lse_a, back, back_lse, query_mem, out_weight)
    return new_memory, embeddings


def solution(mesh):
    split_rows = P(AXES, None)
    split_flat = P(AXES)
    in_specs = (
        split_rows,
        split_flat,
        split_flat,
        split_flat,
        split_flat,
        split_rows,
        P(),
        P(),
        P(),
        P(),
        P(),
        split_flat,
        split_flat,
        split_rows,
        split_rows,
        split_flat,
        P(),
        P(),
        P(),
    )
    body = functools.partial(local, mesh.shape["grp"], mesh.shape["mem"])
    return jax.shard_map(
        body, mesh=mesh, in_specs=in_specs, out_specs=(split_rows, split_rows), check_vma=False
    )
```

```python
import functools
import math

import jax
import jax.numpy as jnp
from jax import lax
from jax.experimental import pallas as pl
from jax.experimental.pallas import tpu as pltpu
from jax.sharding import PartitionSpec as P

HEADS = 2
AXES = ("grp", "mem")
LANES = 128
UNROLL = 32
CHUNKS = 8
NEG = -1e30
TIME_BITS = 12
f32 = jnp.float32
bf16 = jnp.bfloat16
i32 = jnp.int32
VM = pl.BlockSpec(memory_space=pltpu.VMEM)
SM = pl.BlockSpec(memory_space=pltpu.SMEM)
HB = pl.BlockSpec(memory_space=pltpu.HBM)


def dot(a, b):
    return jnp.dot(a, b, preferred_element_type=f32)


def dot_nt(a, b):
    return lax.dot_general(a, b, (((1,), (1,)), ((), ())), preferred_element_type=f32)


def split(x):
    high = x.astype(bf16)
    return high, (x - high.astype(f32)).astype(bf16)


def cosine(x):
    turns = jnp.round(x * (1.0 / math.pi))
    r = x - turns * 3.140625
    r = r - turns * 9.675025939941406e-4
    r = r - turns * 1.5099579909783764e-7
    s = r * r
    p = -2.755731922398589e-7 + s * 2.08767569878681e-9
    p = 2.48015873015873e-5 + s * p
    p = -1.3888888888888889e-3 + s * p
    p = 4.1666666666666664e-2 + s * p
    p = -0.5 + s * p
    p = 1.0 + s * p
    half = turns * 0.5
    odd = half - jnp.floor(half)
    return p * (1.0 - 4.0 * odd)


def run(kernel, args, in_specs, out_shape, out_specs, **rest):
    args = [
        pltpu.with_memory_space_constraint(a, pltpu.HBM) if spec is HB else a
        for a, spec in zip(args, in_specs)
    ]
    outs = [
        pltpu.HBM(o.shape, o.dtype) if spec is HB else o for o, spec in zip(out_shape, out_specs)
    ]
    return pl.pallas_call(
        kernel, out_shape=outs, in_specs=in_specs, out_specs=list(out_specs), **rest
    )(*args)


def params(mib):
    return pltpu.CompilerParams(vmem_limit_bytes=mib << 20)


def cost(flops, nbytes):
    return pl.CostEstimate(flops=int(flops), bytes_accessed=int(nbytes), transcendentals=0)


def move_rows(count, load, store):
    def body(t, carry):
        base = pl.multiple_of(t * UNROLL, UNROLL)
        for part in range(0, UNROLL, 16):
            rows = [load(base + part + u) for u in range(16)]
            for u in range(16):
                store(base + part + u, rows[u])
        return carry

    lax.fori_loop(0, count // UNROLL, body, 0)


def pack_rows(count, src, src_base, dst, dst_base):
    def body(t, carry):
        r = pl.multiple_of(t * 16, 16)
        for half in range(2):
            dst[pl.ds(dst_base + r, 16), half * LANES : (half + 1) * LANES] = src[
                pl.ds(2 * (src_base + r) + half, 16, stride=2), :
            ].astype(bf16)
        return carry

    lax.fori_loop(0, count // 16, body, 0, unroll=4)


def source_kernel(
    idx_hbm, memory, rows_out, table_out, idx, raw, table, stage, in_sem, out_sem, idx_sem
):
    nodes = memory.shape[0]
    step = nodes // CHUNKS
    loads = [
        pltpu.make_async_copy(
            memory.at[pl.ds(c * step, step)], raw.at[pl.ds(c * step, step)], in_sem.at[c]
        )
        for c in range(CHUNKS)
    ]
    saves = [
        pltpu.make_async_copy(
            table.at[pl.ds(2 * c * step, 2 * step)],
            table_out.at[pl.ds(2 * c * step, 2 * step)],
            out_sem.at[c],
        )
        for c in range(CHUNKS)
    ]
    for copy in loads:
        copy.start()
    idx_load = pltpu.make_async_copy(idx_hbm, idx, idx_sem)
    idx_load.start()
    for c in range(CHUNKS):
        loads[c].wait()

        def widen(t, carry):
            r = pl.multiple_of(c * step + t * 16, 16)
            rows = raw[pl.ds(r, 16), :].astype(f32)
            for half in range(2):
                table[pl.ds(2 * r + half, 16, stride=2), :] = rows[
                    :, half * LANES : (half + 1) * LANES
                ]
            return carry

        lax.fori_loop(0, step // 16, widen, 0, unroll=8)
        saves[c].start()
    idx_load.wait()

    def put(k, row):
        stage[pl.ds(2 * k, 2), :] = row

    move_rows(idx.shape[0], lambda k: table[pl.ds(2 * idx[k], 2), :], put)
    pack_rows(idx.shape[0], stage, 0, rows_out, 0)
    for copy in saves:
        copy.wait()


def gather_sources(evt_src, node_memory):
    nodes, width = node_memory.shape
    events = evt_src.shape[0]
    return run(
        source_kernel,
        [evt_src, node_memory],
        out_shape=(
            jax.ShapeDtypeStruct((events, width), bf16),
            jax.ShapeDtypeStruct((2 * nodes, LANES), f32),
        ),
        in_specs=[HB, HB],
        out_specs=(VM, HB),
        scratch_shapes=[
            pltpu.SMEM(evt_src.shape, i32),
            pltpu.VMEM((nodes, width), bf16),
            pltpu.VMEM((2 * nodes, LANES), f32),
            pltpu.VMEM((2 * events, LANES), f32),
            pltpu.SemaphoreType.DMA((CHUNKS,)),
            pltpu.SemaphoreType.DMA((CHUNKS,)),
            pltpu.SemaphoreType.DMA,
        ],
        compiler_params=params(24),
        cost_estimate=cost(0, 20e6),
        name="source_rows",
    )


def prepare_kernel(
    dst_s,
    seen_hbm,
    table_hbm,
    dst_row,
    dst_col,
    time_row,
    freq,
    phase,
    msg_hbm,
    mem_hbm,
    bias,
    pre_hbm,
    inv_hbm,
    rows_hbm,
    seen_s,
    table,
    stage,
    seen_pick,
    seen_row,
    codes,
    msg_weight,
    mem_weight,
    pre_out,
    inv_out,
    rows_out,
    sem,
    out_sem,
):
    events = dst_s.shape[0]
    width = rows_out.shape[1]
    code_width = freq.shape[0]
    loads = [
        pltpu.make_async_copy(a, b, sem.at[k])
        for k, (a, b) in enumerate(
            [(seen_hbm, seen_s), (table_hbm, table), (msg_hbm, msg_weight), (mem_hbm, mem_weight)]
        )
    ]
    for copy in loads:
        copy.start()
    loads[0].wait()

    def look(t, carry):
        base = t * 8
        at = [dst_s[base + u] for u in range(8)]
        got = [seen_s[a] for a in at]
        for u in range(8):
            seen_pick[0, base + u] = got[u]
        return carry

    lax.fori_loop(0, events // 8, look, 0)
    across = pltpu.make_async_copy(seen_pick, seen_row, sem.at[4])
    across.start()
    loads[1].wait()

    def put(k, row):
        stage[pl.ds(2 * k, 2), :] = row

    move_rows(events, lambda k: table[pl.ds(2 * dst_s[k], 2), :], put)
    pack_rows(events, stage, 0, rows_out, 0)
    across.wait()
    step = 256
    for t in range(events // step):
        delta = (time_row[:, pl.ds(t * step, step)] - seen_row[:, pl.ds(t * step, step)]).astype(f32)
        codes[pl.ds(0, code_width), pl.ds(t * step, step)] = cosine(
            freq[...] * delta + phase[...]
        ).astype(bf16)
    codes[pl.ds(code_width, LANES), :] = jnp.ones((LANES, events), bf16)
    loads[2].wait()
    loads[3].wait()

    def block(t, carry):
        r = pl.multiple_of(t * step, step)
        same = jnp.where(dst_col[pl.ds(r, step), :] == dst_row[...], 1.0, 0.0).astype(bf16)
        sums = dot_nt(same, codes[...])
        inv = 1.0 / jnp.maximum(sums[:, code_width:], 1.0)
        code_agg = (sums[:, :code_width] * inv).astype(bf16)
        inv_out[pl.ds(r, step), :] = inv
        memory = rows_out[pl.ds(r, step), :]
        part = dot(code_agg, msg_weight[pl.ds(width, code_width), :]) + bias[...]
        joined = dot(memory, mem_weight[...])
        third = 3 * width
        pre_out[pl.ds(r, step), : 2 * width] = (
            part[:, : 2 * width] + joined[:, : 2 * width] + joined[:, third : third + 2 * width]
        )
        pre_out[pl.ds(r, step), 2 * width : third] = (
            part[:, 2 * width :] + joined[:, 2 * width : third]
        )
        pre_out[pl.ds(r, step), third:] = joined[:, third + 2 * width :]
        return carry

    outs = [(rows_out, rows_hbm), (inv_out, inv_hbm), (pre_out, pre_hbm)]

    def save(k, t):
        r = pl.multiple_of(t * step, step)
        a, b = outs[k]
        return pltpu.make_async_copy(a.at[pl.ds(r, step)], b.at[pl.ds(r, step)], out_sem.at[k, t])

    def run(t, carry):
        block(t, carry)
        for k in range(3):
            save(k, t).start()
        return carry

    lax.fori_loop(0, events // step, run, 0)

    def drain(t, carry):
        for k in range(3):
            save(k, t).wait()
        return carry

    lax.fori_loop(0, events // step, drain, 0)


def prepare(dst, last_update, table, dst_row, dst_col, time_row, freq, phase, msg_weight, mem_weight, bias):
    events = dst.shape[0]
    width = mem_weight.shape[0]
    return run(
        prepare_kernel,
        [dst, last_update, table, dst_row, dst_col, time_row, freq, phase, msg_weight, mem_weight, bias],
        out_shape=(
            jax.ShapeDtypeStruct((events, 4 * width), f32),
            jax.ShapeDtypeStruct((events, LANES), f32),
            jax.ShapeDtypeStruct((events, width), bf16),
        ),
        in_specs=[SM, HB, HB] + [VM] * 5 + [HB, HB, VM],
        out_specs=(HB, HB, HB),
        scratch_shapes=[
            pltpu.SMEM(last_update.shape, i32),
            pltpu.VMEM(table.shape, f32),
            pltpu.VMEM((2 * events, LANES), f32),
            pltpu.SMEM((1, events), i32),
            pltpu.VMEM((1, events), i32),
            pltpu.VMEM((freq.shape[0] + LANES, events), bf16),
            pltpu.VMEM(msg_weight.shape, bf16),
            pltpu.VMEM(mem_weight.shape, bf16),
            pltpu.VMEM((events, 4 * width), f32),
            pltpu.VMEM((events, LANES), f32),
            pltpu.VMEM((events, width), bf16),
            pltpu.SemaphoreType.DMA((5,)),
            pltpu.SemaphoreType.DMA((3, events // 256)),
        ],
        compiler_params=params(40),
        cost_estimate=cost(6e9, 30e6),
        name="prepare",
    )


def update_kernel(
    dst_s,
    req_s,
    qry_s,
    table_hbm,
    got,
    dst_row,
    dst_col,
    pre_hbm,
    inv_hbm,
    rows_hbm,
    msg_hbm,
    found_hbm,
    query_out,
    table_out,
    table,
    updated,
    stage,
    packed,
    pre,
    inv,
    rows,
    msg_weight,
    sem,
    block_sem,
    out_sem,
):
    nodes2 = table_hbm.shape[0]
    events, width = rows.shape
    step = 256
    blocks = [(rows_hbm, rows), (inv_hbm, inv), (pre_hbm, pre)]

    def fetch(k, t):
        r = pl.multiple_of(t * step, step)
        a, b = blocks[k]
        return pltpu.make_async_copy(a.at[pl.ds(r, step)], b.at[pl.ds(r, step)], block_sem.at[k, t])

    weight_load = pltpu.make_async_copy(msg_hbm.at[pl.ds(0, width)], msg_weight, sem.at[1])
    weight_load.start()
    for t in range(events // step):
        for k in range(3):
            fetch(k, t).start()
    load = pltpu.make_async_copy(table_hbm, table.at[pl.ds(0, nodes2)], sem.at[0])
    load.start()

    def block(t, carry):
        r = pl.multiple_of(t * step, step)
        same = jnp.where(dst_col[pl.ds(r, step), :] == dst_row[...], 1.0, 0.0).astype(bf16)
        sums = dot(same, got[...])
        for k in range(3):
            fetch(k, t).wait()
        scale = inv[pl.ds(r, step), :]
        agg = jnp.concatenate(
            [sums[:, h * LANES : (h + 1) * LANES] * scale for h in range(width // LANES)], axis=1
        ).astype(bf16)
        msg = dot(agg, msg_weight[...])
        ready = pre[pl.ds(r, step), :]
        reset = jax.nn.sigmoid(msg[:, :width] + ready[:, :width])
        gate = jax.nn.sigmoid(msg[:, width : 2 * width] + ready[:, width : 2 * width])
        cand = jnp.tanh(
            msg[:, 2 * width :] + ready[:, 2 * width : 3 * width] + reset * ready[:, 3 * width :]
        )
        new = (1.0 - gate) * cand + gate * rows[pl.ds(r, step), :].astype(f32)
        new = new.astype(bf16).astype(f32)
        for half in range(2):
            updated[pl.ds(2 * r + half, step, stride=2), :] = new[:, half * LANES : (half + 1) * LANES]
        return carry

    weight_load.wait()
    lax.fori_loop(0, events // step, block, 0)
    load.wait()

    def put_table(k, row):
        table[pl.ds(2 * dst_s[k], 2), :] = row

    move_rows(events, lambda k: updated[pl.ds(2 * k, 2), :], put_table)
    save = pltpu.make_async_copy(table.at[pl.ds(0, nodes2)], table_out, sem.at[0])
    save.start()

    def put(k, row):
        stage[pl.ds(2 * k, 2), :] = row

    queries = qry_s.shape[0]
    move_rows(queries, lambda k: table[pl.ds(2 * qry_s[k], 2), :], put)
    pack_rows(queries, stage, 0, query_out, 0)
    total = req_s.shape[0]
    chunk = total // 4
    sends = []
    for c in range(4):
        move_rows(chunk, lambda k: table[pl.ds(req_s[c * chunk + k], 2), :], put)
        pack_rows(chunk, stage, 0, packed, c * chunk)
        send = pltpu.make_async_copy(
            packed.at[pl.ds(c * chunk, chunk)],
            found_hbm.at[pl.ds(c * chunk, chunk)],
            out_sem.at[c],
        )
        send.start()
        sends.append(send)
    for send in sends:
        send.wait()
    save.wait()


def update(dst, req2, qry_rows, table, got, dst_row, dst_col, pre, inv, rows, msg_weight):
    events, width = got.shape
    queries = qry_rows.shape[0]
    total = req2.shape[0]
    return run(
        update_kernel,
        [dst, req2, qry_rows, table, got, dst_row, dst_col, pre, inv, rows, msg_weight],
        out_shape=(
            jax.ShapeDtypeStruct((total, width), bf16),
            jax.ShapeDtypeStruct((queries, width), bf16),
            jax.ShapeDtypeStruct(table.shape, f32),
        ),
        in_specs=[SM, SM, SM, HB, VM, VM, VM, HB, HB, HB, HB],
        out_specs=(HB, VM, HB),
        scratch_shapes=[
            pltpu.VMEM((table.shape[0] + 16, LANES), f32),
            pltpu.VMEM((2 * events, LANES), f32),
            pltpu.VMEM((2 * (total // 4), LANES), f32),
            pltpu.VMEM((total, width), bf16),
            pltpu.VMEM(pre.shape, f32),
            pltpu.VMEM(inv.shape, f32),
            pltpu.VMEM(rows.shape, bf16),
            pltpu.VMEM((width, msg_weight.shape[1]), bf16),
            pltpu.SemaphoreType.DMA((2,)),
            pltpu.SemaphoreType.DMA((3, events // 256)),
            pltpu.SemaphoreType.DMA((4,)),
        ],
        compiler_params=params(36),
        cost_estimate=cost(4e9, 40e6),
        name="update",
    )


def narrow_kernel(table, out):
    pack_rows(out.shape[0], table, 0, out, 0)


def narrow(table):
    nodes = table.shape[0] // 2
    step = nodes // 8
    return pl.pallas_call(
        narrow_kernel,
        grid=(8,),
        out_shape=jax.ShapeDtypeStruct((nodes, 2 * LANES), bf16),
        in_specs=[pl.BlockSpec((2 * step, LANES), lambda t: (t, 0))],
        out_specs=pl.BlockSpec((step, 2 * LANES), lambda t: (t, 0)),
        compiler_params=params(16),
        cost_estimate=cost(0, 12e6),
        name="narrow",
    )(pltpu.with_memory_space_constraint(table, pltpu.HBM))


def invert_kernel(slot_s, value_s, out_s):
    fan_out, queries = value_s.shape

    def body(q, carry):
        base = q * fan_out
        for first in range(0, fan_out, 10):
            some = range(first, min(first + 10, fan_out))
            at = [slot_s[base + k] for k in some]
            value = [value_s[k, q] for k in some]
            for a, v in zip(at, value):
                out_s[a] = v
        return carry

    lax.fori_loop(0, queries, body, 0)


def invert(slots, values):
    return pl.pallas_call(
        invert_kernel,
        out_shape=jax.ShapeDtypeStruct(slots.shape, i32),
        in_specs=[SM, SM],
        out_specs=SM,
        cost_estimate=cost(0, 20e6),
        name="invert",
    )(slots, values)


def project_kernel(
    shift,
    query,
    info,
    freq,
    phase,
    query_weight,
    kv_weight,
    qx_hbm,
    qe_hbm,
    et_hbm,
    qx_out,
    qe_out,
    et_out,
    sem,
):
    width = query_weight.shape[0]
    head_dim = width // HEADS
    queries = query.shape[0]
    vec = dot(query[...], query_weight[...]) * (1.0 / math.sqrt(head_dim))
    for h in range(HEADS):
        high, low = split(vec[:, h * head_dim : (h + 1) * head_dim])
        keys = kv_weight[:, h * head_dim : (h + 1) * head_dim]
        folded = dot_nt(high, keys) + dot_nt(low, keys)
        parts = split(folded)
        for k in range(2):
            rows = pl.ds((2 * h + k) * queries, queries)
            qx_out[rows, :] = parts[k][:, :width]
            qe_out[rows, :] = parts[k][:, width:]
    step = 256
    slots = info.shape[1]
    for t in range(slots // step):
        delta = ((info[:, pl.ds(t * step, step)] >> shift) - (1 << TIME_BITS)).astype(f32)
        et_out[:, pl.ds(t * step, step)] = cosine(freq[...] * delta + phase[...]).astype(bf16)
    pairs = ((qx_out, qx_hbm), (qe_out, qe_hbm), (et_out, et_hbm))
    copies = [pltpu.make_async_copy(a, b, sem.at[k]) for k, (a, b) in enumerate(pairs)]
    for copy in copies:
        copy.start()
    for copy in copies:
        copy.wait()


def project(shift, query, info, freq, phase, query_weight, kv_weight):
    queries, width = query.shape
    slots = info.shape[1]
    code_width = freq.shape[0]
    return run(
        functools.partial(project_kernel, shift),
        [query, info, freq, phase, query_weight, kv_weight],
        out_shape=(
            jax.ShapeDtypeStruct((2 * HEADS * queries, width), bf16),
            jax.ShapeDtypeStruct((2 * HEADS * queries, code_width), bf16),
            jax.ShapeDtypeStruct((code_width, slots), bf16),
        ),
        in_specs=[VM] * 6,
        out_specs=(HB, HB, HB),
        scratch_shapes=[
            pltpu.VMEM((2 * HEADS * queries, width), bf16),
            pltpu.VMEM((2 * HEADS * queries, code_width), bf16),
            pltpu.VMEM((code_width, slots), bf16),
            pltpu.SemaphoreType.DMA((3,)),
        ],
        compiler_params=params(16),
        cost_estimate=cost(1e9, 5e6),
        name="project",
    )


def attend_kernel(
    shift,
    sub,
    got,
    qx_hbm,
    qe_hbm,
    et_hbm,
    info,
    kv_hbm,
    part_out,
    lse_out,
    qx,
    qe,
    et,
    kv_weight,
    sem,
):
    pairs = ((qx_hbm, qx), (et_hbm, et), (qe_hbm, qe), (kv_hbm, kv_weight))
    copies = [pltpu.make_async_copy(a, b, sem.at[k]) for k, (a, b) in enumerate(pairs)]
    for copy in copies:
        copy.start()
    for copy in copies:
        copy.wait()
    owners, both, width = got.shape
    per_peer = both // 2
    slots = owners * per_peer
    queries = qx.shape[0] // (2 * HEADS)
    head_dim = width // HEADS
    rows = got[:, sub * per_peer : (sub + 1) * per_peer, :].reshape(slots, width)
    codes = et[...]
    who = info[...] & ((1 << shift) - 1)
    mask = lax.broadcasted_iota(i32, (queries, slots), 0) == who
    logs = []
    for h in range(HEADS):
        high = pl.ds(2 * h * queries, queries)
        low = pl.ds((2 * h + 1) * queries, queries)
        scores = dot_nt(qx[high, :], rows) + dot_nt(qx[low, :], rows)
        scores = scores + dot(qe[high, :], codes) + dot(qe[low, :], codes)
        scores = jnp.where(mask, scores, NEG)
        top = jnp.max(scores, axis=1, keepdims=True)
        weights = jnp.where(mask, jnp.exp(scores - top), 0.0).astype(bf16)
        total = jnp.sum(weights.astype(f32), axis=1, keepdims=True)
        some = total > 0.0
        inv = jnp.where(some, 1.0 / jnp.where(some, total, 1.0), 0.0)
        logs.append(jnp.where(some, top + jnp.log(jnp.where(some, total, 1.0)), NEG))
        mem_high, mem_low = split(dot(weights, rows) * inv)
        code_high, code_low = split(dot_nt(weights, codes) * inv)
        lanes = slice(width + h * head_dim, width + (h + 1) * head_dim)
        value_mem = kv_weight[:width, lanes]
        value_code = kv_weight[width:, lanes]
        part = dot(mem_high, value_mem) + dot(mem_low, value_mem)
        part = part + dot(code_high, value_code) + dot(code_low, value_code)
        part_out[:, h * head_dim : (h + 1) * head_dim] = part.astype(part_out.dtype)
    lane = lax.broadcasted_iota(i32, (queries, LANES), 1)
    spread = jnp.where((lane & 7) < 4, logs[0], logs[1])
    lse_out[...] = jnp.transpose(spread)[:8, :]


def attend(shift, sub, got, qx, qe, et, info, kv_weight, kind, name):
    queries = qx.shape[0] // (2 * HEADS)
    width = got.shape[2]
    return run(
        functools.partial(attend_kernel, shift, sub),
        [got, qx, qe, et, info, kv_weight],
        out_shape=(
            jax.ShapeDtypeStruct((queries, width), kind),
            jax.ShapeDtypeStruct((8, queries), f32),
        ),
        in_specs=[VM, HB, HB, HB, VM, HB],
        out_specs=(VM, VM),
        scratch_shapes=[pltpu.VMEM(a.shape, bf16) for a in (qx, qe, et, kv_weight)]
        + [pltpu.SemaphoreType.DMA((4,))],
        compiler_params=params(32),
        cost_estimate=cost(4e9, 5e6),
        name=name,
    )


def merge_kernel(mine, mine_lse, other, other_lse, query, out_weight, out):
    queries, width = mine.shape
    head_dim = width // HEADS
    pieces = []
    for h in range(HEADS):
        lanes = slice(h * head_dim, (h + 1) * head_dim)
        lse_a = jnp.transpose(jnp.broadcast_to(mine_lse[pl.ds(4 * h, 1), :], (LANES, queries)))
        lse_b = jnp.transpose(jnp.broadcast_to(other_lse[pl.ds(4 * h, 1), :], (LANES, queries)))
        top = jnp.maximum(lse_a, lse_b)
        weight_a = jnp.exp(lse_a - top)
        weight_b = jnp.exp(lse_b - top)
        inv = 1.0 / (weight_a + weight_b)
        pieces.append(
            mine[:, lanes] * (weight_a * inv) + other[:, lanes].astype(f32) * (weight_b * inv)
        )
    attended = jnp.concatenate(pieces, axis=1).astype(bf16)
    result = dot(attended, out_weight[:width, :]) + dot(query[...], out_weight[width:, :])
    out[...] = result.astype(bf16)


def merge(mine, mine_lse, other, other_lse, query, out_weight):
    return pl.pallas_call(
        merge_kernel,
        out_shape=jax.ShapeDtypeStruct(query.shape, bf16),
        in_specs=[VM] * 6,
        out_specs=VM,
        compiler_params=params(8),
        cost_estimate=cost(1e8, 1e6),
        name="merge",
    )(mine, mine_lse, other, other_lse, query, out_weight)


def local(
    group_count,
    mem_count,
    node_memory,
    last_update,
    evt_src,
    evt_dst,
    evt_time,
    evt_counts,
    time_freq,
    time_phase,
    msg_weight,
    mem_weight,
    gru_bias,
    qry_rows,
    qry_time,
    nbr_time,
    nbr_slot,
    req_rows,
    query_weight,
    kv_weight,
    out_weight,
):
    peers = group_count * mem_count
    side_peers = peers // 2
    half_groups = group_count // 2
    nodes, width = node_memory.shape
    events = evt_src.shape[0]
    cap = events // peers
    queries, fan_out = nbr_time.shape
    total_slots = queries * fan_out
    per_peer = total_slots // peers
    side_slots = side_peers * per_peer
    shift = (queries - 1).bit_length()
    side = lax.axis_index("grp") // half_groups
    sides = [list(range(s * side_peers, (s + 1) * side_peers)) for s in range(2)]
    opposite = [(g, (g + half_groups) % group_count) for g in range(group_count)]

    def mine_other(pair):
        return jnp.where(side == 0, pair[0], pair[1]), jnp.where(side == 0, pair[1], pair[0])

    is_live = jnp.arange(cap, dtype=i32)[None, :] < evt_counts[0][:, None]
    target = jnp.where(is_live, evt_dst.reshape(peers, cap), nodes)
    ids = jnp.concatenate(
        [(target << TIME_BITS) + evt_time.reshape(peers, cap), req_rows.reshape(peers, per_peer)],
        axis=1,
    )
    got_ids = lax.all_to_all(ids, AXES, split_axis=0, concat_axis=0, tiled=True)
    sent_rows, table = gather_sources(evt_src, node_memory)
    got_rows = lax.all_to_all(
        sent_rows.reshape(peers, cap, width), AXES, split_axis=0, concat_axis=0, tiled=True
    ).reshape(events, width)

    packed = got_ids[:, :cap].reshape(events)
    dst = packed >> TIME_BITS
    time_row = (packed & ((1 << TIME_BITS) - 1)).reshape(1, events)
    dst_row = jnp.where(dst < nodes, dst, -1).reshape(1, events)
    dst_col = dst.reshape(events, 1)
    mine, other = mine_other(got_ids[:, cap:].reshape(2, side_peers, per_peer))
    req2 = 2 * jnp.concatenate([mine, other], axis=1).reshape(total_slots)
    freq = time_freq.reshape(-1, 1)
    phase = time_phase.reshape(-1, 1)
    bias = gru_bias.reshape(1, -1)
    delta = qry_time[:, None] - nbr_time + (1 << TIME_BITS)
    values = ((delta << shift) + jnp.arange(queries, dtype=i32)[:, None]).T
    info = invert(nbr_slot.reshape(total_slots), values)
    info_mine, info_send = mine_other(info.reshape(2, 1, side_slots))
    req2, info_send = lax.optimization_barrier((req2, info_send))
    info_other = lax.ppermute(info_send, "grp", opposite)
    pre, inv, rows = prepare(
        jnp.minimum(dst, nodes - 1),
        last_update,
        table,
        dst_row,
        dst_col,
        time_row,
        freq,
        phase,
        msg_weight,
        mem_weight,
        bias,
    )
    found, query_mem, new_table = update(
        dst, req2, qry_rows, table, got_rows, dst_row, dst_col, pre, inv, rows, msg_weight
    )
    got = lax.all_to_all(
        found.reshape(side_peers, 2 * per_peer, width),
        AXES,
        split_axis=0,
        concat_axis=0,
        tiled=True,
        axis_index_groups=sides,
    )
    query_other = lax.ppermute(query_mem, "grp", opposite)
    new_memory = narrow(new_table)

    args = (freq, phase, query_weight, kv_weight)
    qx_b, qe_b, et_b = project(shift, query_other, info_other, *args)
    qx_a, qe_a, et_a = project(shift, query_mem, info_mine, *args)
    part_b, lse_b = attend(shift, 1, got, qx_b, qe_b, et_b, info_other, kv_weight, bf16, "attend_other")
    back, back_lse = lax.ppermute(part_b, "grp", opposite), lax.ppermute(lse_b, "grp", opposite)
    part_a, lse_a = attend(shift, 0, got, qx_a, qe_a, et_a, info_mine, kv_weight, f32, "attend_mine")
    embeddings = merge(part_a, lse_a, back, back_lse, query_mem, out_weight)
    return new_memory, embeddings


def solution(mesh):
    split_rows = P(AXES, None)
    split_flat = P(AXES)
    in_specs = (
        split_rows,
        split_flat,
        split_flat,
        split_flat,
        split_flat,
        split_rows,
        P(),
        P(),
        P(),
        P(),
        P(),
        split_flat,
        split_flat,
        split_rows,
        split_rows,
        split_flat,
        P(),
        P(),
        P(),
    )
    body = functools.partial(local, mesh.shape["grp"], mesh.shape["mem"])
    return jax.shard_map(
        body, mesh=mesh, in_specs=in_specs, out_specs=(split_rows, split_rows), check_vma=False
    )
```

```python
import functools
import math

import jax
import jax.numpy as jnp
from jax import lax
from jax.experimental import pallas as pl
from jax.experimental.pallas import tpu as pltpu
from jax.sharding import PartitionSpec as P


HEADS = 2
AXES = ("grp", "mem")
LANES = 128
UNROLL = 32
ROWS = 512
CHUNKS = 8
NEG = -1e30
TIME_BITS = 12
f32 = jnp.float32
bf16 = jnp.bfloat16
i32 = jnp.int32
VM = pl.BlockSpec(memory_space=pltpu.VMEM)
SM = pl.BlockSpec(memory_space=pltpu.SMEM)
HB = pl.BlockSpec(memory_space=pltpu.HBM)


def dot(a, b):
    return jnp.dot(a, b, preferred_element_type=f32)


def dot_nt(a, b):
    return lax.dot_general(a, b, (((1,), (1,)), ((), ())), preferred_element_type=f32)


def split(x):
    high = x.astype(bf16)
    return high, (x - high.astype(f32)).astype(bf16)


def cosine(x):
    turns = jnp.round(x * (1.0 / math.pi))
    r = x - turns * 3.140625
    r = r - turns * 9.675025939941406e-4
    r = r - turns * 1.5099579909783764e-7
    s = r * r
    p = -2.755731922398589e-7 + s * 2.08767569878681e-9
    p = 2.48015873015873e-5 + s * p
    p = -1.3888888888888889e-3 + s * p
    p = 4.1666666666666664e-2 + s * p
    p = -0.5 + s * p
    p = 1.0 + s * p
    half = turns * 0.5
    odd = half - jnp.floor(half)
    return p * (1.0 - 4.0 * odd)


def run(kernel, args, in_specs, out_shape, out_specs, **rest):
    args = [
        pltpu.with_memory_space_constraint(a, pltpu.HBM) if spec is HB else a
        for a, spec in zip(args, in_specs)
    ]
    outs = [
        pltpu.HBM(o.shape, o.dtype) if spec is HB else o for o, spec in zip(out_shape, out_specs)
    ]
    return pl.pallas_call(
        kernel, out_shape=outs, in_specs=in_specs, out_specs=list(out_specs), **rest
    )(*args)


def params(mib):
    return pltpu.CompilerParams(vmem_limit_bytes=mib << 20)


def cost(flops, nbytes):
    return pl.CostEstimate(flops=int(flops), bytes_accessed=int(nbytes), transcendentals=0)


def move_rows(count, load, store):
    def body(t, carry):
        base = pl.multiple_of(t * UNROLL, UNROLL)
        for part in range(0, UNROLL, 16):
            rows = [load(base + part + u) for u in range(16)]
            for u in range(16):
                store(base + part + u, rows[u])
        return carry

    lax.fori_loop(0, count // UNROLL, body, 0)


def pack_rows(count, src, src_base, dst, dst_base):
    def body(t, carry):
        r = pl.multiple_of(t * 16, 16)
        for half in range(2):
            dst[pl.ds(dst_base + r, 16), half * LANES : (half + 1) * LANES] = src[
                pl.ds(2 * (src_base + r) + half, 16, stride=2), :
            ].astype(bf16)
        return carry

    lax.fori_loop(0, count // 16, body, 0, unroll=4)


def start_table(memory, raw, sem):
    step = memory.shape[0] // CHUNKS
    loads = [
        pltpu.make_async_copy(
            memory.at[pl.ds(c * step, step)], raw.at[pl.ds(c * step, step)], sem.at[c]
        )
        for c in range(CHUNKS)
    ]
    for copy in loads:
        copy.start()
    return loads


def widen_table(loads, raw, table):
    step = raw.shape[0] // len(loads)
    for c in range(len(loads)):
        loads[c].wait()

        def widen(t, carry):
            r = pl.multiple_of(c * step + t * 64, 64)
            rows = raw[pl.ds(r, 64), :].astype(f32)
            for half in range(2):
                table[pl.ds(2 * r + half, 64, stride=2), :] = rows[
                    :, half * LANES : (half + 1) * LANES
                ]
            return carry

        lax.fori_loop(0, step // 64, widen, 0, unroll=2)


def source_kernel(idx_hbm, memory, rows_out, idx, raw, table, stage, in_sem, idx_sem):
    loads = start_table(memory, raw, in_sem)
    idx_load = pltpu.make_async_copy(idx_hbm, idx, idx_sem)
    idx_load.start()
    widen_table(loads, raw, table)
    idx_load.wait()

    def put(k, row):
        stage[pl.ds(2 * k, 2), :] = row

    move_rows(idx.shape[0], lambda k: table[pl.ds(2 * idx[k], 2), :], put)
    pack_rows(idx.shape[0], stage, 0, rows_out, 0)


def gather_sources(evt_src, node_memory):
    nodes, width = node_memory.shape
    events = evt_src.shape[0]
    return run(
        source_kernel,
        [evt_src, node_memory],
        out_shape=(jax.ShapeDtypeStruct((events, width), bf16),),
        in_specs=[HB, HB],
        out_specs=(VM,),
        scratch_shapes=[
            pltpu.SMEM(evt_src.shape, i32),
            pltpu.VMEM((nodes, width), bf16),
            pltpu.VMEM((2 * nodes, LANES), f32),
            pltpu.VMEM((2 * events, LANES), f32),
            pltpu.SemaphoreType.DMA((CHUNKS,)),
            pltpu.SemaphoreType.DMA,
        ],
        compiler_params=params(24),
        cost_estimate=cost(0, 20e6),
        name="source_rows",
    )[0]


def prepare_kernel(
    dst_s,
    seen_hbm,
    memory,
    dst_row,
    dst_col,
    time_row,
    freq,
    phase,
    msg_hbm,
    mem_hbm,
    bias,
    pre_hbm,
    inv_hbm,
    rows_hbm,
    seen_s,
    raw,
    table,
    stage,
    seen_pick,
    seen_row,
    codes,
    msg_weight,
    mem_weight,
    pre_out,
    inv_out,
    rows_out,
    sem,
    out_sem,
    table_sem,
):
    events = dst_s.shape[0]
    width = rows_out.shape[1]
    code_width = freq.shape[0]
    loads = [
        pltpu.make_async_copy(a, b, sem.at[k])
        for k, (a, b) in enumerate(
            [(seen_hbm, seen_s), (msg_hbm, msg_weight), (mem_hbm, mem_weight)]
        )
    ]
    for copy in loads:
        copy.start()
    table_loads = start_table(memory, raw, table_sem)
    loads[0].wait()

    def look(t, carry):
        base = t * 8
        at = [dst_s[base + u] for u in range(8)]
        got = [seen_s[a] for a in at]
        for u in range(8):
            seen_pick[0, base + u] = got[u]
        return carry

    lax.fori_loop(0, events // 8, look, 0)
    across = pltpu.make_async_copy(seen_pick, seen_row, sem.at[3])
    across.start()
    widen_table(table_loads, raw, table)

    def put(k, row):
        stage[pl.ds(2 * k, 2), :] = row

    move_rows(events, lambda k: table[pl.ds(2 * dst_s[k], 2), :], put)
    pack_rows(events, stage, 0, rows_out, 0)
    across.wait()
    for t in range(events // LANES):
        at = pl.ds(t * LANES, LANES)
        delta = (time_row[:, at] - seen_row[:, at]).astype(f32)
        codes[at, :code_width] = jnp.transpose(cosine(freq[...] * delta + phase[...])).astype(bf16)
    codes[:, code_width:] = jnp.ones((events, LANES), bf16)
    loads[1].wait()
    loads[2].wait()
    step = min(ROWS, events)

    def block(t, carry):
        r = pl.multiple_of(t * step, step)
        same = jnp.where(dst_col[pl.ds(r, step), :] == dst_row[...], 1.0, 0.0).astype(bf16)
        sums = dot(same, codes[...])
        inv = 1.0 / jnp.maximum(sums[:, code_width:], 1.0)
        code_agg = (sums[:, :code_width] * inv).astype(bf16)
        inv_out[pl.ds(r, step), :] = inv
        memory = rows_out[pl.ds(r, step), :]
        part = dot(code_agg, msg_weight[pl.ds(width, code_width), :]) + bias[...]
        joined = dot(memory, mem_weight[...])
        third = 3 * width
        pre_out[pl.ds(r, step), : 2 * width] = (
            part[:, : 2 * width] + joined[:, : 2 * width] + joined[:, third : third + 2 * width]
        )
        pre_out[pl.ds(r, step), 2 * width : third] = (
            part[:, 2 * width :] + joined[:, 2 * width : third]
        )
        pre_out[pl.ds(r, step), third:] = joined[:, third + 2 * width :]
        return carry

    outs = [(rows_out, rows_hbm), (inv_out, inv_hbm), (pre_out, pre_hbm)]

    def save(k, t):
        r = pl.multiple_of(t * step, step)
        a, b = outs[k]
        return pltpu.make_async_copy(a.at[pl.ds(r, step)], b.at[pl.ds(r, step)], out_sem.at[k, t])

    def run(t, carry):
        block(t, carry)
        for k in range(3):
            save(k, t).start()
        return carry

    lax.fori_loop(0, events // step, run, 0)

    def drain(t, carry):
        for k in range(3):
            save(k, t).wait()
        return carry

    lax.fori_loop(0, events // step, drain, 0)


def prepare(dst, last_update, node_memory, dst_row, dst_col, time_row, freq, phase, msg_weight, mem_weight, bias):
    events = dst.shape[0]
    width = mem_weight.shape[0]
    return run(
        prepare_kernel,
        [dst, last_update, node_memory, dst_row, dst_col, time_row, freq, phase, msg_weight, mem_weight, bias],
        out_shape=(
            jax.ShapeDtypeStruct((events, 4 * width), f32),
            jax.ShapeDtypeStruct((events, LANES), f32),
            jax.ShapeDtypeStruct((events, width), bf16),
        ),
        in_specs=[SM, HB, HB] + [VM] * 5 + [HB, HB, VM],
        out_specs=(HB, HB, HB),
        scratch_shapes=[
            pltpu.SMEM(last_update.shape, i32),
            pltpu.VMEM(node_memory.shape, bf16),
            pltpu.VMEM((2 * node_memory.shape[0], LANES), f32),
            pltpu.VMEM((2 * events, LANES), f32),
            pltpu.SMEM((1, events), i32),
            pltpu.VMEM((1, events), i32),
            pltpu.VMEM((events, freq.shape[0] + LANES), bf16),
            pltpu.VMEM(msg_weight.shape, bf16),
            pltpu.VMEM(mem_weight.shape, bf16),
            pltpu.VMEM((events, 4 * width), f32),
            pltpu.VMEM((events, LANES), f32),
            pltpu.VMEM((events, width), bf16),
            pltpu.SemaphoreType.DMA((4,)),
            pltpu.SemaphoreType.DMA((3, events // min(ROWS, events))),
            pltpu.SemaphoreType.DMA((CHUNKS,)),
        ],
        compiler_params=params(48),
        cost_estimate=cost(6e9, 30e6),
        name="prepare",
    )


def update_kernel(
    dst_s,
    req_s,
    qry_s,
    memory,
    got,
    dst_row,
    dst_col,
    pre_hbm,
    inv_hbm,
    rows_hbm,
    msg_hbm,
    found_hbm,
    query_out,
    memory_out,
    raw,
    table,
    updated,
    stage,
    packed,
    pre,
    inv,
    rows,
    msg_weight,
    sem,
    block_sem,
    out_sem,
    table_sem,
):
    events, width = rows.shape
    step = min(ROWS, events)
    blocks = [(rows_hbm, rows), (inv_hbm, inv), (pre_hbm, pre)]

    def fetch(k, t):
        r = pl.multiple_of(t * step, step)
        a, b = blocks[k]
        return pltpu.make_async_copy(a.at[pl.ds(r, step)], b.at[pl.ds(r, step)], block_sem.at[k, t])

    weight_load = pltpu.make_async_copy(msg_hbm.at[pl.ds(0, width)], msg_weight, sem.at[0])
    count = events // step
    share = raw.shape[0] // count

    def table_load(t):
        r = pl.multiple_of(t * share, share)
        return pltpu.make_async_copy(
            memory.at[pl.ds(r, share)], raw.at[pl.ds(r, share)], table_sem.at[t]
        )

    for k in range(3):
        fetch(k, 0).start()
    weight_load.start()

    def block(t, carry):
        r = pl.multiple_of(t * step, step)
        same = jnp.where(dst_col[pl.ds(r, step), :] == dst_row[...], 1.0, 0.0).astype(bf16)
        sums = dot(same, got[...])
        for k in range(3):
            fetch(k, t).wait()

        @pl.when(t + 1 < count)
        def _():
            for k in range(3):
                fetch(k, t + 1).start()

        table_load(t).start()
        scale = inv[pl.ds(r, step), :]
        agg = jnp.concatenate(
            [sums[:, h * LANES : (h + 1) * LANES] * scale for h in range(width // LANES)], axis=1
        ).astype(bf16)
        msg = dot(agg, msg_weight[...])
        ready = pre[pl.ds(r, step), :]
        reset = jax.nn.sigmoid(msg[:, :width] + ready[:, :width])
        gate = jax.nn.sigmoid(msg[:, width : 2 * width] + ready[:, width : 2 * width])
        cand = jnp.tanh(
            msg[:, 2 * width :] + ready[:, 2 * width : 3 * width] + reset * ready[:, 3 * width :]
        )
        new = (1.0 - gate) * cand + gate * rows[pl.ds(r, step), :].astype(f32)
        new = new.astype(bf16).astype(f32)
        for half in range(2):
            updated[pl.ds(2 * r + half, step, stride=2), :] = new[:, half * LANES : (half + 1) * LANES]
        return carry

    weight_load.wait()
    lax.fori_loop(0, count, block, 0)
    widen_table([table_load(t) for t in range(count)], raw, table)

    def put_table(k, row):
        table[pl.ds(2 * dst_s[k], 2), :] = row

    move_rows(events, lambda k: updated[pl.ds(2 * k, 2), :], put_table)
    saves = []
    for c in range(count):
        pack_rows(share, table, c * share, raw, c * share)
        save = pltpu.make_async_copy(
            raw.at[pl.ds(c * share, share)], memory_out.at[pl.ds(c * share, share)], table_sem.at[c]
        )
        save.start()
        saves.append(save)

    def put(k, row):
        stage[pl.ds(2 * k, 2), :] = row

    queries = qry_s.shape[0]
    move_rows(queries, lambda k: table[pl.ds(2 * qry_s[k], 2), :], put)
    pack_rows(queries, stage, 0, query_out, 0)
    total = req_s.shape[0]
    chunk = total // 4
    sends = []
    for c in range(4):
        move_rows(chunk, lambda k: table[pl.ds(req_s[c * chunk + k], 2), :], put)
        pack_rows(chunk, stage, 0, packed, c * chunk)
        send = pltpu.make_async_copy(
            packed.at[pl.ds(c * chunk, chunk)],
            found_hbm.at[pl.ds(c * chunk, chunk)],
            out_sem.at[c],
        )
        send.start()
        sends.append(send)
    for send in sends:
        send.wait()
    for save in saves:
        save.wait()


def update(dst, req2, qry_rows, node_memory, got, dst_row, dst_col, pre, inv, rows, msg_weight):
    events, width = got.shape
    queries = qry_rows.shape[0]
    total = req2.shape[0]
    return run(
        update_kernel,
        [dst, req2, qry_rows, node_memory, got, dst_row, dst_col, pre, inv, rows, msg_weight],
        out_shape=(
            jax.ShapeDtypeStruct((total, width), bf16),
            jax.ShapeDtypeStruct((queries, width), bf16),
            jax.ShapeDtypeStruct(node_memory.shape, bf16),
        ),
        in_specs=[SM, SM, SM, HB, VM, VM, VM, HB, HB, HB, HB],
        out_specs=(HB, VM, HB),
        scratch_shapes=[
            pltpu.VMEM(node_memory.shape, bf16),
            pltpu.VMEM((2 * node_memory.shape[0] + 16, LANES), f32),
            pltpu.VMEM((2 * events, LANES), f32),
            pltpu.VMEM((2 * (total // 4), LANES), f32),
            pltpu.VMEM((total, width), bf16),
            pltpu.VMEM(pre.shape, f32),
            pltpu.VMEM(inv.shape, f32),
            pltpu.VMEM(rows.shape, bf16),
            pltpu.VMEM((width, msg_weight.shape[1]), bf16),
            pltpu.SemaphoreType.DMA((1,)),
            pltpu.SemaphoreType.DMA((3, events // min(ROWS, events))),
            pltpu.SemaphoreType.DMA((4,)),
            pltpu.SemaphoreType.DMA((events // min(ROWS, events),)),
        ],
        compiler_params=params(44),
        cost_estimate=cost(4e9, 40e6),
        name="update",
    )


def invert_kernel(slots, values, out):
    total = slots.shape[1]
    high = total // LANES
    where = slots[...]
    rows = lax.broadcasted_iota(i32, (high, total), 0)
    at_row = rows == (where >> 7)
    lanes = lax.broadcasted_iota(i32, (LANES, total), 0)
    at_lane = jnp.where(lanes == (where & 127), 1.0, 0.0).astype(bf16)
    result = jnp.zeros((high, LANES), i32)
    for digit in range(3):
        part = ((values[...] >> (8 * digit)) & 255).astype(f32)
        spread = jnp.where(at_row, part, 0.0).astype(bf16)
        result = result + (dot_nt(spread, at_lane).astype(i32) << (8 * digit))
    out[...] = result


def invert(slots, values):
    total = slots.shape[1]
    return run(
        invert_kernel,
        [slots, values],
        out_shape=(jax.ShapeDtypeStruct((total // LANES, LANES), i32),),
        in_specs=[VM, VM],
        out_specs=(VM,),
        compiler_params=params(24),
        cost_estimate=cost(1e9, 5e6),
        name="invert",
    )[0]


def project_kernel(
    shift,
    query,
    info,
    freq,
    phase,
    query_weight,
    kv_weight,
    qx_hbm,
    qe_hbm,
    et_hbm,
    qx_out,
    qe_out,
    et_out,
    sem,
):
    width = query_weight.shape[0]
    head_dim = width // HEADS
    queries = query.shape[0]
    vec = dot(query[...], query_weight[...]) * (1.0 / math.sqrt(head_dim))
    for h in range(HEADS):
        high, low = split(vec[:, h * head_dim : (h + 1) * head_dim])
        keys = kv_weight[:, h * head_dim : (h + 1) * head_dim]
        folded = dot_nt(high, keys) + dot_nt(low, keys)
        parts = split(folded)
        for k in range(2):
            rows = pl.ds((2 * h + k) * queries, queries)
            qx_out[rows, :] = parts[k][:, :width]
            qe_out[rows, :] = parts[k][:, width:]
    step = 256
    slots = info.shape[1]
    for t in range(slots // step):
        delta = ((info[:, pl.ds(t * step, step)] >> shift) - (1 << TIME_BITS)).astype(f32)
        et_out[:, pl.ds(t * step, step)] = cosine(freq[...] * delta + phase[...]).astype(bf16)
    pairs = ((qx_out, qx_hbm), (qe_out, qe_hbm), (et_out, et_hbm))
    copies = [pltpu.make_async_copy(a, b, sem.at[k]) for k, (a, b) in enumerate(pairs)]
    for copy in copies:
        copy.start()
    for copy in copies:
        copy.wait()


def project(shift, query, info, freq, phase, query_weight, kv_weight):
    queries, width = query.shape
    slots = info.shape[1]
    code_width = freq.shape[0]
    return run(
        functools.partial(project_kernel, shift),
        [query, info, freq, phase, query_weight, kv_weight],
        out_shape=(
            jax.ShapeDtypeStruct((2 * HEADS * queries, width), bf16),
            jax.ShapeDtypeStruct((2 * HEADS * queries, code_width), bf16),
            jax.ShapeDtypeStruct((code_width, slots), bf16),
        ),
        in_specs=[VM] * 6,
        out_specs=(HB, HB, HB),
        scratch_shapes=[
            pltpu.VMEM((2 * HEADS * queries, width), bf16),
            pltpu.VMEM((2 * HEADS * queries, code_width), bf16),
            pltpu.VMEM((code_width, slots), bf16),
            pltpu.SemaphoreType.DMA((3,)),
        ],
        compiler_params=params(16),
        cost_estimate=cost(1e9, 5e6),
        name="project",
    )


def attend_kernel(
    shift,
    sub,
    got,
    qx_hbm,
    qe_hbm,
    et_hbm,
    info,
    kv_hbm,
    part_out,
    lse_out,
    qx,
    qe,
    et,
    kv_weight,
    sem,
):
    pairs = ((qx_hbm, qx), (et_hbm, et), (qe_hbm, qe), (kv_hbm, kv_weight))
    copies = [pltpu.make_async_copy(a, b, sem.at[k]) for k, (a, b) in enumerate(pairs)]
    for copy in copies:
        copy.start()
    for copy in copies:
        copy.wait()
    owners, both, width = got.shape
    per_peer = both // 2
    slots = owners * per_peer
    queries = qx.shape[0] // (2 * HEADS)
    head_dim = width // HEADS
    rows = got[:, sub * per_peer : (sub + 1) * per_peer, :].reshape(slots, width)
    codes = et[...]
    who = info[...] & ((1 << shift) - 1)
    mask = lax.broadcasted_iota(i32, (queries, slots), 0) == who
    logs = []
    for h in range(HEADS):
        high = pl.ds(2 * h * queries, queries)
        low = pl.ds((2 * h + 1) * queries, queries)
        scores = dot_nt(qx[high, :], rows) + dot_nt(qx[low, :], rows)
        scores = scores + dot(qe[high, :], codes) + dot(qe[low, :], codes)
        scores = jnp.where(mask, scores, NEG)
        top = jnp.max(scores, axis=1, keepdims=True)
        weights = jnp.where(mask, jnp.exp(scores - top), 0.0).astype(bf16)
        total = jnp.sum(weights.astype(f32), axis=1, keepdims=True)
        some = total > 0.0
        inv = jnp.where(some, 1.0 / jnp.where(some, total, 1.0), 0.0)
        logs.append(jnp.where(some, top + jnp.log(jnp.where(some, total, 1.0)), NEG))
        mem_high, mem_low = split(dot(weights, rows) * inv)
        code_high, code_low = split(dot_nt(weights, codes) * inv)
        lanes = slice(width + h * head_dim, width + (h + 1) * head_dim)
        value_mem = kv_weight[:width, lanes]
        value_code = kv_weight[width:, lanes]
        part = dot(mem_high, value_mem) + dot(mem_low, value_mem)
        part = part + dot(code_high, value_code) + dot(code_low, value_code)
        part_out[:, h * head_dim : (h + 1) * head_dim] = part.astype(part_out.dtype)
    lane = lax.broadcasted_iota(i32, (queries, LANES), 1)
    spread = jnp.where((lane & 7) < 4, logs[0], logs[1])
    lse_out[...] = jnp.transpose(spread)[:8, :]


def attend(shift, sub, got, qx, qe, et, info, kv_weight, kind, name):
    queries = qx.shape[0] // (2 * HEADS)
    width = got.shape[2]
    return run(
        functools.partial(attend_kernel, shift, sub),
        [got, qx, qe, et, info, kv_weight],
        out_shape=(
            jax.ShapeDtypeStruct((queries, width), kind),
            jax.ShapeDtypeStruct((8, queries), f32),
        ),
        in_specs=[VM, HB, HB, HB, VM, HB],
        out_specs=(VM, VM),
        scratch_shapes=[pltpu.VMEM(a.shape, bf16) for a in (qx, qe, et, kv_weight)]
        + [pltpu.SemaphoreType.DMA((4,))],
        compiler_params=params(32),
        cost_estimate=cost(4e9, 5e6),
        name=name,
    )


def merge_kernel(mine, mine_lse, other, other_lse, query, out_weight, out):
    queries, width = mine.shape
    head_dim = width // HEADS
    pieces = []
    for h in range(HEADS):
        lanes = slice(h * head_dim, (h + 1) * head_dim)
        lse_a = jnp.transpose(jnp.broadcast_to(mine_lse[pl.ds(4 * h, 1), :], (LANES, queries)))
        lse_b = jnp.transpose(jnp.broadcast_to(other_lse[pl.ds(4 * h, 1), :], (LANES, queries)))
        top = jnp.maximum(lse_a, lse_b)
        weight_a = jnp.exp(lse_a - top)
        weight_b = jnp.exp(lse_b - top)
        inv = 1.0 / (weight_a + weight_b)
        pieces.append(
            mine[:, lanes] * (weight_a * inv) + other[:, lanes].astype(f32) * (weight_b * inv)
        )
    attended = jnp.concatenate(pieces, axis=1).astype(bf16)
    result = dot(attended, out_weight[:width, :]) + dot(query[...], out_weight[width:, :])
    out[...] = result.astype(bf16)


def merge(mine, mine_lse, other, other_lse, query, out_weight):
    return pl.pallas_call(
        merge_kernel,
        out_shape=jax.ShapeDtypeStruct(query.shape, bf16),
        in_specs=[VM] * 6,
        out_specs=VM,
        compiler_params=params(8),
        cost_estimate=cost(1e8, 1e6),
        name="merge",
    )(mine, mine_lse, other, other_lse, query, out_weight)


def local(
    group_count,
    mem_count,
    node_memory,
    last_update,
    evt_src,
    evt_dst,
    evt_time,
    evt_counts,
    time_freq,
    time_phase,
    msg_weight,
    mem_weight,
    gru_bias,
    qry_rows,
    qry_time,
    nbr_time,
    nbr_slot,
    req_rows,
    query_weight,
    kv_weight,
    out_weight,
):
    peers = group_count * mem_count
    side_peers = peers // 2
    half_groups = group_count // 2
    nodes, width = node_memory.shape
    events = evt_src.shape[0]
    cap = events // peers
    queries, fan_out = nbr_time.shape
    total_slots = queries * fan_out
    per_peer = total_slots // peers
    side_slots = side_peers * per_peer
    shift = (queries - 1).bit_length()
    side = lax.axis_index("grp") // half_groups
    sides = [list(range(s * side_peers, (s + 1) * side_peers)) for s in range(2)]
    opposite = [(g, (g + half_groups) % group_count) for g in range(group_count)]

    def mine_other(pair):
        return jnp.where(side == 0, pair[0], pair[1]), jnp.where(side == 0, pair[1], pair[0])

    is_live = jnp.arange(cap, dtype=i32)[None, :] < evt_counts[0][:, None]
    target = jnp.where(is_live, evt_dst.reshape(peers, cap), nodes)
    ids = jnp.concatenate(
        [(target << TIME_BITS) + evt_time.reshape(peers, cap), req_rows.reshape(peers, per_peer)],
        axis=1,
    )
    got_ids = lax.all_to_all(ids, AXES, split_axis=0, concat_axis=0, tiled=True)
    sent_rows = gather_sources(evt_src, node_memory)
    got_rows = lax.all_to_all(
        sent_rows.reshape(peers, cap, width), AXES, split_axis=0, concat_axis=0, tiled=True
    ).reshape(events, width)

    packed = got_ids[:, :cap].reshape(events)
    dst = packed >> TIME_BITS
    time_row = (packed & ((1 << TIME_BITS) - 1)).reshape(1, events)
    dst_row = jnp.where(dst < nodes, dst, -1).reshape(1, events)
    dst_col = dst.reshape(events, 1)
    mine, other = mine_other(got_ids[:, cap:].reshape(2, side_peers, per_peer))
    req2 = 2 * jnp.concatenate([mine, other], axis=1).reshape(total_slots)
    freq = time_freq.reshape(-1, 1)
    phase = time_phase.reshape(-1, 1)
    bias = gru_bias.reshape(1, -1)
    delta = qry_time[:, None] - nbr_time + (1 << TIME_BITS)
    values = (delta << shift) + jnp.arange(queries, dtype=i32)[:, None]
    info = invert(nbr_slot, values.reshape(1, total_slots))
    info_mine, info_send = mine_other(info.reshape(2, 1, side_slots))
    req2, info_send = lax.optimization_barrier((req2, info_send))
    info_other = lax.ppermute(info_send, "grp", opposite)
    pre, inv, rows = prepare(
        jnp.minimum(dst, nodes - 1),
        last_update,
        node_memory,
        dst_row,
        dst_col,
        time_row,
        freq,
        phase,
        msg_weight,
        mem_weight,
        bias,
    )
    found, query_mem, new_memory = update(
        dst, req2, qry_rows, node_memory, got_rows, dst_row, dst_col, pre, inv, rows, msg_weight
    )
    query_other = lax.ppermute(query_mem, "grp", opposite)
    got = lax.all_to_all(
        found.reshape(side_peers, 2 * per_peer, width),
        AXES,
        split_axis=0,
        concat_axis=0,
        tiled=True,
        axis_index_groups=sides,
    )

    args = (freq, phase, query_weight, kv_weight)
    qx_b, qe_b, et_b = project(shift, query_other, info_other, *args)
    qx_a, qe_a, et_a = project(shift, query_mem, info_mine, *args)
    part_b, lse_b = attend(shift, 1, got, qx_b, qe_b, et_b, info_other, kv_weight, bf16, "attend_other")
    back, back_lse = lax.ppermute(part_b, "grp", opposite), lax.ppermute(lse_b, "grp", opposite)
    part_a, lse_a = attend(shift, 0, got, qx_a, qe_a, et_a, info_mine, kv_weight, f32, "attend_mine")
    embeddings = merge(part_a, lse_a, back, back_lse, query_mem, out_weight)
    return new_memory, embeddings


def solution(mesh):
    split_rows = P(AXES, None)
    split_flat = P(AXES)
    in_specs = (
        split_rows,
        split_flat,
        split_flat,
        split_flat,
        split_flat,
        split_rows,
        P(),
        P(),
        P(),
        P(),
        P(),
        split_flat,
        split_flat,
        split_rows,
        split_rows,
        split_flat,
        P(),
        P(),
        P(),
    )
    body = functools.partial(local, mesh.shape["grp"], mesh.shape["mem"])
    return jax.shard_map(
        body, mesh=mesh, in_specs=in_specs, out_specs=(split_rows, split_rows), check_vma=False
    )
```

```python
import functools
import math

import jax
import jax.numpy as jnp
from jax import lax
from jax.experimental import pallas as pl
from jax.experimental.pallas import tpu as pltpu
from jax.sharding import PartitionSpec as P


HEADS = 2
AXES = ("grp", "mem")
LANES = 128
UNROLL = 32
ROWS = 512
SENDS = 8
CHUNKS = 8
NEG = -1e30
TIME_BITS = 12
f32 = jnp.float32
bf16 = jnp.bfloat16
i32 = jnp.int32
VM = pl.BlockSpec(memory_space=pltpu.VMEM)
SM = pl.BlockSpec(memory_space=pltpu.SMEM)
HB = pl.BlockSpec(memory_space=pltpu.HBM)


def dot(a, b):
    return jnp.dot(a, b, preferred_element_type=f32)


def dot_nt(a, b):
    return lax.dot_general(a, b, (((1,), (1,)), ((), ())), preferred_element_type=f32)


def split(x):
    high = x.astype(bf16)
    return high, (x - high.astype(f32)).astype(bf16)


def cosine(x):
    turns = jnp.round(x * (1.0 / math.pi))
    r = x - turns * 3.140625
    r = r - turns * 9.675025939941406e-4
    r = r - turns * 1.5099579909783764e-7
    s = r * r
    p = -2.755731922398589e-7 + s * 2.08767569878681e-9
    p = 2.48015873015873e-5 + s * p
    p = -1.3888888888888889e-3 + s * p
    p = 4.1666666666666664e-2 + s * p
    p = -0.5 + s * p
    p = 1.0 + s * p
    half = turns * 0.5
    odd = half - jnp.floor(half)
    return p * (1.0 - 4.0 * odd)


def run(kernel, args, in_specs, out_shape, out_specs, **rest):
    args = [
        pltpu.with_memory_space_constraint(a, pltpu.HBM) if spec is HB else a
        for a, spec in zip(args, in_specs)
    ]
    outs = [
        pltpu.HBM(o.shape, o.dtype) if spec is HB else o for o, spec in zip(out_shape, out_specs)
    ]
    return pl.pallas_call(
        kernel, out_shape=outs, in_specs=in_specs, out_specs=list(out_specs), **rest
    )(*args)


def params(mib):
    return pltpu.CompilerParams(vmem_limit_bytes=mib << 20)


def cost(flops, nbytes):
    return pl.CostEstimate(flops=int(flops), bytes_accessed=int(nbytes), transcendentals=0)


def move_rows(count, load, store):
    def body(t, carry):
        base = pl.multiple_of(t * UNROLL, UNROLL)
        for part in range(0, UNROLL, 16):
            rows = [load(base + part + u) for u in range(16)]
            for u in range(16):
                store(base + part + u, rows[u])
        return carry

    lax.fori_loop(0, count // UNROLL, body, 0)


def pack_rows(count, src, src_base, dst, dst_base):
    def body(t, carry):
        r = pl.multiple_of(t * 16, 16)
        for half in range(2):
            dst[pl.ds(dst_base + r, 16), half * LANES : (half + 1) * LANES] = src[
                pl.ds(2 * (src_base + r) + half, 16, stride=2), :
            ].astype(bf16)
        return carry

    lax.fori_loop(0, count // 16, body, 0, unroll=4)


def gather_rows(index, first, count, scale, table, stage, dst, dst_base):
    def pack(at):
        for r in range(0, UNROLL, 16):
            for half in range(2):
                dst[pl.ds(dst_base + at + r, 16), half * LANES : (half + 1) * LANES] = stage[
                    pl.ds(2 * (at + r) + half, 16, stride=2), :
                ].astype(bf16)

    def body(t, carry):
        base = pl.multiple_of(t * UNROLL, UNROLL)
        last = pl.multiple_of(jnp.maximum(t - 1, 0) * UNROLL, UNROLL)
        for part in range(0, UNROLL, 16):
            rows = [
                table[pl.ds(scale * index[first + base + part + u], 2), :] for u in range(16)
            ]
            for u in range(16):
                stage[pl.ds(2 * (base + part + u), 2), :] = rows[u]
        pack(last)
        return carry

    lax.fori_loop(0, count // UNROLL, body, 0)
    pack(count - UNROLL)


def start_table(memory, raw, sem):
    step = memory.shape[0] // CHUNKS
    loads = [
        pltpu.make_async_copy(
            memory.at[pl.ds(c * step, step)], raw.at[pl.ds(c * step, step)], sem.at[c]
        )
        for c in range(CHUNKS)
    ]
    for copy in loads:
        copy.start()
    return loads


def widen_table(loads, raw, table):
    step = raw.shape[0] // len(loads)
    for c in range(len(loads)):
        loads[c].wait()

        def widen(t, carry):
            r = pl.multiple_of(c * step + t * 64, 64)
            rows = raw[pl.ds(r, 64), :].astype(f32)
            for half in range(2):
                table[pl.ds(2 * r + half, 64, stride=2), :] = rows[
                    :, half * LANES : (half + 1) * LANES
                ]
            return carry

        lax.fori_loop(0, step // 64, widen, 0, unroll=2)


def source_kernel(idx_hbm, memory, rows_out, idx, raw, table, stage, in_sem, idx_sem):
    loads = start_table(memory, raw, in_sem)
    idx_load = pltpu.make_async_copy(idx_hbm, idx, idx_sem)
    idx_load.start()
    widen_table(loads, raw, table)
    idx_load.wait()
    gather_rows(idx, 0, idx.shape[0], 2, table, stage, rows_out, 0)


def gather_sources(evt_src, node_memory):
    nodes, width = node_memory.shape
    events = evt_src.shape[0]
    return run(
        source_kernel,
        [evt_src, node_memory],
        out_shape=(jax.ShapeDtypeStruct((events, width), bf16),),
        in_specs=[HB, HB],
        out_specs=(VM,),
        scratch_shapes=[
            pltpu.SMEM(evt_src.shape, i32),
            pltpu.VMEM((nodes, width), bf16),
            pltpu.VMEM((2 * nodes, LANES), f32),
            pltpu.VMEM((2 * events, LANES), f32),
            pltpu.SemaphoreType.DMA((CHUNKS,)),
            pltpu.SemaphoreType.DMA,
        ],
        compiler_params=params(24),
        cost_estimate=cost(0, 20e6),
        name="source_rows",
    )[0]


def prepare_kernel(
    dst_s,
    seen,
    memory,
    dst_row,
    dst_col,
    time_row,
    freq,
    phase,
    msg_hbm,
    mem_hbm,
    bias,
    pre_hbm,
    inv_hbm,
    rows_hbm,
    raw,
    table,
    stage,
    codes,
    msg_weight,
    mem_weight,
    pre_out,
    inv_out,
    rows_out,
    sem,
    out_sem,
    table_sem,
):
    events = dst_s.shape[0]
    width = rows_out.shape[1]
    code_width = freq.shape[0]
    pairs = ((msg_hbm, msg_weight), (mem_hbm, mem_weight))
    loads = [pltpu.make_async_copy(a, b, sem.at[k]) for k, (a, b) in enumerate(pairs)]
    table_loads = start_table(memory, raw, table_sem)
    for copy in loads:
        copy.start()
    target = dst_row[...]
    groups = seen.shape[0]
    at_group = lax.broadcasted_iota(i32, (groups, events), 0) == (target >> 7)
    at_group = jnp.where(at_group, 1.0, 0.0).astype(bf16)
    by_lane = jnp.transpose(seen[...].astype(f32)).astype(i32)
    high = dot((by_lane >> 8).astype(f32).astype(bf16), at_group)
    low = dot((by_lane & 255).astype(f32).astype(bf16), at_group)
    at_lane = lax.broadcasted_iota(i32, (LANES, events), 0) == (target & 127)
    last = jnp.sum(jnp.where(at_lane, 256.0 * high + low, 0.0), axis=0, keepdims=True)
    delta = time_row[...].astype(f32) - last
    for t in range(events // LANES):
        at = pl.ds(t * LANES, LANES)
        part = delta[:, t * LANES : (t + 1) * LANES]
        codes[at, :code_width] = jnp.transpose(cosine(freq[...] * part + phase[...])).astype(bf16)
    codes[:, code_width:] = jnp.ones((events, LANES), bf16)
    widen_table(table_loads, raw, table)
    gather_rows(dst_s, 0, events, 2, table, stage, rows_out, 0)
    for copy in loads:
        copy.wait()
    step = min(ROWS, events)

    def block(t, carry):
        r = pl.multiple_of(t * step, step)
        same = jnp.where(dst_col[pl.ds(r, step), :] == dst_row[...], 1.0, 0.0).astype(bf16)
        sums = dot(same, codes[...])
        inv = 1.0 / jnp.maximum(sums[:, code_width:], 1.0)
        code_agg = (sums[:, :code_width] * inv).astype(bf16)
        inv_out[pl.ds(r, step), :] = inv
        memory = rows_out[pl.ds(r, step), :]
        part = dot(code_agg, msg_weight[pl.ds(width, code_width), :]) + bias[...]
        joined = dot(memory, mem_weight[...])
        third = 3 * width
        pre_out[pl.ds(r, step), : 2 * width] = (
            part[:, : 2 * width] + joined[:, : 2 * width] + joined[:, third : third + 2 * width]
        ).astype(bf16)
        pre_out[pl.ds(r, step), 2 * width : third] = (
            part[:, 2 * width :] + joined[:, 2 * width : third]
        ).astype(bf16)
        pre_out[pl.ds(r, step), third:] = joined[:, third + 2 * width :].astype(bf16)
        return carry

    outs = [(rows_out, rows_hbm), (inv_out, inv_hbm), (pre_out, pre_hbm)]

    def save(k, t):
        r = pl.multiple_of(t * step, step)
        a, b = outs[k]
        return pltpu.make_async_copy(a.at[pl.ds(r, step)], b.at[pl.ds(r, step)], out_sem.at[k, t])

    def run(t, carry):
        block(t, carry)
        for k in range(3):
            save(k, t).start()
        return carry

    lax.fori_loop(0, events // step, run, 0)

    def drain(t, carry):
        for k in range(3):
            save(k, t).wait()
        return carry

    lax.fori_loop(0, events // step, drain, 0)


def prepare(dst, last_update, node_memory, dst_row, dst_col, time_row, freq, phase, msg_weight, mem_weight, bias):
    events = dst.shape[0]
    width = mem_weight.shape[0]
    return run(
        prepare_kernel,
        [dst, last_update, node_memory, dst_row, dst_col, time_row, freq, phase, msg_weight, mem_weight, bias],
        out_shape=(
            jax.ShapeDtypeStruct((events, 4 * width), bf16),
            jax.ShapeDtypeStruct((events, LANES), f32),
            jax.ShapeDtypeStruct((events, width), bf16),
        ),
        in_specs=[SM, VM, HB] + [VM] * 5 + [HB, HB, VM],
        out_specs=(HB, HB, HB),
        scratch_shapes=[
            pltpu.VMEM(node_memory.shape, bf16),
            pltpu.VMEM((2 * node_memory.shape[0], LANES), f32),
            pltpu.VMEM((2 * events, LANES), f32),
            pltpu.VMEM((events, freq.shape[0] + LANES), bf16),
            pltpu.VMEM(msg_weight.shape, bf16),
            pltpu.VMEM(mem_weight.shape, bf16),
            pltpu.VMEM((events, 4 * width), bf16),
            pltpu.VMEM((events, LANES), f32),
            pltpu.VMEM((events, width), bf16),
            pltpu.SemaphoreType.DMA((2,)),
            pltpu.SemaphoreType.DMA((3, events // min(ROWS, events))),
            pltpu.SemaphoreType.DMA((CHUNKS,)),
        ],
        compiler_params=params(48),
        cost_estimate=cost(6e9, 30e6),
        name="prepare",
    )


def update_kernel(
    dst_s,
    req_s,
    qry_s,
    memory,
    got,
    dst_row,
    dst_col,
    pre_hbm,
    inv_hbm,
    rows_hbm,
    msg_hbm,
    found_hbm,
    query_out,
    memory_out,
    raw,
    table,
    updated,
    stage,
    packed,
    pre,
    inv,
    rows,
    msg_weight,
    sem,
    block_sem,
    out_sem,
    table_sem,
):
    events, width = rows.shape
    step = min(ROWS, events)
    blocks = [(rows_hbm, rows), (inv_hbm, inv), (pre_hbm, pre)]

    def fetch(k, t):
        r = pl.multiple_of(t * step, step)
        a, b = blocks[k]
        return pltpu.make_async_copy(a.at[pl.ds(r, step)], b.at[pl.ds(r, step)], block_sem.at[k, t])

    weight_load = pltpu.make_async_copy(msg_hbm.at[pl.ds(0, width)], msg_weight, sem.at[0])
    count = events // step
    share = raw.shape[0] // count

    def table_load(t):
        r = pl.multiple_of(t * share, share)
        return pltpu.make_async_copy(
            memory.at[pl.ds(r, share)], raw.at[pl.ds(r, share)], table_sem.at[t]
        )

    for k in range(3):
        fetch(k, 0).start()
    weight_load.start()
    if count > 1:
        for k in range(3):
            fetch(k, 1).start()

    def block(t, carry):
        r = pl.multiple_of(t * step, step)
        same = jnp.where(dst_col[pl.ds(r, step), :] == dst_row[...], 1.0, 0.0).astype(bf16)
        sums = dot(same, got[...])
        for k in range(3):
            fetch(k, t).wait()

        @pl.when(t + 2 < count)
        def _():
            for k in range(3):
                fetch(k, t + 2).start()

        @pl.when(t < count // 2)
        def _():
            table_load(2 * t).start()
            table_load(2 * t + 1).start()

        scale = inv[pl.ds(r, step), :]
        agg = jnp.concatenate(
            [sums[:, h * LANES : (h + 1) * LANES] * scale for h in range(width // LANES)], axis=1
        ).astype(bf16)
        msg = dot(agg, msg_weight[...])
        ready = pre[pl.ds(r, step), :].astype(f32)
        reset = jax.nn.sigmoid(msg[:, :width] + ready[:, :width])
        gate = jax.nn.sigmoid(msg[:, width : 2 * width] + ready[:, width : 2 * width])
        cand = jnp.tanh(
            msg[:, 2 * width :] + ready[:, 2 * width : 3 * width] + reset * ready[:, 3 * width :]
        )
        new = (1.0 - gate) * cand + gate * rows[pl.ds(r, step), :].astype(f32)
        new = new.astype(bf16).astype(f32)
        for half in range(2):
            updated[pl.ds(2 * r + half, step, stride=2), :] = new[:, half * LANES : (half + 1) * LANES]
        return carry

    weight_load.wait()
    lax.fori_loop(0, count, block, 0)
    widen_table([table_load(t) for t in range(count)], raw, table)

    def put_table(k, row):
        table[pl.ds(2 * dst_s[k], 2), :] = row

    move_rows(events, lambda k: updated[pl.ds(2 * k, 2), :], put_table)
    saves = []
    for c in range(count):
        pack_rows(share, table, c * share, raw, c * share)
        save = pltpu.make_async_copy(
            raw.at[pl.ds(c * share, share)], memory_out.at[pl.ds(c * share, share)], table_sem.at[c]
        )
        save.start()
        saves.append(save)

    queries = qry_s.shape[0]
    gather_rows(qry_s, 0, queries, 2, table, stage, query_out, 0)
    total = req_s.shape[0]
    chunk = total // SENDS
    sends = []
    for c in range(SENDS):
        gather_rows(req_s, c * chunk, chunk, 1, table, stage, packed, c * chunk)
        send = pltpu.make_async_copy(
            packed.at[pl.ds(c * chunk, chunk)],
            found_hbm.at[pl.ds(c * chunk, chunk)],
            out_sem.at[c],
        )
        send.start()
        sends.append(send)
    for send in sends:
        send.wait()
    for save in saves:
        save.wait()


def update(dst, req2, qry_rows, node_memory, got, dst_row, dst_col, pre, inv, rows, msg_weight):
    events, width = got.shape
    queries = qry_rows.shape[0]
    total = req2.shape[0]
    return run(
        update_kernel,
        [dst, req2, qry_rows, node_memory, got, dst_row, dst_col, pre, inv, rows, msg_weight],
        out_shape=(
            jax.ShapeDtypeStruct((total, width), bf16),
            jax.ShapeDtypeStruct((queries, width), bf16),
            jax.ShapeDtypeStruct(node_memory.shape, bf16),
        ),
        in_specs=[SM, SM, SM, HB, VM, VM, VM, HB, HB, HB, HB],
        out_specs=(HB, VM, HB),
        scratch_shapes=[
            pltpu.VMEM(node_memory.shape, bf16),
            pltpu.VMEM((2 * node_memory.shape[0] + 16, LANES), f32),
            pltpu.VMEM((2 * events, LANES), f32),
            pltpu.VMEM((2 * max(total // SENDS, queries), LANES), f32),
            pltpu.VMEM((total, width), bf16),
            pltpu.VMEM(pre.shape, bf16),
            pltpu.VMEM(inv.shape, f32),
            pltpu.VMEM(rows.shape, bf16),
            pltpu.VMEM((width, msg_weight.shape[1]), bf16),
            pltpu.SemaphoreType.DMA((1,)),
            pltpu.SemaphoreType.DMA((3, events // min(ROWS, events))),
            pltpu.SemaphoreType.DMA((SENDS,)),
            pltpu.SemaphoreType.DMA((events // min(ROWS, events),)),
        ],
        compiler_params=params(44),
        cost_estimate=cost(4e9, 40e6),
        name="update",
    )


def invert_kernel(slots, values, out):
    total = slots.shape[1]
    high = total // LANES
    where = slots[...]
    rows = lax.broadcasted_iota(i32, (high, total), 0)
    at_row = rows == (where >> 7)
    lanes = lax.broadcasted_iota(i32, (LANES, total), 0)
    at_lane = jnp.where(lanes == (where & 127), 1.0, 0.0).astype(bf16)
    result = jnp.zeros((high, LANES), i32)
    for digit in range(3):
        part = ((values[...] >> (8 * digit)) & 255).astype(f32)
        spread = jnp.where(at_row, part, 0.0).astype(bf16)
        result = result + (dot_nt(spread, at_lane).astype(i32) << (8 * digit))
    out[...] = result


def invert(slots, values):
    total = slots.shape[1]
    return run(
        invert_kernel,
        [slots, values],
        out_shape=(jax.ShapeDtypeStruct((total // LANES, LANES), i32),),
        in_specs=[VM, VM],
        out_specs=(VM,),
        compiler_params=params(24),
        cost_estimate=cost(1e9, 5e6),
        name="invert",
    )[0]


def project_kernel(
    shift,
    query,
    info,
    freq,
    phase,
    query_weight,
    kv_weight,
    qx_hbm,
    et_hbm,
    se_hbm,
    qx,
    et,
    se,
    sem,
):
    width = query_weight.shape[0]
    head_dim = width // HEADS
    queries = query.shape[0]
    step = 256
    slots = info.shape[1]
    who = info[...] & ((1 << shift) - 1)
    delta = ((info[...] >> shift) - (1 << TIME_BITS)).astype(f32)
    for t in range(slots // step):
        part = delta[:, t * step : (t + 1) * step]
        et[:, pl.ds(t * step, step)] = cosine(freq[...] * part + phase[...]).astype(bf16)
    mask = lax.broadcasted_iota(i32, (queries, slots), 0) == who
    vec = dot(query[...], query_weight[...]) * (1.0 / math.sqrt(head_dim))
    for h in range(HEADS):
        high, low = split(vec[:, h * head_dim : (h + 1) * head_dim])
        keys = kv_weight[:, h * head_dim : (h + 1) * head_dim]
        folded = dot_nt(high, keys) + dot_nt(low, keys)
        high, low = split(folded)
        rows = pl.ds(2 * h * queries, queries)
        qx[rows, :] = high[:, :width]
        qx[pl.ds((2 * h + 1) * queries, queries), :] = low[:, :width]
        scores = dot(high[:, width:], et[...]) + dot(low[:, width:], et[...])
        se[pl.ds(h * queries, queries), :] = jnp.where(mask, scores, NEG)
    pairs = ((qx, qx_hbm), (et, et_hbm), (se, se_hbm))
    copies = [pltpu.make_async_copy(a, b, sem.at[k]) for k, (a, b) in enumerate(pairs)]
    for copy in copies:
        copy.start()
    for copy in copies:
        copy.wait()


def project(shift, query, info, freq, phase, query_weight, kv_weight):
    queries, width = query.shape
    slots = info.shape[1]
    outs = (
        jax.ShapeDtypeStruct((2 * HEADS * queries, width), bf16),
        jax.ShapeDtypeStruct((freq.shape[0], slots), bf16),
        jax.ShapeDtypeStruct((HEADS * queries, slots), f32),
    )
    return run(
        functools.partial(project_kernel, shift),
        [query, info, freq, phase, query_weight, kv_weight],
        out_shape=outs,
        in_specs=[VM] * 6,
        out_specs=(HB, HB, HB),
        scratch_shapes=[pltpu.VMEM(o.shape, o.dtype) for o in outs] + [pltpu.SemaphoreType.DMA((3,))],
        compiler_params=params(32),
        cost_estimate=cost(1e9, 10e6),
        name="project",
    )


def attend_kernel(
    sub,
    got,
    qx_hbm,
    et_hbm,
    se_hbm,
    kv_hbm,
    part_out,
    lse_out,
    qx,
    et,
    se,
    kv_weight,
    sem,
    se_sem,
):
    owners, both, width = got.shape
    per_peer = both // 2
    slots = owners * per_peer
    queries = qx.shape[0] // (2 * HEADS)
    head_dim = width // HEADS
    pairs = ((qx_hbm, qx), (et_hbm, et), (kv_hbm, kv_weight))
    copies = [pltpu.make_async_copy(a, b, sem.at[k]) for k, (a, b) in enumerate(pairs)]

    def load_se(h):
        at = pl.ds(h * queries, queries)
        return pltpu.make_async_copy(se_hbm.at[at], se.at[at], se_sem.at[h])

    for copy in copies:
        copy.start()
    for h in range(HEADS):
        load_se(h).start()
    rows = got[:, sub * per_peer : (sub + 1) * per_peer, :].reshape(slots, width)
    logs = []
    for h in range(HEADS):
        if h == 0:
            copies[0].wait()
        both_parts = dot_nt(qx[pl.ds(2 * h * queries, 2 * queries), :], rows)
        load_se(h).wait()
        scores = both_parts[:queries] + both_parts[queries:] + se[pl.ds(h * queries, queries), :]
        top = jnp.maximum(jnp.max(scores, axis=1, keepdims=True), 0.1 * NEG)
        weights = jnp.exp(scores - top).astype(bf16)
        total = jnp.sum(weights.astype(f32), axis=1, keepdims=True)
        some = total > 0.0
        inv = jnp.where(some, 1.0 / jnp.where(some, total, 1.0), 0.0)
        logs.append(jnp.where(some, top + jnp.log(jnp.where(some, total, 1.0)), NEG))
        if h == 0:
            copies[1].wait()
            copies[2].wait()
        mem_high, mem_low = split(dot(weights, rows) * inv)
        code_high, code_low = split(dot_nt(weights, et[...]) * inv)
        lanes = slice(width + h * head_dim, width + (h + 1) * head_dim)
        value_mem = kv_weight[:width, lanes]
        value_code = kv_weight[width:, lanes]
        part = dot(mem_high, value_mem) + dot(mem_low, value_mem)
        part = part + dot(code_high, value_code) + dot(code_low, value_code)
        part_out[:, h * head_dim : (h + 1) * head_dim] = part.astype(part_out.dtype)
    lane = lax.broadcasted_iota(i32, (queries, LANES), 1)
    spread = jnp.where((lane & 7) < 4, logs[0], logs[1])
    lse_out[...] = jnp.transpose(spread)[:8, :]


def attend(sub, got, qx, et, se, kv_weight, kind, name):
    queries = qx.shape[0] // (2 * HEADS)
    width = got.shape[2]
    return run(
        functools.partial(attend_kernel, sub),
        [got, qx, et, se, kv_weight],
        out_shape=(
            jax.ShapeDtypeStruct((queries, width), kind),
            jax.ShapeDtypeStruct((8, queries), f32),
        ),
        in_specs=[VM, HB, HB, HB, HB],
        out_specs=(VM, VM),
        scratch_shapes=[pltpu.VMEM(a.shape, a.dtype) for a in (qx, et, se, kv_weight)]
        + [pltpu.SemaphoreType.DMA((3,)), pltpu.SemaphoreType.DMA((HEADS,))],
        compiler_params=params(40),
        cost_estimate=cost(4e9, 10e6),
        name=name,
    )


def merge_kernel(mine, mine_lse, other, other_lse, query, out_weight, out):
    queries, width = mine.shape
    head_dim = width // HEADS
    pieces = []
    for h in range(HEADS):
        lanes = slice(h * head_dim, (h + 1) * head_dim)
        lse_a = jnp.transpose(jnp.broadcast_to(mine_lse[pl.ds(4 * h, 1), :], (LANES, queries)))
        lse_b = jnp.transpose(jnp.broadcast_to(other_lse[pl.ds(4 * h, 1), :], (LANES, queries)))
        top = jnp.maximum(lse_a, lse_b)
        weight_a = jnp.exp(lse_a - top)
        weight_b = jnp.exp(lse_b - top)
        inv = 1.0 / (weight_a + weight_b)
        pieces.append(
            mine[:, lanes] * (weight_a * inv) + other[:, lanes].astype(f32) * (weight_b * inv)
        )
    attended = jnp.concatenate(pieces, axis=1).astype(bf16)
    result = dot(attended, out_weight[:width, :]) + dot(query[...], out_weight[width:, :])
    out[...] = result.astype(bf16)


def merge(mine, mine_lse, other, other_lse, query, out_weight):
    return pl.pallas_call(
        merge_kernel,
        out_shape=jax.ShapeDtypeStruct(query.shape, bf16),
        in_specs=[VM] * 6,
        out_specs=VM,
        compiler_params=params(8),
        cost_estimate=cost(1e8, 1e6),
        name="merge",
    )(mine, mine_lse, other, other_lse, query, out_weight)


def local(
    group_count,
    mem_count,
    node_memory,
    last_update,
    evt_src,
    evt_dst,
    evt_time,
    evt_counts,
    time_freq,
    time_phase,
    msg_weight,
    mem_weight,
    gru_bias,
    qry_rows,
    qry_time,
    nbr_time,
    nbr_slot,
    req_rows,
    query_weight,
    kv_weight,
    out_weight,
):
    peers = group_count * mem_count
    side_peers = peers // 2
    half_groups = group_count // 2
    nodes, width = node_memory.shape
    events = evt_src.shape[0]
    cap = events // peers
    queries, fan_out = nbr_time.shape
    total_slots = queries * fan_out
    per_peer = total_slots // peers
    side_slots = side_peers * per_peer
    shift = (queries - 1).bit_length()
    side = lax.axis_index("grp") // half_groups
    sides = [list(range(s * side_peers, (s + 1) * side_peers)) for s in range(2)]
    opposite = [(g, (g + half_groups) % group_count) for g in range(group_count)]

    def mine_other(pair):
        return jnp.where(side == 0, pair[0], pair[1]), jnp.where(side == 0, pair[1], pair[0])

    is_live = jnp.arange(cap, dtype=i32)[None, :] < evt_counts[0][:, None]
    target = jnp.where(is_live, evt_dst.reshape(peers, cap), nodes)
    ids = jnp.concatenate(
        [(target << TIME_BITS) + evt_time.reshape(peers, cap), req_rows.reshape(peers, per_peer)],
        axis=1,
    )
    got_ids = lax.all_to_all(ids, AXES, split_axis=0, concat_axis=0, tiled=True)
    sent_rows = gather_sources(evt_src, node_memory)
    got_rows = lax.all_to_all(
        sent_rows.reshape(peers, cap, width), AXES, split_axis=0, concat_axis=0, tiled=True
    ).reshape(events, width)

    packed = got_ids[:, :cap].reshape(events)
    dst = packed >> TIME_BITS
    time_row = (packed & ((1 << TIME_BITS) - 1)).reshape(1, events)
    dst_row = jnp.where(dst < nodes, dst, -1).reshape(1, events)
    dst_col = dst.reshape(events, 1)
    mine, other = mine_other(got_ids[:, cap:].reshape(2, side_peers, per_peer))
    req2 = 2 * jnp.concatenate([mine, other], axis=1).reshape(total_slots)
    freq = time_freq.reshape(-1, 1)
    phase = time_phase.reshape(-1, 1)
    bias = gru_bias.reshape(1, -1)
    delta = qry_time[:, None] - nbr_time + (1 << TIME_BITS)
    values = (delta << shift) + jnp.arange(queries, dtype=i32)[:, None]
    info = invert(nbr_slot, values.reshape(1, total_slots))
    info_mine, info_send = mine_other(info.reshape(2, 1, side_slots))
    req2, info_send = lax.optimization_barrier((req2, info_send))
    info_other = lax.ppermute(info_send, "grp", opposite)
    pre, inv, rows = prepare(
        jnp.minimum(dst, nodes - 1),
        last_update.reshape(-1, LANES),
        node_memory,
        dst_row,
        dst_col,
        time_row,
        freq,
        phase,
        msg_weight,
        mem_weight,
        bias,
    )
    found, query_mem, new_memory = update(
        dst, req2, qry_rows, node_memory, got_rows, dst_row, dst_col, pre, inv, rows, msg_weight
    )
    query_other = lax.ppermute(query_mem, "grp", opposite)
    got = lax.all_to_all(
        found.reshape(side_peers, 2 * per_peer, width),
        AXES,
        split_axis=0,
        concat_axis=0,
        tiled=True,
        axis_index_groups=sides,
    )

    args = (freq, phase, query_weight, kv_weight)
    other = project(shift, query_other, info_other, *args)
    own = project(shift, query_mem, info_mine, *args)
    part_b, lse_b = attend(1, got, *other, kv_weight, bf16, "attend_other")
    back, back_lse = lax.ppermute(part_b, "grp", opposite), lax.ppermute(lse_b, "grp", opposite)
    part_a, lse_a = attend(0, got, *own, kv_weight, f32, "attend_mine")
    embeddings = merge(part_a, lse_a, back, back_lse, query_mem, out_weight)
    return new_memory, embeddings


def solution(mesh):
    split_rows = P(AXES, None)
    split_flat = P(AXES)
    in_specs = (
        split_rows,
        split_flat,
        split_flat,
        split_flat,
        split_flat,
        split_rows,
        P(),
        P(),
        P(),
        P(),
        P(),
        split_flat,
        split_flat,
        split_rows,
        split_rows,
        split_flat,
        P(),
        P(),
        P(),
    )
    body = functools.partial(local, mesh.shape["grp"], mesh.shape["mem"])
    return jax.shard_map(
        body, mesh=mesh, in_specs=in_specs, out_specs=(split_rows, split_rows), check_vma=False
    )
```

```python
import functools
import math

import jax
import jax.numpy as jnp
from jax import lax
from jax.experimental import pallas as pl
from jax.experimental.pallas import tpu as pltpu
from jax.sharding import PartitionSpec as P


HEADS = 2
AXES = ("grp", "mem")
LANES = 128
UNROLL = 32
ROWS = 512
SENDS = 8
CHUNKS = 8
NEG = -1e30
TIME_BITS = 12
f32 = jnp.float32
bf16 = jnp.bfloat16
i32 = jnp.int32
VM = pl.BlockSpec(memory_space=pltpu.VMEM)
SM = pl.BlockSpec(memory_space=pltpu.SMEM)
HB = pl.BlockSpec(memory_space=pltpu.HBM)


def dot(a, b):
    return jnp.dot(a, b, preferred_element_type=f32)


def dot_nt(a, b):
    return lax.dot_general(a, b, (((1,), (1,)), ((), ())), preferred_element_type=f32)


def split(x):
    high = x.astype(bf16)
    return high, (x - high.astype(f32)).astype(bf16)


def cosine(x):
    turns = jnp.round(x * (1.0 / math.pi))
    r = x - turns * 3.140625
    r = r - turns * 9.675025939941406e-4
    r = r - turns * 1.5099579909783764e-7
    s = r * r
    p = -2.755731922398589e-7 + s * 2.08767569878681e-9
    p = 2.48015873015873e-5 + s * p
    p = -1.3888888888888889e-3 + s * p
    p = 4.1666666666666664e-2 + s * p
    p = -0.5 + s * p
    p = 1.0 + s * p
    half = turns * 0.5
    odd = half - jnp.floor(half)
    return p * (1.0 - 4.0 * odd)


def run(kernel, args, in_specs, out_shape, out_specs, **rest):
    args = [
        pltpu.with_memory_space_constraint(a, pltpu.HBM) if spec is HB else a
        for a, spec in zip(args, in_specs)
    ]
    outs = [
        pltpu.HBM(o.shape, o.dtype) if spec is HB else o for o, spec in zip(out_shape, out_specs)
    ]
    return pl.pallas_call(
        kernel, out_shape=outs, in_specs=in_specs, out_specs=list(out_specs), **rest
    )(*args)


def params(mib):
    return pltpu.CompilerParams(vmem_limit_bytes=mib << 20)


def cost(flops, nbytes):
    return pl.CostEstimate(flops=int(flops), bytes_accessed=int(nbytes), transcendentals=0)


def move_rows(count, load, store):
    def body(t, carry):
        base = pl.multiple_of(t * UNROLL, UNROLL)
        for part in range(0, UNROLL, 16):
            rows = [load(base + part + u) for u in range(16)]
            for u in range(16):
                store(base + part + u, rows[u])
        return carry

    lax.fori_loop(0, count // UNROLL, body, 0)


def pack_rows(count, src, src_base, dst, dst_base):
    def body(t, carry):
        r = pl.multiple_of(t * 16, 16)
        for half in range(2):
            dst[pl.ds(dst_base + r, 16), half * LANES : (half + 1) * LANES] = src[
                pl.ds(2 * (src_base + r) + half, 16, stride=2), :
            ].astype(bf16)
        return carry

    lax.fori_loop(0, count // 16, body, 0, unroll=4)


def gather_rows(index, first, count, scale, table, stage, dst, dst_base):
    def pack(at):
        for r in range(0, UNROLL, 16):
            for half in range(2):
                dst[pl.ds(dst_base + at + r, 16), half * LANES : (half + 1) * LANES] = stage[
                    pl.ds(2 * (at + r) + half, 16, stride=2), :
                ].astype(bf16)

    def body(t, carry):
        base = pl.multiple_of(t * UNROLL, UNROLL)
        last = pl.multiple_of(jnp.maximum(t - 1, 0) * UNROLL, UNROLL)
        for part in range(0, UNROLL, 16):
            rows = [
                table[pl.ds(scale * index[first + base + part + u], 2), :] for u in range(16)
            ]
            for u in range(16):
                stage[pl.ds(2 * (base + part + u), 2), :] = rows[u]
        pack(last)
        return carry

    lax.fori_loop(0, count // UNROLL, body, 0)
    pack(count - UNROLL)


def start_table(memory, raw, sem):
    step = memory.shape[0] // CHUNKS
    loads = [
        pltpu.make_async_copy(
            memory.at[pl.ds(c * step, step)], raw.at[pl.ds(c * step, step)], sem.at[c]
        )
        for c in range(CHUNKS)
    ]
    for copy in loads:
        copy.start()
    return loads


def widen_table(loads, raw, table):
    step = raw.shape[0] // len(loads)
    for c in range(len(loads)):
        loads[c].wait()

        def widen(t, carry):
            r = pl.multiple_of(c * step + t * 64, 64)
            rows = raw[pl.ds(r, 64), :].astype(f32)
            for half in range(2):
                table[pl.ds(2 * r + half, 64, stride=2), :] = rows[
                    :, half * LANES : (half + 1) * LANES
                ]
            return carry

        lax.fori_loop(0, step // 64, widen, 0, unroll=2)


def source_kernel(idx_hbm, memory, rows_out, idx, raw, table, stage, in_sem, idx_sem):
    loads = start_table(memory, raw, in_sem)
    idx_load = pltpu.make_async_copy(idx_hbm, idx, idx_sem)
    idx_load.start()
    widen_table(loads, raw, table)
    idx_load.wait()
    gather_rows(idx, 0, idx.shape[0], 2, table, stage, rows_out, 0)


def gather_sources(evt_src, node_memory):
    nodes, width = node_memory.shape
    events = evt_src.shape[0]
    return run(
        source_kernel,
        [evt_src, node_memory],
        out_shape=(jax.ShapeDtypeStruct((events, width), bf16),),
        in_specs=[HB, HB],
        out_specs=(VM,),
        scratch_shapes=[
            pltpu.SMEM(evt_src.shape, i32),
            pltpu.VMEM((nodes, width), bf16),
            pltpu.VMEM((2 * nodes, LANES), f32),
            pltpu.VMEM((2 * events, LANES), f32),
            pltpu.SemaphoreType.DMA((CHUNKS,)),
            pltpu.SemaphoreType.DMA,
        ],
        compiler_params=params(24),
        cost_estimate=cost(0, 20e6),
        name="source_rows",
    )[0]


def prepare_kernel(
    dst_s,
    seen,
    memory,
    dst_row,
    dst_col,
    time_row,
    freq,
    phase,
    msg_hbm,
    mem_hbm,
    bias,
    pre_hbm,
    inv_hbm,
    rows_hbm,
    raw,
    table,
    stage,
    codes,
    msg_weight,
    mem_weight,
    pre_out,
    inv_out,
    rows_out,
    sem,
    out_sem,
    table_sem,
):
    events = dst_s.shape[0]
    width = rows_out.shape[1]
    code_width = freq.shape[0]
    pairs = ((msg_hbm, msg_weight), (mem_hbm, mem_weight))
    loads = [pltpu.make_async_copy(a, b, sem.at[k]) for k, (a, b) in enumerate(pairs)]
    table_loads = start_table(memory, raw, table_sem)
    for copy in loads:
        copy.start()
    target = dst_row[...]
    groups = seen.shape[0]
    at_group = lax.broadcasted_iota(i32, (groups, events), 0) == (target >> 7)
    at_group = jnp.where(at_group, 1.0, 0.0).astype(bf16)
    by_lane = jnp.transpose(seen[...].astype(f32)).astype(i32)
    high = dot((by_lane >> 8).astype(f32).astype(bf16), at_group)
    low = dot((by_lane & 255).astype(f32).astype(bf16), at_group)
    at_lane = lax.broadcasted_iota(i32, (LANES, events), 0) == (target & 127)
    last = jnp.sum(jnp.where(at_lane, 256.0 * high + low, 0.0), axis=0, keepdims=True)
    delta = time_row[...].astype(f32) - last
    for t in range(events // LANES):
        at = pl.ds(t * LANES, LANES)
        part = delta[:, t * LANES : (t + 1) * LANES]
        codes[at, :code_width] = jnp.transpose(cosine(freq[...] * part + phase[...])).astype(bf16)
    codes[:, code_width:] = jnp.ones((events, LANES), bf16)
    widen_table(table_loads, raw, table)
    gather_rows(dst_s, 0, events, 2, table, stage, rows_out, 0)
    for copy in loads:
        copy.wait()
    step = min(ROWS, events)

    def block(t, carry):
        r = pl.multiple_of(t * step, step)
        same = jnp.where(dst_col[pl.ds(r, step), :] == dst_row[...], 1.0, 0.0).astype(bf16)
        sums = dot(same, codes[...])
        inv = 1.0 / jnp.maximum(sums[:, code_width:], 1.0)
        code_agg = (sums[:, :code_width] * inv).astype(bf16)
        inv_out[pl.ds(r, step), :] = inv
        memory = rows_out[pl.ds(r, step), :]
        part = dot(code_agg, msg_weight[pl.ds(width, code_width), :]) + bias[...]
        joined = dot(memory, mem_weight[...])
        third = 3 * width
        pre_out[pl.ds(r, step), : 2 * width] = (
            part[:, : 2 * width] + joined[:, : 2 * width] + joined[:, third : third + 2 * width]
        ).astype(bf16)
        pre_out[pl.ds(r, step), 2 * width : third] = (
            part[:, 2 * width :] + joined[:, 2 * width : third]
        ).astype(bf16)
        pre_out[pl.ds(r, step), third:] = joined[:, third + 2 * width :].astype(bf16)
        return carry

    outs = [(rows_out, rows_hbm), (inv_out, inv_hbm), (pre_out, pre_hbm)]

    def save(k, t):
        r = pl.multiple_of(t * step, step)
        a, b = outs[k]
        return pltpu.make_async_copy(a.at[pl.ds(r, step)], b.at[pl.ds(r, step)], out_sem.at[k, t])

    def run(t, carry):
        block(t, carry)
        for k in range(3):
            save(k, t).start()
        return carry

    lax.fori_loop(0, events // step, run, 0)

    def drain(t, carry):
        for k in range(3):
            save(k, t).wait()
        return carry

    lax.fori_loop(0, events // step, drain, 0)


def prepare(dst, last_update, node_memory, dst_row, dst_col, time_row, freq, phase, msg_weight, mem_weight, bias):
    events = dst.shape[0]
    width = mem_weight.shape[0]
    return run(
        prepare_kernel,
        [dst, last_update, node_memory, dst_row, dst_col, time_row, freq, phase, msg_weight, mem_weight, bias],
        out_shape=(
            jax.ShapeDtypeStruct((events, 4 * width), bf16),
            jax.ShapeDtypeStruct((events, LANES), f32),
            jax.ShapeDtypeStruct((events, width), bf16),
        ),
        in_specs=[SM, VM, HB] + [VM] * 5 + [HB, HB, VM],
        out_specs=(HB, HB, HB),
        scratch_shapes=[
            pltpu.VMEM(node_memory.shape, bf16),
            pltpu.VMEM((2 * node_memory.shape[0], LANES), f32),
            pltpu.VMEM((2 * events, LANES), f32),
            pltpu.VMEM((events, freq.shape[0] + LANES), bf16),
            pltpu.VMEM(msg_weight.shape, bf16),
            pltpu.VMEM(mem_weight.shape, bf16),
            pltpu.VMEM((events, 4 * width), bf16),
            pltpu.VMEM((events, LANES), f32),
            pltpu.VMEM((events, width), bf16),
            pltpu.SemaphoreType.DMA((2,)),
            pltpu.SemaphoreType.DMA((3, events // min(ROWS, events))),
            pltpu.SemaphoreType.DMA((CHUNKS,)),
        ],
        compiler_params=params(48),
        cost_estimate=cost(6e9, 30e6),
        name="prepare",
    )


def update_kernel(
    dst_s,
    req_s,
    qry_s,
    memory,
    got,
    dst_row,
    dst_col,
    pre_hbm,
    inv_hbm,
    rows_hbm,
    msg_hbm,
    found_hbm,
    query_out,
    new_hbm,
    raw,
    table,
    updated,
    new_rows,
    stage,
    packed,
    pre,
    inv,
    rows,
    msg_weight,
    sem,
    block_sem,
    out_sem,
    table_sem,
    new_sem,
):
    events, width = rows.shape
    step = min(ROWS, events)
    blocks = [(rows_hbm, rows), (inv_hbm, inv), (pre_hbm, pre)]

    def fetch(k, t):
        r = pl.multiple_of(t * step, step)
        a, b = blocks[k]
        return pltpu.make_async_copy(a.at[pl.ds(r, step)], b.at[pl.ds(r, step)], block_sem.at[k, t])

    weight_load = pltpu.make_async_copy(msg_hbm.at[pl.ds(0, width)], msg_weight, sem.at[0])
    count = events // step
    share = raw.shape[0] // count

    def put_new(t):
        at = pl.ds(pl.multiple_of(t * step, step), step)
        return pltpu.make_async_copy(new_rows.at[at], new_hbm.at[at], new_sem.at[t])

    def table_load(t):
        r = pl.multiple_of(t * share, share)
        return pltpu.make_async_copy(
            memory.at[pl.ds(r, share)], raw.at[pl.ds(r, share)], table_sem.at[t]
        )

    for k in range(3):
        fetch(k, 0).start()
    weight_load.start()
    if count > 1:
        for k in range(3):
            fetch(k, 1).start()

    def block(t, carry):
        r = pl.multiple_of(t * step, step)
        same = jnp.where(dst_col[pl.ds(r, step), :] == dst_row[...], 1.0, 0.0).astype(bf16)
        sums = dot(same, got[...])
        for k in range(3):
            fetch(k, t).wait()

        @pl.when(t + 2 < count)
        def _():
            for k in range(3):
                fetch(k, t + 2).start()

        @pl.when(t < count // 2)
        def _():
            table_load(2 * t).start()
            table_load(2 * t + 1).start()

        scale = inv[pl.ds(r, step), :]
        agg = jnp.concatenate(
            [sums[:, h * LANES : (h + 1) * LANES] * scale for h in range(width // LANES)], axis=1
        ).astype(bf16)
        msg = dot(agg, msg_weight[...])
        ready = pre[pl.ds(r, step), :].astype(f32)
        reset = jax.nn.sigmoid(msg[:, :width] + ready[:, :width])
        gate = jax.nn.sigmoid(msg[:, width : 2 * width] + ready[:, width : 2 * width])
        cand = jnp.tanh(
            msg[:, 2 * width :] + ready[:, 2 * width : 3 * width] + reset * ready[:, 3 * width :]
        )
        new = (1.0 - gate) * cand + gate * rows[pl.ds(r, step), :].astype(f32)
        new = new.astype(bf16)
        new_rows[pl.ds(r, step), :] = new
        put_new(t).start()
        new = new.astype(f32)
        for half in range(2):
            updated[pl.ds(2 * r + half, step, stride=2), :] = new[:, half * LANES : (half + 1) * LANES]
        return carry

    weight_load.wait()
    lax.fori_loop(0, count, block, 0)
    widen_table([table_load(t) for t in range(count)], raw, table)

    def put_table(k, row):
        table[pl.ds(2 * dst_s[k], 2), :] = row

    move_rows(events, lambda k: updated[pl.ds(2 * k, 2), :], put_table)
    queries = qry_s.shape[0]
    gather_rows(qry_s, 0, queries, 2, table, stage, query_out, 0)
    total = req_s.shape[0]
    chunk = total // SENDS
    sends = []
    for c in range(SENDS):
        gather_rows(req_s, c * chunk, chunk, 1, table, stage, packed, c * chunk)
        send = pltpu.make_async_copy(
            packed.at[pl.ds(c * chunk, chunk)],
            found_hbm.at[pl.ds(c * chunk, chunk)],
            out_sem.at[c],
        )
        send.start()
        sends.append(send)
    for send in sends:
        send.wait()
    for t in range(count):
        put_new(t).wait()


def update(dst, req2, qry_rows, node_memory, got, dst_row, dst_col, pre, inv, rows, msg_weight):
    events, width = got.shape
    queries = qry_rows.shape[0]
    total = req2.shape[0]
    return run(
        update_kernel,
        [dst, req2, qry_rows, node_memory, got, dst_row, dst_col, pre, inv, rows, msg_weight],
        out_shape=(
            jax.ShapeDtypeStruct((total, width), bf16),
            jax.ShapeDtypeStruct((queries, width), bf16),
            jax.ShapeDtypeStruct((events, width), bf16),
        ),
        in_specs=[SM, SM, SM, HB, VM, VM, VM, HB, HB, HB, HB],
        out_specs=(HB, VM, HB),
        scratch_shapes=[
            pltpu.VMEM(node_memory.shape, bf16),
            pltpu.VMEM((2 * node_memory.shape[0] + 16, LANES), f32),
            pltpu.VMEM((2 * events, LANES), f32),
            pltpu.VMEM((events, width), bf16),
            pltpu.VMEM((2 * max(total // SENDS, queries), LANES), f32),
            pltpu.VMEM((total, width), bf16),
            pltpu.VMEM(pre.shape, bf16),
            pltpu.VMEM(inv.shape, f32),
            pltpu.VMEM(rows.shape, bf16),
            pltpu.VMEM((width, msg_weight.shape[1]), bf16),
            pltpu.SemaphoreType.DMA((1,)),
            pltpu.SemaphoreType.DMA((3, events // min(ROWS, events))),
            pltpu.SemaphoreType.DMA((SENDS,)),
            pltpu.SemaphoreType.DMA((events // min(ROWS, events),)),
            pltpu.SemaphoreType.DMA((events // min(ROWS, events),)),
        ],
        compiler_params=params(44),
        cost_estimate=cost(4e9, 40e6),
        name="update",
    )


def write_back_kernel(dst_s, memory, new_hbm, memory_out, raw, new, table, updated, sem, new_sem):
    loads = start_table(memory, raw, sem)
    new_load = pltpu.make_async_copy(new_hbm, new, new_sem)
    new_load.start()
    widen_table(loads, raw, table)
    new_load.wait()
    events = new.shape[0]

    def spread(t, carry):
        r = pl.multiple_of(t * 64, 64)
        rows = new[pl.ds(r, 64), :].astype(f32)
        for half in range(2):
            updated[pl.ds(2 * r + half, 64, stride=2), :] = rows[:, half * LANES : (half + 1) * LANES]
        return carry

    lax.fori_loop(0, events // 64, spread, 0)

    def put(k, row):
        table[pl.ds(2 * dst_s[k], 2), :] = row

    move_rows(events, lambda k: updated[pl.ds(2 * k, 2), :], put)
    share = raw.shape[0] // CHUNKS
    saves = []
    for c in range(CHUNKS):
        pack_rows(share, table, c * share, raw, c * share)
        save = pltpu.make_async_copy(
            raw.at[pl.ds(c * share, share)], memory_out.at[pl.ds(c * share, share)], sem.at[c]
        )
        save.start()
        saves.append(save)
    for save in saves:
        save.wait()


def write_back(dst, node_memory, new):
    nodes, _ = node_memory.shape
    events = new.shape[0]
    return run(
        write_back_kernel,
        [dst, node_memory, new],
        out_shape=(jax.ShapeDtypeStruct(node_memory.shape, bf16),),
        in_specs=[SM, HB, HB],
        out_specs=(HB,),
        scratch_shapes=[
            pltpu.VMEM(node_memory.shape, bf16),
            pltpu.VMEM(new.shape, bf16),
            pltpu.VMEM((2 * nodes + 16, LANES), f32),
            pltpu.VMEM((2 * events, LANES), f32),
            pltpu.SemaphoreType.DMA((CHUNKS,)),
            pltpu.SemaphoreType.DMA,
        ],
        compiler_params=params(32),
        cost_estimate=cost(0, 20e6),
        name="write_back",
    )[0]


def invert_kernel(slots, values, out):
    total = slots.shape[1]
    high = total // LANES
    where = slots[...]
    rows = lax.broadcasted_iota(i32, (high, total), 0)
    at_row = rows == (where >> 7)
    lanes = lax.broadcasted_iota(i32, (LANES, total), 0)
    at_lane = jnp.where(lanes == (where & 127), 1.0, 0.0).astype(bf16)
    result = jnp.zeros((high, LANES), i32)
    for digit in range(3):
        part = ((values[...] >> (8 * digit)) & 255).astype(f32)
        spread = jnp.where(at_row, part, 0.0).astype(bf16)
        result = result + (dot_nt(spread, at_lane).astype(i32) << (8 * digit))
    out[...] = result


def invert(slots, values):
    total = slots.shape[1]
    return run(
        invert_kernel,
        [slots, values],
        out_shape=(jax.ShapeDtypeStruct((total // LANES, LANES), i32),),
        in_specs=[VM, VM],
        out_specs=(VM,),
        compiler_params=params(24),
        cost_estimate=cost(1e9, 5e6),
        name="invert",
    )[0]


def project_kernel(
    shift,
    query,
    info,
    freq,
    phase,
    query_weight,
    kv_weight,
    qx_hbm,
    et_hbm,
    se_hbm,
    qx,
    et,
    se,
    sem,
):
    width = query_weight.shape[0]
    head_dim = width // HEADS
    queries = query.shape[0]
    step = 256
    slots = info.shape[1]
    who = info[...] & ((1 << shift) - 1)
    delta = ((info[...] >> shift) - (1 << TIME_BITS)).astype(f32)
    for t in range(slots // step):
        part = delta[:, t * step : (t + 1) * step]
        et[:, pl.ds(t * step, step)] = cosine(freq[...] * part + phase[...]).astype(bf16)
    mask = lax.broadcasted_iota(i32, (queries, slots), 0) == who
    vec = dot(query[...], query_weight[...]) * (1.0 / math.sqrt(head_dim))
    for h in range(HEADS):
        high, low = split(vec[:, h * head_dim : (h + 1) * head_dim])
        keys = kv_weight[:, h * head_dim : (h + 1) * head_dim]
        folded = dot_nt(high, keys) + dot_nt(low, keys)
        high, low = split(folded)
        rows = pl.ds(2 * h * queries, queries)
        qx[rows, :] = high[:, :width]
        qx[pl.ds((2 * h + 1) * queries, queries), :] = low[:, :width]
        scores = dot(high[:, width:], et[...]) + dot(low[:, width:], et[...])
        se[pl.ds(h * queries, queries), :] = jnp.where(mask, scores, NEG)
    pairs = ((qx, qx_hbm), (et, et_hbm), (se, se_hbm))
    copies = [pltpu.make_async_copy(a, b, sem.at[k]) for k, (a, b) in enumerate(pairs)]
    for copy in copies:
        copy.start()
    for copy in copies:
        copy.wait()


def project(shift, query, info, freq, phase, query_weight, kv_weight):
    queries, width = query.shape
    slots = info.shape[1]
    outs = (
        jax.ShapeDtypeStruct((2 * HEADS * queries, width), bf16),
        jax.ShapeDtypeStruct((freq.shape[0], slots), bf16),
        jax.ShapeDtypeStruct((HEADS * queries, slots), f32),
    )
    return run(
        functools.partial(project_kernel, shift),
        [query, info, freq, phase, query_weight, kv_weight],
        out_shape=outs,
        in_specs=[VM] * 6,
        out_specs=(HB, HB, HB),
        scratch_shapes=[pltpu.VMEM(o.shape, o.dtype) for o in outs] + [pltpu.SemaphoreType.DMA((3,))],
        compiler_params=params(32),
        cost_estimate=cost(1e9, 10e6),
        name="project",
    )


def attend_kernel(
    sub,
    got,
    qx_hbm,
    et_hbm,
    se_hbm,
    kv_hbm,
    part_out,
    lse_out,
    qx,
    et,
    se,
    kv_weight,
    sem,
    se_sem,
):
    owners, both, width = got.shape
    per_peer = both // 2
    slots = owners * per_peer
    queries = qx.shape[0] // (2 * HEADS)
    head_dim = width // HEADS
    pairs = ((qx_hbm, qx), (et_hbm, et), (kv_hbm, kv_weight))
    copies = [pltpu.make_async_copy(a, b, sem.at[k]) for k, (a, b) in enumerate(pairs)]

    def load_se(h):
        at = pl.ds(h * queries, queries)
        return pltpu.make_async_copy(se_hbm.at[at], se.at[at], se_sem.at[h])

    for copy in copies:
        copy.start()
    for h in range(HEADS):
        load_se(h).start()
    rows = got[:, sub * per_peer : (sub + 1) * per_peer, :].reshape(slots, width)
    logs = []
    for h in range(HEADS):
        if h == 0:
            copies[0].wait()
        both_parts = dot_nt(qx[pl.ds(2 * h * queries, 2 * queries), :], rows)
        load_se(h).wait()
        scores = both_parts[:queries] + both_parts[queries:] + se[pl.ds(h * queries, queries), :]
        top = jnp.maximum(jnp.max(scores, axis=1, keepdims=True), 0.1 * NEG)
        weights = jnp.exp(scores - top).astype(bf16)
        total = jnp.sum(weights.astype(f32), axis=1, keepdims=True)
        some = total > 0.0
        inv = jnp.where(some, 1.0 / jnp.where(some, total, 1.0), 0.0)
        logs.append(jnp.where(some, top + jnp.log(jnp.where(some, total, 1.0)), NEG))
        if h == 0:
            copies[1].wait()
            copies[2].wait()
        mem_high, mem_low = split(dot(weights, rows) * inv)
        code_high, code_low = split(dot_nt(weights, et[...]) * inv)
        lanes = slice(width + h * head_dim, width + (h + 1) * head_dim)
        value_mem = kv_weight[:width, lanes]
        value_code = kv_weight[width:, lanes]
        part = dot(mem_high, value_mem) + dot(mem_low, value_mem)
        part = part + dot(code_high, value_code) + dot(code_low, value_code)
        part_out[:, h * head_dim : (h + 1) * head_dim] = part.astype(part_out.dtype)
    lane = lax.broadcasted_iota(i32, (queries, LANES), 1)
    spread = jnp.where((lane & 7) < 4, logs[0], logs[1])
    lse_out[...] = jnp.transpose(spread)[:8, :]


def attend(sub, got, qx, et, se, kv_weight, kind, name):
    queries = qx.shape[0] // (2 * HEADS)
    width = got.shape[2]
    return run(
        functools.partial(attend_kernel, sub),
        [got, qx, et, se, kv_weight],
        out_shape=(
            jax.ShapeDtypeStruct((queries, width), kind),
            jax.ShapeDtypeStruct((8, queries), f32),
        ),
        in_specs=[VM, HB, HB, HB, HB],
        out_specs=(VM, VM),
        scratch_shapes=[pltpu.VMEM(a.shape, a.dtype) for a in (qx, et, se, kv_weight)]
        + [pltpu.SemaphoreType.DMA((3,)), pltpu.SemaphoreType.DMA((HEADS,))],
        compiler_params=params(40),
        cost_estimate=cost(4e9, 10e6),
        name=name,
    )


def merge_kernel(mine, mine_lse, other, other_lse, query, out_weight, out):
    queries, width = mine.shape
    head_dim = width // HEADS
    pieces = []
    for h in range(HEADS):
        lanes = slice(h * head_dim, (h + 1) * head_dim)
        lse_a = jnp.transpose(jnp.broadcast_to(mine_lse[pl.ds(4 * h, 1), :], (LANES, queries)))
        lse_b = jnp.transpose(jnp.broadcast_to(other_lse[pl.ds(4 * h, 1), :], (LANES, queries)))
        top = jnp.maximum(lse_a, lse_b)
        weight_a = jnp.exp(lse_a - top)
        weight_b = jnp.exp(lse_b - top)
        inv = 1.0 / (weight_a + weight_b)
        pieces.append(
            mine[:, lanes] * (weight_a * inv) + other[:, lanes].astype(f32) * (weight_b * inv)
        )
    attended = jnp.concatenate(pieces, axis=1).astype(bf16)
    result = dot(attended, out_weight[:width, :]) + dot(query[...], out_weight[width:, :])
    out[...] = result.astype(bf16)


def merge(mine, mine_lse, other, other_lse, query, out_weight):
    return pl.pallas_call(
        merge_kernel,
        out_shape=jax.ShapeDtypeStruct(query.shape, bf16),
        in_specs=[VM] * 6,
        out_specs=VM,
        compiler_params=params(8),
        cost_estimate=cost(1e8, 1e6),
        name="merge",
    )(mine, mine_lse, other, other_lse, query, out_weight)


def local(
    group_count,
    mem_count,
    node_memory,
    last_update,
    evt_src,
    evt_dst,
    evt_time,
    evt_counts,
    time_freq,
    time_phase,
    msg_weight,
    mem_weight,
    gru_bias,
    qry_rows,
    qry_time,
    nbr_time,
    nbr_slot,
    req_rows,
    query_weight,
    kv_weight,
    out_weight,
):
    peers = group_count * mem_count
    side_peers = peers // 2
    half_groups = group_count // 2
    nodes, width = node_memory.shape
    events = evt_src.shape[0]
    cap = events // peers
    queries, fan_out = nbr_time.shape
    total_slots = queries * fan_out
    per_peer = total_slots // peers
    side_slots = side_peers * per_peer
    shift = (queries - 1).bit_length()
    side = lax.axis_index("grp") // half_groups
    sides = [list(range(s * side_peers, (s + 1) * side_peers)) for s in range(2)]
    opposite = [(g, (g + half_groups) % group_count) for g in range(group_count)]

    def mine_other(pair):
        return jnp.where(side == 0, pair[0], pair[1]), jnp.where(side == 0, pair[1], pair[0])

    is_live = jnp.arange(cap, dtype=i32)[None, :] < evt_counts[0][:, None]
    target = jnp.where(is_live, evt_dst.reshape(peers, cap), nodes)
    ids = jnp.concatenate(
        [(target << TIME_BITS) + evt_time.reshape(peers, cap), req_rows.reshape(peers, per_peer)],
        axis=1,
    )
    got_ids = lax.all_to_all(ids, AXES, split_axis=0, concat_axis=0, tiled=True)
    sent_rows = gather_sources(evt_src, node_memory)
    got_rows = lax.all_to_all(
        sent_rows.reshape(peers, cap, width), AXES, split_axis=0, concat_axis=0, tiled=True
    )
    got_rows = got_rows.reshape(events, width)
    qry_time, got_ids = lax.optimization_barrier((qry_time, got_ids))

    packed = got_ids[:, :cap].reshape(events)
    dst = packed >> TIME_BITS
    time_row = (packed & ((1 << TIME_BITS) - 1)).reshape(1, events)
    dst_row = jnp.where(dst < nodes, dst, -1).reshape(1, events)
    dst_col = dst.reshape(events, 1)
    mine, other = mine_other(got_ids[:, cap:].reshape(2, side_peers, per_peer))
    req2 = 2 * jnp.concatenate([mine, other], axis=1).reshape(total_slots)
    freq = time_freq.reshape(-1, 1)
    phase = time_phase.reshape(-1, 1)
    bias = gru_bias.reshape(1, -1)
    delta = qry_time[:, None] - nbr_time + (1 << TIME_BITS)
    values = (delta << shift) + jnp.arange(queries, dtype=i32)[:, None]
    info = invert(nbr_slot, values.reshape(1, total_slots))
    info_mine, info_send = mine_other(info.reshape(2, 1, side_slots))
    req2, info_send = lax.optimization_barrier((req2, info_send))
    info_other = lax.ppermute(info_send, "grp", opposite)
    pre, inv, rows = prepare(
        jnp.minimum(dst, nodes - 1),
        last_update.reshape(-1, LANES),
        node_memory,
        dst_row,
        dst_col,
        time_row,
        freq,
        phase,
        msg_weight,
        mem_weight,
        bias,
    )
    found, query_mem, new_rows = update(
        dst, req2, qry_rows, node_memory, got_rows, dst_row, dst_col, pre, inv, rows, msg_weight
    )
    query_other = lax.ppermute(query_mem, "grp", opposite)
    got = lax.all_to_all(
        found.reshape(side_peers, 2 * per_peer, width),
        AXES,
        split_axis=0,
        concat_axis=0,
        tiled=True,
        axis_index_groups=sides,
    )
    new_memory = write_back(dst, node_memory, new_rows)

    args = (freq, phase, query_weight, kv_weight)
    other = project(shift, query_other, info_other, *args)
    own = project(shift, query_mem, info_mine, *args)
    part_b, lse_b = attend(1, got, *other, kv_weight, bf16, "attend_other")
    back, back_lse = lax.ppermute(part_b, "grp", opposite), lax.ppermute(lse_b, "grp", opposite)
    part_a, lse_a = attend(0, got, *own, kv_weight, f32, "attend_mine")
    embeddings = merge(part_a, lse_a, back, back_lse, query_mem, out_weight)
    return new_memory, embeddings


def solution(mesh):
    split_rows = P(AXES, None)
    split_flat = P(AXES)
    in_specs = (
        split_rows,
        split_flat,
        split_flat,
        split_flat,
        split_flat,
        split_rows,
        P(),
        P(),
        P(),
        P(),
        P(),
        split_flat,
        split_flat,
        split_rows,
        split_rows,
        split_flat,
        P(),
        P(),
        P(),
    )
    body = functools.partial(local, mesh.shape["grp"], mesh.shape["mem"])
    return jax.shard_map(
        body, mesh=mesh, in_specs=in_specs, out_specs=(split_rows, split_rows), check_vma=False
    )
```

```python
import functools
import math

import jax
import jax.numpy as jnp
from jax import lax
from jax.experimental import pallas as pl
from jax.experimental.pallas import tpu as pltpu
from jax.sharding import PartitionSpec as P


HEADS = 2
AXES = ("grp", "mem")
LANES = 128
UNROLL = 32
ROWS = 512
SENDS = 8
CHUNKS = 8
NEG = -1e30
TIME_BITS = 12
f32 = jnp.float32
bf16 = jnp.bfloat16
i32 = jnp.int32
VM = pl.BlockSpec(memory_space=pltpu.VMEM)
SM = pl.BlockSpec(memory_space=pltpu.SMEM)
HB = pl.BlockSpec(memory_space=pltpu.HBM)


def dot(a, b):
    return jnp.dot(a, b, preferred_element_type=f32)


def dot_nt(a, b):
    return lax.dot_general(a, b, (((1,), (1,)), ((), ())), preferred_element_type=f32)


def split(x):
    high = x.astype(bf16)
    return high, (x - high.astype(f32)).astype(bf16)


def cosine(x):
    turns = jnp.round(x * (1.0 / math.pi))
    r = x - turns * 3.140625
    r = r - turns * 9.675025939941406e-4
    r = r - turns * 1.5099579909783764e-7
    s = r * r
    p = -2.755731922398589e-7 + s * 2.08767569878681e-9
    p = 2.48015873015873e-5 + s * p
    p = -1.3888888888888889e-3 + s * p
    p = 4.1666666666666664e-2 + s * p
    p = -0.5 + s * p
    p = 1.0 + s * p
    half = turns * 0.5
    odd = half - jnp.floor(half)
    return p * (1.0 - 4.0 * odd)


def run(kernel, args, in_specs, out_shape, out_specs, **rest):
    args = [
        pltpu.with_memory_space_constraint(a, pltpu.HBM) if spec is HB else a
        for a, spec in zip(args, in_specs)
    ]
    outs = [
        pltpu.HBM(o.shape, o.dtype) if spec is HB else o for o, spec in zip(out_shape, out_specs)
    ]
    return pl.pallas_call(
        kernel, out_shape=outs, in_specs=in_specs, out_specs=list(out_specs), **rest
    )(*args)


def params(mib):
    return pltpu.CompilerParams(vmem_limit_bytes=mib << 20)


def cost(flops, nbytes):
    return pl.CostEstimate(flops=int(flops), bytes_accessed=int(nbytes), transcendentals=0)


def move_rows(count, load, store):
    def body(t, carry):
        base = pl.multiple_of(t * UNROLL, UNROLL)
        for part in range(0, UNROLL, 16):
            rows = [load(base + part + u) for u in range(16)]
            for u in range(16):
                store(base + part + u, rows[u])
        return carry

    lax.fori_loop(0, count // UNROLL, body, 0)


def pack_rows(count, src, src_base, dst, dst_base):
    def body(t, carry):
        r = pl.multiple_of(t * 16, 16)
        for half in range(2):
            dst[pl.ds(dst_base + r, 16), half * LANES : (half + 1) * LANES] = src[
                pl.ds(2 * (src_base + r) + half, 16, stride=2), :
            ].astype(bf16)
        return carry

    lax.fori_loop(0, count // 16, body, 0, unroll=4)


def gather_rows(index, first, count, scale, table, stage, dst, dst_base):
    def pack(at):
        for r in range(0, UNROLL, 16):
            for half in range(2):
                dst[pl.ds(dst_base + at + r, 16), half * LANES : (half + 1) * LANES] = stage[
                    pl.ds(2 * (at + r) + half, 16, stride=2), :
                ].astype(bf16)

    def body(t, carry):
        base = pl.multiple_of(t * UNROLL, UNROLL)
        last = pl.multiple_of(jnp.maximum(t - 1, 0) * UNROLL, UNROLL)
        for part in range(0, UNROLL, 16):
            rows = [
                table[pl.ds(scale * index[first + base + part + u], 2), :] for u in range(16)
            ]
            for u in range(16):
                stage[pl.ds(2 * (base + part + u), 2), :] = rows[u]
        pack(last)
        return carry

    lax.fori_loop(0, count // UNROLL, body, 0)
    pack(count - UNROLL)


def start_table(memory, raw, sem):
    step = memory.shape[0] // CHUNKS
    loads = [
        pltpu.make_async_copy(
            memory.at[pl.ds(c * step, step)], raw.at[pl.ds(c * step, step)], sem.at[c]
        )
        for c in range(CHUNKS)
    ]
    for copy in loads:
        copy.start()
    return loads


def widen_table(loads, raw, table):
    step = raw.shape[0] // len(loads)
    for c in range(len(loads)):
        loads[c].wait()

        def widen(t, carry):
            r = pl.multiple_of(c * step + t * 64, 64)
            rows = raw[pl.ds(r, 64), :].astype(f32)
            for half in range(2):
                table[pl.ds(2 * r + half, 64, stride=2), :] = rows[
                    :, half * LANES : (half + 1) * LANES
                ]
            return carry

        lax.fori_loop(0, step // 64, widen, 0, unroll=2)


def per_peer_rows(src, share, dst):
    group = math.lcm(share, LANES)
    members, depth = group // share, group // LANES
    count = src.shape[0] // depth
    for member in range(members):
        pieces = []
        for at in range(share * member, share * (member + 1)):
            row, lane = divmod(at, LANES)
            if not pieces or lane == 0:
                pieces.append([row, lane, 0])
            pieces[-1][2] += 1
        parts = [
            src[pl.ds(row, count, stride=depth), :][:, lane : lane + size]
            for row, lane, size in pieces
        ]
        room = dst.shape[0] * LANES - share
        if room:
            parts.append(jnp.zeros((count, room), i32))
        line = jnp.concatenate(parts, axis=1)
        for block in range(dst.shape[0]):
            dst[block, pl.ds(member, count, stride=members), :] = line[
                :, block * LANES : (block + 1) * LANES
            ]


def ids_kernel(cap, nodes, target, when, request, counts, out, events, requests, both):
    peers = counts.shape[1]
    both[...] = (target[...] << TIME_BITS) + when[...]
    per_peer_rows(both, cap, events)
    per_peer_rows(request, request.shape[0] * LANES // peers, requests)
    row = lax.broadcasted_iota(i32, (peers, peers), 0)
    lane = lax.broadcasted_iota(i32, (peers, peers), 1)
    live = jnp.sum(
        jnp.where(row == lane, jnp.broadcast_to(counts[...], (peers, peers)), 0).astype(f32),
        axis=1,
        keepdims=True,
    )
    slot = lax.broadcasted_iota(i32, (peers, LANES), 1).astype(f32)
    sent = jnp.where(slot < live, events[0], nodes << TIME_BITS)
    out[:, 0, :LANES] = sent
    for block in range(requests.shape[0]):
        out[:, 0, (block + 1) * LANES : (block + 2) * LANES] = requests[block]


def pack_ids(cap, nodes, evt_dst, evt_time, req_rows, evt_counts):
    peers = evt_counts.shape[1]
    per_peer = req_rows.shape[0] // peers
    blocks = pl.cdiv(per_peer, LANES)
    return pl.pallas_call(
        functools.partial(ids_kernel, cap, nodes),
        out_shape=jax.ShapeDtypeStruct((peers, 1, (1 + blocks) * LANES), i32),
        in_specs=[VM] * 4,
        out_specs=VM,
        scratch_shapes=[
            pltpu.VMEM((1, peers, LANES), i32),
            pltpu.VMEM((blocks, peers, LANES), i32),
            pltpu.VMEM((evt_dst.shape[0] // LANES, LANES), i32),
        ],
        compiler_params=params(4),
        cost_estimate=cost(0, 1e5),
        name="pack_ids",
    )(
        evt_dst.reshape(-1, LANES),
        evt_time.reshape(-1, LANES),
        req_rows.reshape(-1, LANES),
        evt_counts,
    )


def source_kernel(idx_hbm, memory, rows_out, idx, raw, table, stage, in_sem, idx_sem):
    loads = start_table(memory, raw, in_sem)
    idx_load = pltpu.make_async_copy(idx_hbm, idx, idx_sem)
    idx_load.start()
    widen_table(loads, raw, table)
    idx_load.wait()
    gather_rows(idx, 0, idx.shape[0], 2, table, stage, rows_out, 0)


def gather_sources(evt_src, node_memory):
    nodes, width = node_memory.shape
    events = evt_src.shape[0]
    return run(
        source_kernel,
        [evt_src, node_memory],
        out_shape=(jax.ShapeDtypeStruct((events, width), bf16),),
        in_specs=[HB, HB],
        out_specs=(VM,),
        scratch_shapes=[
            pltpu.SMEM(evt_src.shape, i32),
            pltpu.VMEM((nodes, width), bf16),
            pltpu.VMEM((2 * nodes, LANES), f32),
            pltpu.VMEM((2 * events, LANES), f32),
            pltpu.SemaphoreType.DMA((CHUNKS,)),
            pltpu.SemaphoreType.DMA,
        ],
        compiler_params=params(24),
        cost_estimate=cost(0, 20e6),
        name="source_rows",
    )[0]


def prepare_kernel(
    dst_s,
    seen,
    memory,
    dst_row,
    dst_col,
    time_row,
    freq,
    phase,
    msg_hbm,
    mem_hbm,
    bias,
    pre_hbm,
    inv_hbm,
    rows_hbm,
    raw,
    table,
    stage,
    codes,
    msg_weight,
    mem_weight,
    pre_out,
    inv_out,
    rows_out,
    sem,
    out_sem,
    table_sem,
):
    events = dst_s.shape[0]
    width = rows_out.shape[1]
    code_width = freq.shape[0]
    pairs = ((msg_hbm, msg_weight), (mem_hbm, mem_weight))
    loads = [pltpu.make_async_copy(a, b, sem.at[k]) for k, (a, b) in enumerate(pairs)]
    table_loads = start_table(memory, raw, table_sem)
    for copy in loads:
        copy.start()
    target = dst_row[...]
    groups = seen.shape[0]
    at_group = lax.broadcasted_iota(i32, (groups, events), 0) == (target >> 7)
    at_group = jnp.where(at_group, 1.0, 0.0).astype(bf16)
    by_lane = jnp.transpose(seen[...].astype(f32)).astype(i32)
    high = dot((by_lane >> 8).astype(f32).astype(bf16), at_group)
    low = dot((by_lane & 255).astype(f32).astype(bf16), at_group)
    at_lane = lax.broadcasted_iota(i32, (LANES, events), 0) == (target & 127)
    last = jnp.sum(jnp.where(at_lane, 256.0 * high + low, 0.0), axis=0, keepdims=True)
    delta = time_row[...].astype(f32) - last
    for t in range(events // LANES):
        at = pl.ds(t * LANES, LANES)
        part = delta[:, t * LANES : (t + 1) * LANES]
        codes[at, :code_width] = jnp.transpose(cosine(freq[...] * part + phase[...])).astype(bf16)
    codes[:, code_width:] = jnp.ones((events, LANES), bf16)
    widen_table(table_loads, raw, table)
    gather_rows(dst_s, 0, events, 2, table, stage, rows_out, 0)
    for copy in loads:
        copy.wait()
    step = min(ROWS, events)

    def block(t, carry):
        r = pl.multiple_of(t * step, step)
        same = jnp.where(dst_col[pl.ds(r, step), :] == dst_row[...], 1.0, 0.0).astype(bf16)
        sums = dot(same, codes[...])
        inv = 1.0 / jnp.maximum(sums[:, code_width:], 1.0)
        code_agg = (sums[:, :code_width] * inv).astype(bf16)
        inv_out[pl.ds(r, step), :] = inv
        memory = rows_out[pl.ds(r, step), :]
        part = dot(code_agg, msg_weight[pl.ds(width, code_width), :]) + bias[...]
        joined = dot(memory, mem_weight[...])
        third = 3 * width
        pre_out[pl.ds(r, step), : 2 * width] = (
            part[:, : 2 * width] + joined[:, : 2 * width] + joined[:, third : third + 2 * width]
        ).astype(bf16)
        pre_out[pl.ds(r, step), 2 * width : third] = (
            part[:, 2 * width :] + joined[:, 2 * width : third]
        ).astype(bf16)
        pre_out[pl.ds(r, step), third:] = joined[:, third + 2 * width :].astype(bf16)
        return carry

    outs = [(rows_out, rows_hbm), (inv_out, inv_hbm), (pre_out, pre_hbm)]

    def save(k, t):
        r = pl.multiple_of(t * step, step)
        a, b = outs[k]
        return pltpu.make_async_copy(a.at[pl.ds(r, step)], b.at[pl.ds(r, step)], out_sem.at[k, t])

    def run(t, carry):
        block(t, carry)
        for k in range(3):
            save(k, t).start()
        return carry

    lax.fori_loop(0, events // step, run, 0)

    def drain(t, carry):
        for k in range(3):
            save(k, t).wait()
        return carry

    lax.fori_loop(0, events // step, drain, 0)


def prepare(dst, last_update, node_memory, dst_row, dst_col, time_row, freq, phase, msg_weight, mem_weight, bias):
    events = dst.shape[0]
    width = mem_weight.shape[0]
    return run(
        prepare_kernel,
        [dst, last_update, node_memory, dst_row, dst_col, time_row, freq, phase, msg_weight, mem_weight, bias],
        out_shape=(
            jax.ShapeDtypeStruct((events, 4 * width), bf16),
            jax.ShapeDtypeStruct((events, LANES), f32),
            jax.ShapeDtypeStruct((events, width), bf16),
        ),
        in_specs=[SM, VM, HB] + [VM] * 5 + [HB, HB, VM],
        out_specs=(HB, HB, HB),
        scratch_shapes=[
            pltpu.VMEM(node_memory.shape, bf16),
            pltpu.VMEM((2 * node_memory.shape[0], LANES), f32),
            pltpu.VMEM((2 * events, LANES), f32),
            pltpu.VMEM((events, freq.shape[0] + LANES), bf16),
            pltpu.VMEM(msg_weight.shape, bf16),
            pltpu.VMEM(mem_weight.shape, bf16),
            pltpu.VMEM((events, 4 * width), bf16),
            pltpu.VMEM((events, LANES), f32),
            pltpu.VMEM((events, width), bf16),
            pltpu.SemaphoreType.DMA((2,)),
            pltpu.SemaphoreType.DMA((3, events // min(ROWS, events))),
            pltpu.SemaphoreType.DMA((CHUNKS,)),
        ],
        compiler_params=params(48),
        cost_estimate=cost(6e9, 30e6),
        name="prepare",
    )


def update_kernel(
    dst_s,
    req_s,
    qry_s,
    memory,
    got,
    dst_row,
    dst_col,
    pre_hbm,
    inv_hbm,
    rows_hbm,
    msg_hbm,
    found_hbm,
    query_out,
    new_hbm,
    raw,
    table,
    updated,
    new_rows,
    stage,
    packed,
    pre,
    inv,
    rows,
    msg_weight,
    sem,
    block_sem,
    out_sem,
    table_sem,
    new_sem,
):
    events, width = rows.shape
    step = min(ROWS, events)
    blocks = [(rows_hbm, rows), (inv_hbm, inv), (pre_hbm, pre)]

    def fetch(k, t):
        r = pl.multiple_of(t * step, step)
        a, b = blocks[k]
        return pltpu.make_async_copy(a.at[pl.ds(r, step)], b.at[pl.ds(r, step)], block_sem.at[k, t])

    weight_load = pltpu.make_async_copy(msg_hbm.at[pl.ds(0, width)], msg_weight, sem.at[0])
    count = events // step
    share = raw.shape[0] // count

    def put_new(t):
        at = pl.ds(pl.multiple_of(t * step, step), step)
        return pltpu.make_async_copy(new_rows.at[at], new_hbm.at[at], new_sem.at[t])

    def table_load(t):
        r = pl.multiple_of(t * share, share)
        return pltpu.make_async_copy(
            memory.at[pl.ds(r, share)], raw.at[pl.ds(r, share)], table_sem.at[t]
        )

    for k in range(3):
        fetch(k, 0).start()
    weight_load.start()
    if count > 1:
        for k in range(3):
            fetch(k, 1).start()

    def block(t, carry):
        r = pl.multiple_of(t * step, step)
        same = jnp.where(dst_col[pl.ds(r, step), :] == dst_row[...], 1.0, 0.0).astype(bf16)
        sums = dot(same, got[...])
        for k in range(3):
            fetch(k, t).wait()

        @pl.when(t + 2 < count)
        def _():
            for k in range(3):
                fetch(k, t + 2).start()

        @pl.when(t < count // 2)
        def _():
            table_load(2 * t).start()
            table_load(2 * t + 1).start()

        scale = inv[pl.ds(r, step), :]
        agg = jnp.concatenate(
            [sums[:, h * LANES : (h + 1) * LANES] * scale for h in range(width // LANES)], axis=1
        ).astype(bf16)
        msg = dot(agg, msg_weight[...])
        ready = pre[pl.ds(r, step), :].astype(f32)
        reset = jax.nn.sigmoid(msg[:, :width] + ready[:, :width])
        gate = jax.nn.sigmoid(msg[:, width : 2 * width] + ready[:, width : 2 * width])
        cand = jnp.tanh(
            msg[:, 2 * width :] + ready[:, 2 * width : 3 * width] + reset * ready[:, 3 * width :]
        )
        new = (1.0 - gate) * cand + gate * rows[pl.ds(r, step), :].astype(f32)
        new = new.astype(bf16)
        new_rows[pl.ds(r, step), :] = new
        put_new(t).start()
        new = new.astype(f32)
        for half in range(2):
            updated[pl.ds(2 * r + half, step, stride=2), :] = new[:, half * LANES : (half + 1) * LANES]
        return carry

    weight_load.wait()
    lax.fori_loop(0, count, block, 0)
    widen_table([table_load(t) for t in range(count)], raw, table)

    def put_table(k, row):
        table[pl.ds(2 * dst_s[k], 2), :] = row

    move_rows(events, lambda k: updated[pl.ds(2 * k, 2), :], put_table)
    queries = qry_s.shape[0]
    gather_rows(qry_s, 0, queries, 2, table, stage, query_out, 0)
    total = req_s.shape[0]
    chunk = total // SENDS
    sends = []
    for c in range(SENDS):
        gather_rows(req_s, c * chunk, chunk, 1, table, stage, packed, c * chunk)
        send = pltpu.make_async_copy(
            packed.at[pl.ds(c * chunk, chunk)],
            found_hbm.at[pl.ds(c * chunk, chunk)],
            out_sem.at[c],
        )
        send.start()
        sends.append(send)
    for send in sends:
        send.wait()
    for t in range(count):
        put_new(t).wait()


def update(dst, req2, qry_rows, node_memory, got, dst_row, dst_col, pre, inv, rows, msg_weight):
    events, width = got.shape
    queries = qry_rows.shape[0]
    total = req2.shape[0]
    return run(
        update_kernel,
        [dst, req2, qry_rows, node_memory, got, dst_row, dst_col, pre, inv, rows, msg_weight],
        out_shape=(
            jax.ShapeDtypeStruct((total, width), bf16),
            jax.ShapeDtypeStruct((queries, width), bf16),
            jax.ShapeDtypeStruct((events, width), bf16),
        ),
        in_specs=[SM, SM, SM, HB, VM, VM, VM, HB, HB, HB, HB],
        out_specs=(HB, VM, HB),
        scratch_shapes=[
            pltpu.VMEM(node_memory.shape, bf16),
            pltpu.VMEM((2 * node_memory.shape[0] + 16, LANES), f32),
            pltpu.VMEM((2 * events, LANES), f32),
            pltpu.VMEM((events, width), bf16),
            pltpu.VMEM((2 * max(total // SENDS, queries), LANES), f32),
            pltpu.VMEM((total, width), bf16),
            pltpu.VMEM(pre.shape, bf16),
            pltpu.VMEM(inv.shape, f32),
            pltpu.VMEM(rows.shape, bf16),
            pltpu.VMEM((width, msg_weight.shape[1]), bf16),
            pltpu.SemaphoreType.DMA((1,)),
            pltpu.SemaphoreType.DMA((3, events // min(ROWS, events))),
            pltpu.SemaphoreType.DMA((SENDS,)),
            pltpu.SemaphoreType.DMA((events // min(ROWS, events),)),
            pltpu.SemaphoreType.DMA((events // min(ROWS, events),)),
        ],
        compiler_params=params(44),
        cost_estimate=cost(4e9, 40e6),
        name="update",
    )


def write_back_kernel(dst_s, memory, new_hbm, memory_out, raw, new, table, updated, sem, new_sem):
    loads = start_table(memory, raw, sem)
    new_load = pltpu.make_async_copy(new_hbm, new, new_sem)
    new_load.start()
    widen_table(loads, raw, table)
    new_load.wait()
    events = new.shape[0]

    def spread(t, carry):
        r = pl.multiple_of(t * 64, 64)
        rows = new[pl.ds(r, 64), :].astype(f32)
        for half in range(2):
            updated[pl.ds(2 * r + half, 64, stride=2), :] = rows[:, half * LANES : (half + 1) * LANES]
        return carry

    lax.fori_loop(0, events // 64, spread, 0)

    def put(k, row):
        table[pl.ds(2 * dst_s[k], 2), :] = row

    move_rows(events, lambda k: updated[pl.ds(2 * k, 2), :], put)
    share = raw.shape[0] // CHUNKS
    saves = []
    for c in range(CHUNKS):
        pack_rows(share, table, c * share, raw, c * share)
        save = pltpu.make_async_copy(
            raw.at[pl.ds(c * share, share)], memory_out.at[pl.ds(c * share, share)], sem.at[c]
        )
        save.start()
        saves.append(save)
    for save in saves:
        save.wait()


def write_back(dst, node_memory, new):
    nodes, _ = node_memory.shape
    events = new.shape[0]
    return run(
        write_back_kernel,
        [dst, node_memory, new],
        out_shape=(jax.ShapeDtypeStruct(node_memory.shape, bf16),),
        in_specs=[SM, HB, HB],
        out_specs=(HB,),
        scratch_shapes=[
            pltpu.VMEM(node_memory.shape, bf16),
            pltpu.VMEM(new.shape, bf16),
            pltpu.VMEM((2 * nodes + 16, LANES), f32),
            pltpu.VMEM((2 * events, LANES), f32),
            pltpu.SemaphoreType.DMA((CHUNKS,)),
            pltpu.SemaphoreType.DMA,
        ],
        compiler_params=params(32),
        cost_estimate=cost(0, 20e6),
        name="write_back",
    )[0]


def invert_kernel(slots, values, out):
    total = slots.shape[1]
    high = total // LANES
    where = slots[...]
    rows = lax.broadcasted_iota(i32, (high, total), 0)
    at_row = rows == (where >> 7)
    lanes = lax.broadcasted_iota(i32, (LANES, total), 0)
    at_lane = jnp.where(lanes == (where & 127), 1.0, 0.0).astype(bf16)
    result = jnp.zeros((high, LANES), i32)
    for digit in range(3):
        part = ((values[...] >> (8 * digit)) & 255).astype(f32)
        spread = jnp.where(at_row, part, 0.0).astype(bf16)
        result = result + (dot_nt(spread, at_lane).astype(i32) << (8 * digit))
    out[...] = result


def invert(slots, values):
    total = slots.shape[1]
    return run(
        invert_kernel,
        [slots, values],
        out_shape=(jax.ShapeDtypeStruct((total // LANES, LANES), i32),),
        in_specs=[VM, VM],
        out_specs=(VM,),
        compiler_params=params(24),
        cost_estimate=cost(1e9, 5e6),
        name="invert",
    )[0]


def project_kernel(
    shift,
    query,
    info,
    freq,
    phase,
    query_weight,
    kv_weight,
    qx_hbm,
    et_hbm,
    se_hbm,
    qx,
    et,
    se,
    sem,
):
    width = query_weight.shape[0]
    head_dim = width // HEADS
    queries = query.shape[0]
    step = 256
    slots = info.shape[1]
    who = info[...] & ((1 << shift) - 1)
    delta = ((info[...] >> shift) - (1 << TIME_BITS)).astype(f32)
    for t in range(slots // step):
        part = delta[:, t * step : (t + 1) * step]
        et[:, pl.ds(t * step, step)] = cosine(freq[...] * part + phase[...]).astype(bf16)
    mask = lax.broadcasted_iota(i32, (queries, slots), 0) == who
    vec = dot(query[...], query_weight[...]) * (1.0 / math.sqrt(head_dim))
    for h in range(HEADS):
        high, low = split(vec[:, h * head_dim : (h + 1) * head_dim])
        keys = kv_weight[:, h * head_dim : (h + 1) * head_dim]
        folded = dot_nt(high, keys) + dot_nt(low, keys)
        high, low = split(folded)
        rows = pl.ds(2 * h * queries, queries)
        qx[rows, :] = high[:, :width]
        qx[pl.ds((2 * h + 1) * queries, queries), :] = low[:, :width]
        scores = dot(high[:, width:], et[...]) + dot(low[:, width:], et[...])
        se[pl.ds(h * queries, queries), :] = jnp.where(mask, scores, NEG)
    pairs = ((qx, qx_hbm), (et, et_hbm), (se, se_hbm))
    copies = [pltpu.make_async_copy(a, b, sem.at[k]) for k, (a, b) in enumerate(pairs)]
    for copy in copies:
        copy.start()
    for copy in copies:
        copy.wait()


def project(shift, query, info, freq, phase, query_weight, kv_weight):
    queries, width = query.shape
    slots = info.shape[1]
    outs = (
        jax.ShapeDtypeStruct((2 * HEADS * queries, width), bf16),
        jax.ShapeDtypeStruct((freq.shape[0], slots), bf16),
        jax.ShapeDtypeStruct((HEADS * queries, slots), f32),
    )
    return run(
        functools.partial(project_kernel, shift),
        [query, info, freq, phase, query_weight, kv_weight],
        out_shape=outs,
        in_specs=[VM] * 6,
        out_specs=(HB, HB, HB),
        scratch_shapes=[pltpu.VMEM(o.shape, o.dtype) for o in outs] + [pltpu.SemaphoreType.DMA((3,))],
        compiler_params=params(32),
        cost_estimate=cost(1e9, 10e6),
        name="project",
    )


def attend_kernel(
    sub,
    got,
    qx_hbm,
    et_hbm,
    se_hbm,
    kv_hbm,
    part_out,
    lse_out,
    qx,
    et,
    se,
    kv_weight,
    sem,
    se_sem,
):
    owners, both, width = got.shape
    per_peer = both // 2
    slots = owners * per_peer
    queries = qx.shape[0] // (2 * HEADS)
    head_dim = width // HEADS
    pairs = ((qx_hbm, qx), (et_hbm, et), (kv_hbm, kv_weight))
    copies = [pltpu.make_async_copy(a, b, sem.at[k]) for k, (a, b) in enumerate(pairs)]

    def load_se(h):
        at = pl.ds(h * queries, queries)
        return pltpu.make_async_copy(se_hbm.at[at], se.at[at], se_sem.at[h])

    for copy in copies:
        copy.start()
    for h in range(HEADS):
        load_se(h).start()
    rows = got[:, sub * per_peer : (sub + 1) * per_peer, :].reshape(slots, width)
    logs = []
    for h in range(HEADS):
        if h == 0:
            copies[0].wait()
        both_parts = dot_nt(qx[pl.ds(2 * h * queries, 2 * queries), :], rows)
        load_se(h).wait()
        scores = both_parts[:queries] + both_parts[queries:] + se[pl.ds(h * queries, queries), :]
        top = jnp.maximum(jnp.max(scores, axis=1, keepdims=True), 0.1 * NEG)
        weights = jnp.exp(scores - top).astype(bf16)
        total = jnp.sum(weights.astype(f32), axis=1, keepdims=True)
        some = total > 0.0
        inv = jnp.where(some, 1.0 / jnp.where(some, total, 1.0), 0.0)
        logs.append(jnp.where(some, top + jnp.log(jnp.where(some, total, 1.0)), NEG))
        if h == 0:
            copies[1].wait()
            copies[2].wait()
        mem_high, mem_low = split(dot(weights, rows) * inv)
        code_high, code_low = split(dot_nt(weights, et[...]) * inv)
        lanes = slice(width + h * head_dim, width + (h + 1) * head_dim)
        value_mem = kv_weight[:width, lanes]
        value_code = kv_weight[width:, lanes]
        part = dot(mem_high, value_mem) + dot(mem_low, value_mem)
        part = part + dot(code_high, value_code) + dot(code_low, value_code)
        part_out[:, h * head_dim : (h + 1) * head_dim] = part.astype(part_out.dtype)
    lane = lax.broadcasted_iota(i32, (queries, LANES), 1)
    spread = jnp.where((lane & 7) < 4, logs[0], logs[1])
    lse_out[...] = jnp.transpose(spread)[:8, :]


def attend(sub, got, qx, et, se, kv_weight, kind, name):
    queries = qx.shape[0] // (2 * HEADS)
    width = got.shape[2]
    return run(
        functools.partial(attend_kernel, sub),
        [got, qx, et, se, kv_weight],
        out_shape=(
            jax.ShapeDtypeStruct((queries, width), kind),
            jax.ShapeDtypeStruct((8, queries), f32),
        ),
        in_specs=[VM, HB, HB, HB, HB],
        out_specs=(VM, VM),
        scratch_shapes=[pltpu.VMEM(a.shape, a.dtype) for a in (qx, et, se, kv_weight)]
        + [pltpu.SemaphoreType.DMA((3,)), pltpu.SemaphoreType.DMA((HEADS,))],
        compiler_params=params(40),
        cost_estimate=cost(4e9, 10e6),
        name=name,
    )


def merge_kernel(mine, mine_lse, other, other_lse, query, out_weight, out):
    queries, width = mine.shape
    head_dim = width // HEADS
    pieces = []
    for h in range(HEADS):
        lanes = slice(h * head_dim, (h + 1) * head_dim)
        lse_a = jnp.transpose(jnp.broadcast_to(mine_lse[pl.ds(4 * h, 1), :], (LANES, queries)))
        lse_b = jnp.transpose(jnp.broadcast_to(other_lse[pl.ds(4 * h, 1), :], (LANES, queries)))
        top = jnp.maximum(lse_a, lse_b)
        weight_a = jnp.exp(lse_a - top)
        weight_b = jnp.exp(lse_b - top)
        inv = 1.0 / (weight_a + weight_b)
        pieces.append(
            mine[:, lanes] * (weight_a * inv) + other[:, lanes].astype(f32) * (weight_b * inv)
        )
    attended = jnp.concatenate(pieces, axis=1).astype(bf16)
    result = dot(attended, out_weight[:width, :]) + dot(query[...], out_weight[width:, :])
    out[...] = result.astype(bf16)


def merge(mine, mine_lse, other, other_lse, query, out_weight):
    return pl.pallas_call(
        merge_kernel,
        out_shape=jax.ShapeDtypeStruct(query.shape, bf16),
        in_specs=[VM] * 6,
        out_specs=VM,
        compiler_params=params(8),
        cost_estimate=cost(1e8, 1e6),
        name="merge",
    )(mine, mine_lse, other, other_lse, query, out_weight)


def local(
    group_count,
    mem_count,
    node_memory,
    last_update,
    evt_src,
    evt_dst,
    evt_time,
    evt_counts,
    time_freq,
    time_phase,
    msg_weight,
    mem_weight,
    gru_bias,
    qry_rows,
    qry_time,
    nbr_time,
    nbr_slot,
    req_rows,
    query_weight,
    kv_weight,
    out_weight,
):
    peers = group_count * mem_count
    side_peers = peers // 2
    half_groups = group_count // 2
    nodes, width = node_memory.shape
    events = evt_src.shape[0]
    cap = events // peers
    queries, fan_out = nbr_time.shape
    total_slots = queries * fan_out
    per_peer = total_slots // peers
    side_slots = side_peers * per_peer
    shift = (queries - 1).bit_length()
    side = lax.axis_index("grp") // half_groups
    sides = [list(range(s * side_peers, (s + 1) * side_peers)) for s in range(2)]
    opposite = [(g, (g + half_groups) % group_count) for g in range(group_count)]

    def mine_other(pair):
        return jnp.where(side == 0, pair[0], pair[1]), jnp.where(side == 0, pair[1], pair[0])

    ids = pack_ids(cap, nodes, evt_dst, evt_time, req_rows, evt_counts)
    got_ids = lax.all_to_all(ids, AXES, split_axis=0, concat_axis=0, tiled=True)[:, 0]
    sent_rows = gather_sources(evt_src, node_memory)
    got_rows = lax.all_to_all(
        sent_rows.reshape(peers, cap, width), AXES, split_axis=0, concat_axis=0, tiled=True
    )
    got_rows = got_rows.reshape(events, width)
    qry_time, time_freq, time_phase, gru_bias, got_ids = lax.optimization_barrier(
        (qry_time, time_freq, time_phase, gru_bias, got_ids)
    )

    packed = got_ids[:, :cap].reshape(events)
    dst = packed >> TIME_BITS
    time_row = (packed & ((1 << TIME_BITS) - 1)).reshape(1, events)
    dst_row = jnp.where(dst < nodes, dst, -1).reshape(1, events)
    dst_col = dst.reshape(events, 1)
    mine, other = mine_other(got_ids[:, LANES : LANES + per_peer].reshape(2, side_peers, per_peer))
    req2 = 2 * jnp.concatenate([mine, other], axis=1).reshape(total_slots)
    freq = time_freq.reshape(-1, 1)
    phase = time_phase.reshape(-1, 1)
    bias = gru_bias.reshape(1, -1)
    delta = qry_time[:, None] - nbr_time + (1 << TIME_BITS)
    values = (delta << shift) + jnp.arange(queries, dtype=i32)[:, None]
    info = invert(nbr_slot, values.reshape(1, total_slots))
    info_mine, info_send = mine_other(info.reshape(2, 1, side_slots))
    req2, info_send = lax.optimization_barrier((req2, info_send))
    info_other = lax.ppermute(info_send, "grp", opposite)
    pre, inv, rows = prepare(
        jnp.minimum(dst, nodes - 1),
        last_update.reshape(-1, LANES),
        node_memory,
        dst_row,
        dst_col,
        time_row,
        freq,
        phase,
        msg_weight,
        mem_weight,
        bias,
    )
    found, query_mem, new_rows = update(
        dst, req2, qry_rows, node_memory, got_rows, dst_row, dst_col, pre, inv, rows, msg_weight
    )
    query_other = lax.ppermute(query_mem, "grp", opposite)
    got = lax.all_to_all(
        found.reshape(side_peers, 2 * per_peer, width),
        AXES,
        split_axis=0,
        concat_axis=0,
        tiled=True,
        axis_index_groups=sides,
    )
    new_memory = write_back(dst, node_memory, new_rows)

    args = (freq, phase, query_weight, kv_weight)
    other = project(shift, query_other, info_other, *args)
    own = project(shift, query_mem, info_mine, *args)
    part_b, lse_b = attend(1, got, *other, kv_weight, bf16, "attend_other")
    back, back_lse = lax.ppermute(part_b, "grp", opposite), lax.ppermute(lse_b, "grp", opposite)
    part_a, lse_a = attend(0, got, *own, kv_weight, f32, "attend_mine")
    embeddings = merge(part_a, lse_a, back, back_lse, query_mem, out_weight)
    return new_memory, embeddings


def solution(mesh):
    split_rows = P(AXES, None)
    split_flat = P(AXES)
    in_specs = (
        split_rows,
        split_flat,
        split_flat,
        split_flat,
        split_flat,
        split_rows,
        P(),
        P(),
        P(),
        P(),
        P(),
        split_flat,
        split_flat,
        split_rows,
        split_rows,
        split_flat,
        P(),
        P(),
        P(),
    )
    body = functools.partial(local, mesh.shape["grp"], mesh.shape["mem"])
    return jax.shard_map(
        body, mesh=mesh, in_specs=in_specs, out_specs=(split_rows, split_rows), check_vma=False
    )
```

```python
import functools
import math

import jax
import jax.numpy as jnp
from jax import lax
from jax.experimental import pallas as pl
from jax.experimental.pallas import tpu as pltpu
from jax.sharding import PartitionSpec as P


HEADS = 2
AXES = ("grp", "mem")
LANES = 128
UNROLL = 128
ROWS = 512
SENDS = 8
CHUNKS = 8
NEG = -1e30
TIME_BITS = 12
f32 = jnp.float32
bf16 = jnp.bfloat16
i32 = jnp.int32
VM = pl.BlockSpec(memory_space=pltpu.VMEM)
SM = pl.BlockSpec(memory_space=pltpu.SMEM)
HB = pl.BlockSpec(memory_space=pltpu.HBM)


def dot(a, b):
    return jnp.dot(a, b, preferred_element_type=f32)


def dot_nt(a, b):
    return lax.dot_general(a, b, (((1,), (1,)), ((), ())), preferred_element_type=f32)


def split(x):
    high = x.astype(bf16)
    return high, (x - high.astype(f32)).astype(bf16)


def cosine(x):
    turns = jnp.round(x * (1.0 / math.pi))
    r = x - turns * 3.140625
    r = r - turns * 9.675025939941406e-4
    r = r - turns * 1.5099579909783764e-7
    s = r * r
    p = -2.755731922398589e-7 + s * 2.08767569878681e-9
    p = 2.48015873015873e-5 + s * p
    p = -1.3888888888888889e-3 + s * p
    p = 4.1666666666666664e-2 + s * p
    p = -0.5 + s * p
    p = 1.0 + s * p
    half = turns * 0.5
    odd = half - jnp.floor(half)
    return p * (1.0 - 4.0 * odd)


def run(kernel, args, in_specs, out_shape, out_specs, **rest):
    args = [
        pltpu.with_memory_space_constraint(a, pltpu.HBM) if spec is HB else a
        for a, spec in zip(args, in_specs)
    ]
    outs = [
        pltpu.HBM(o.shape, o.dtype) if spec is HB else o for o, spec in zip(out_shape, out_specs)
    ]
    return pl.pallas_call(
        kernel, out_shape=outs, in_specs=in_specs, out_specs=list(out_specs), **rest
    )(*args)


def params(mib):
    return pltpu.CompilerParams(vmem_limit_bytes=mib << 20)


def cost(flops, nbytes):
    return pl.CostEstimate(flops=int(flops), bytes_accessed=int(nbytes), transcendentals=0)


def move_rows(count, load, store):
    def body(t, carry):
        base = pl.multiple_of(t * UNROLL, UNROLL)
        for part in range(0, UNROLL, 16):
            rows = [load(base + part + u) for u in range(16)]
            for u in range(16):
                store(base + part + u, rows[u])
        return carry

    lax.fori_loop(0, count // UNROLL, body, 0)


def pack_rows(count, src, src_base, dst, dst_base):
    def body(t, carry):
        r = pl.multiple_of(t * 16, 16)
        for half in range(2):
            dst[pl.ds(dst_base + r, 16), half * LANES : (half + 1) * LANES] = src[
                pl.ds(2 * (src_base + r) + half, 16, stride=2), :
            ].astype(bf16)
        return carry

    lax.fori_loop(0, count // 16, body, 0, unroll=4)


def gather_rows(index, first, count, scale, table, stage, dst, dst_base):
    def pack(at):
        for r in range(0, UNROLL, 16):
            for half in range(2):
                dst[pl.ds(dst_base + at + r, 16), half * LANES : (half + 1) * LANES] = stage[
                    pl.ds(2 * (at + r) + half, 16, stride=2), :
                ].astype(bf16)

    def body(t, carry):
        base = pl.multiple_of(t * UNROLL, UNROLL)
        last = pl.multiple_of(jnp.maximum(t - 1, 0) * UNROLL, UNROLL)
        for part in range(0, UNROLL, 16):
            rows = [
                table[pl.ds(scale * index[first + base + part + u], 2), :] for u in range(16)
            ]
            for u in range(16):
                stage[pl.ds(2 * (base + part + u), 2), :] = rows[u]
        pack(last)
        return carry

    lax.fori_loop(0, count // UNROLL, body, 0)
    pack(count - UNROLL)


def start_table(memory, raw, sem):
    step = memory.shape[0] // CHUNKS
    loads = [
        pltpu.make_async_copy(
            memory.at[pl.ds(c * step, step)], raw.at[pl.ds(c * step, step)], sem.at[c]
        )
        for c in range(CHUNKS)
    ]
    for copy in loads:
        copy.start()
    return loads


def widen_table(loads, raw, table):
    step = raw.shape[0] // len(loads)
    for c in range(len(loads)):
        loads[c].wait()

        def widen(t, carry):
            r = pl.multiple_of(c * step + t * 64, 64)
            rows = raw[pl.ds(r, 64), :].astype(f32)
            for half in range(2):
                table[pl.ds(2 * r + half, 64, stride=2), :] = rows[
                    :, half * LANES : (half + 1) * LANES
                ]
            return carry

        lax.fori_loop(0, step // 64, widen, 0, unroll=2)


def per_peer_rows(src, share, dst):
    group = math.lcm(share, LANES)
    members, depth = group // share, group // LANES
    count = src.shape[0] // depth
    for member in range(members):
        pieces = []
        for at in range(share * member, share * (member + 1)):
            row, lane = divmod(at, LANES)
            if not pieces or lane == 0:
                pieces.append([row, lane, 0])
            pieces[-1][2] += 1
        parts = [
            src[pl.ds(row, count, stride=depth), :][:, lane : lane + size]
            for row, lane, size in pieces
        ]
        room = dst.shape[0] * LANES - share
        if room:
            parts.append(jnp.zeros((count, room), i32))
        line = jnp.concatenate(parts, axis=1)
        for block in range(dst.shape[0]):
            dst[block, pl.ds(member, count, stride=members), :] = line[
                :, block * LANES : (block + 1) * LANES
            ]


def ids_kernel(
    cap,
    nodes,
    target_hbm,
    when_hbm,
    request_hbm,
    counts_hbm,
    out,
    events,
    requests,
    both,
    target,
    when,
    request,
    counts,
    sem,
):
    pairs = (
        (target_hbm, target),
        (when_hbm, when),
        (request_hbm, request),
        (counts_hbm, counts),
    )
    loads = [pltpu.make_async_copy(a, b, sem.at[k]) for k, (a, b) in enumerate(pairs)]
    for copy in loads:
        copy.start()
    for copy in loads:
        copy.wait()
    peers = counts.shape[1]
    both[...] = (target[...] << TIME_BITS) + when[...]
    per_peer_rows(both, cap, events)
    per_peer_rows(request, request.shape[0] * LANES // peers, requests)
    row = lax.broadcasted_iota(i32, (peers, peers), 0)
    lane = lax.broadcasted_iota(i32, (peers, peers), 1)
    live = jnp.sum(
        jnp.where(row == lane, jnp.broadcast_to(counts[...], (peers, peers)), 0).astype(f32),
        axis=1,
        keepdims=True,
    )
    slot = lax.broadcasted_iota(i32, (peers, LANES), 1).astype(f32)
    sent = jnp.where(slot < live, events[0], nodes << TIME_BITS)
    out[:, 0, :LANES] = sent
    for block in range(requests.shape[0]):
        out[:, 0, (block + 1) * LANES : (block + 2) * LANES] = requests[block]


def pack_ids(cap, nodes, evt_dst, evt_time, req_rows, evt_counts):
    peers = evt_counts.shape[1]
    per_peer = req_rows.shape[0] // peers
    blocks = pl.cdiv(per_peer, LANES)
    args = [a.reshape(-1, LANES) for a in (evt_dst, evt_time, req_rows)] + [evt_counts]
    return run(
        functools.partial(ids_kernel, cap, nodes),
        args,
        out_shape=(jax.ShapeDtypeStruct((peers, 1, (1 + blocks) * LANES), i32),),
        in_specs=[HB] * 4,
        out_specs=(VM,),
        scratch_shapes=[
            pltpu.VMEM((1, peers, LANES), i32),
            pltpu.VMEM((blocks, peers, LANES), i32),
            pltpu.VMEM((evt_dst.shape[0] // LANES, LANES), i32),
        ]
        + [pltpu.VMEM(a.shape, i32) for a in args]
        + [pltpu.SemaphoreType.DMA((4,))],
        compiler_params=params(4),
        cost_estimate=cost(0, 1e5),
        name="pack_ids",
    )[0]


def source_kernel(idx_hbm, memory, rows_out, idx, raw, table, stage, in_sem, idx_sem):
    loads = start_table(memory, raw, in_sem)
    idx_load = pltpu.make_async_copy(idx_hbm, idx, idx_sem)
    idx_load.start()
    widen_table(loads, raw, table)
    idx_load.wait()
    gather_rows(idx, 0, idx.shape[0], 2, table, stage, rows_out, 0)


def gather_sources(evt_src, node_memory):
    nodes, width = node_memory.shape
    events = evt_src.shape[0]
    return run(
        source_kernel,
        [evt_src, node_memory],
        out_shape=(jax.ShapeDtypeStruct((events, width), bf16),),
        in_specs=[HB, HB],
        out_specs=(VM,),
        scratch_shapes=[
            pltpu.SMEM(evt_src.shape, i32),
            pltpu.VMEM((nodes, width), bf16),
            pltpu.VMEM((2 * nodes, LANES), f32),
            pltpu.VMEM((2 * events, LANES), f32),
            pltpu.SemaphoreType.DMA((CHUNKS,)),
            pltpu.SemaphoreType.DMA,
        ],
        compiler_params=params(24),
        cost_estimate=cost(0, 20e6),
        name="source_rows",
    )[0]


def prepare_kernel(
    dst_s,
    seen,
    memory,
    dst_row,
    dst_col,
    time_row,
    freq,
    phase,
    msg_hbm,
    mem_hbm,
    bias,
    pre_hbm,
    inv_hbm,
    rows_hbm,
    raw,
    table,
    stage,
    codes,
    msg_weight,
    mem_weight,
    pre_out,
    inv_out,
    rows_out,
    sem,
    out_sem,
    table_sem,
):
    events = dst_s.shape[0]
    width = rows_out.shape[1]
    code_width = freq.shape[0]
    pairs = ((msg_hbm, msg_weight), (mem_hbm, mem_weight))
    loads = [pltpu.make_async_copy(a, b, sem.at[k]) for k, (a, b) in enumerate(pairs)]
    table_loads = start_table(memory, raw, table_sem)
    for copy in loads:
        copy.start()
    target = dst_row[...]
    groups = seen.shape[0]
    at_group = lax.broadcasted_iota(i32, (groups, events), 0) == (target >> 7)
    at_group = jnp.where(at_group, 1.0, 0.0).astype(bf16)
    by_lane = jnp.transpose(seen[...].astype(f32)).astype(i32)
    high = dot((by_lane >> 8).astype(f32).astype(bf16), at_group)
    low = dot((by_lane & 255).astype(f32).astype(bf16), at_group)
    at_lane = lax.broadcasted_iota(i32, (LANES, events), 0) == (target & 127)
    last = jnp.sum(jnp.where(at_lane, 256.0 * high + low, 0.0), axis=0, keepdims=True)
    delta = time_row[...].astype(f32) - last
    for t in range(events // LANES):
        at = pl.ds(t * LANES, LANES)
        part = delta[:, t * LANES : (t + 1) * LANES]
        codes[at, :code_width] = jnp.transpose(cosine(freq[...] * part + phase[...])).astype(bf16)
    codes[:, code_width:] = jnp.ones((events, LANES), bf16)
    widen_table(table_loads, raw, table)
    gather_rows(dst_s, 0, events, 2, table, stage, rows_out, 0)
    for copy in loads:
        copy.wait()
    step = min(ROWS, events)

    def block(t, carry):
        r = pl.multiple_of(t * step, step)
        same = jnp.where(dst_col[pl.ds(r, step), :] == dst_row[...], 1.0, 0.0).astype(bf16)
        sums = dot(same, codes[...])
        inv = 1.0 / jnp.maximum(sums[:, code_width:], 1.0)
        code_agg = (sums[:, :code_width] * inv).astype(bf16)
        inv_out[pl.ds(r, step), :] = inv
        memory = rows_out[pl.ds(r, step), :]
        part = dot(code_agg, msg_weight[pl.ds(width, code_width), :]) + bias[...]
        joined = dot(memory, mem_weight[...])
        third = 3 * width
        pre_out[pl.ds(r, step), : 2 * width] = (
            part[:, : 2 * width] + joined[:, : 2 * width] + joined[:, third : third + 2 * width]
        ).astype(bf16)
        pre_out[pl.ds(r, step), 2 * width : third] = (
            part[:, 2 * width :] + joined[:, 2 * width : third]
        ).astype(bf16)
        pre_out[pl.ds(r, step), third:] = joined[:, third + 2 * width :].astype(bf16)
        return carry

    outs = [(rows_out, rows_hbm), (inv_out, inv_hbm), (pre_out, pre_hbm)]

    def save(k, t):
        r = pl.multiple_of(t * step, step)
        a, b = outs[k]
        return pltpu.make_async_copy(a.at[pl.ds(r, step)], b.at[pl.ds(r, step)], out_sem.at[k, t])

    def run(t, carry):
        block(t, carry)
        for k in range(3):
            save(k, t).start()
        return carry

    lax.fori_loop(0, events // step, run, 0)

    def drain(t, carry):
        for k in range(3):
            save(k, t).wait()
        return carry

    lax.fori_loop(0, events // step, drain, 0)


def prepare(dst, last_update, node_memory, dst_row, dst_col, time_row, freq, phase, msg_weight, mem_weight, bias):
    events = dst.shape[0]
    width = mem_weight.shape[0]
    return run(
        prepare_kernel,
        [dst, last_update, node_memory, dst_row, dst_col, time_row, freq, phase, msg_weight, mem_weight, bias],
        out_shape=(
            jax.ShapeDtypeStruct((events, 4 * width), bf16),
            jax.ShapeDtypeStruct((events, LANES), f32),
            jax.ShapeDtypeStruct((events, width), bf16),
        ),
        in_specs=[SM, VM, HB] + [VM] * 5 + [HB, HB, VM],
        out_specs=(HB, HB, HB),
        scratch_shapes=[
            pltpu.VMEM(node_memory.shape, bf16),
            pltpu.VMEM((2 * node_memory.shape[0], LANES), f32),
            pltpu.VMEM((2 * events, LANES), f32),
            pltpu.VMEM((events, freq.shape[0] + LANES), bf16),
            pltpu.VMEM(msg_weight.shape, bf16),
            pltpu.VMEM(mem_weight.shape, bf16),
            pltpu.VMEM((events, 4 * width), bf16),
            pltpu.VMEM((events, LANES), f32),
            pltpu.VMEM((events, width), bf16),
            pltpu.SemaphoreType.DMA((2,)),
            pltpu.SemaphoreType.DMA((3, events // min(ROWS, events))),
            pltpu.SemaphoreType.DMA((CHUNKS,)),
        ],
        compiler_params=params(48),
        cost_estimate=cost(6e9, 30e6),
        name="prepare",
    )


def update_kernel(
    dst_s,
    req_s,
    qry_s,
    memory,
    got,
    dst_row,
    dst_col,
    pre_hbm,
    inv_hbm,
    rows_hbm,
    msg_hbm,
    found_hbm,
    query_out,
    new_hbm,
    raw,
    table,
    updated,
    new_rows,
    stage,
    packed,
    pre,
    inv,
    rows,
    msg_weight,
    sem,
    block_sem,
    out_sem,
    table_sem,
    new_sem,
):
    events, width = rows.shape
    step = min(ROWS, events)
    blocks = [(rows_hbm, rows), (inv_hbm, inv), (pre_hbm, pre)]

    def fetch(k, t):
        r = pl.multiple_of(t * step, step)
        a, b = blocks[k]
        return pltpu.make_async_copy(a.at[pl.ds(r, step)], b.at[pl.ds(r, step)], block_sem.at[k, t])

    weight_load = pltpu.make_async_copy(msg_hbm.at[pl.ds(0, width)], msg_weight, sem.at[0])
    count = events // step
    share = raw.shape[0] // count

    def put_new(t):
        at = pl.ds(pl.multiple_of(t * step, step), step)
        return pltpu.make_async_copy(new_rows.at[at], new_hbm.at[at], new_sem.at[t])

    def table_load(t):
        r = pl.multiple_of(t * share, share)
        return pltpu.make_async_copy(
            memory.at[pl.ds(r, share)], raw.at[pl.ds(r, share)], table_sem.at[t]
        )

    for k in range(3):
        fetch(k, 0).start()
    weight_load.start()
    if count > 1:
        for k in range(3):
            fetch(k, 1).start()

    def block(t, carry):
        r = pl.multiple_of(t * step, step)
        same = jnp.where(dst_col[pl.ds(r, step), :] == dst_row[...], 1.0, 0.0).astype(bf16)
        sums = dot(same, got[...])
        for k in range(3):
            fetch(k, t).wait()

        @pl.when(t + 2 < count)
        def _():
            for k in range(3):
                fetch(k, t + 2).start()

        @pl.when(t < count // 2)
        def _():
            table_load(2 * t).start()
            table_load(2 * t + 1).start()

        scale = inv[pl.ds(r, step), :]
        agg = jnp.concatenate(
            [sums[:, h * LANES : (h + 1) * LANES] * scale for h in range(width // LANES)], axis=1
        ).astype(bf16)
        msg = dot(agg, msg_weight[...])
        ready = pre[pl.ds(r, step), :].astype(f32)
        reset = jax.nn.sigmoid(msg[:, :width] + ready[:, :width])
        gate = jax.nn.sigmoid(msg[:, width : 2 * width] + ready[:, width : 2 * width])
        cand = jnp.tanh(
            msg[:, 2 * width :] + ready[:, 2 * width : 3 * width] + reset * ready[:, 3 * width :]
        )
        new = (1.0 - gate) * cand + gate * rows[pl.ds(r, step), :].astype(f32)
        new = new.astype(bf16)
        new_rows[pl.ds(r, step), :] = new
        put_new(t).start()
        new = new.astype(f32)
        for half in range(2):
            updated[pl.ds(2 * r + half, step, stride=2), :] = new[:, half * LANES : (half + 1) * LANES]
        return carry

    weight_load.wait()
    lax.fori_loop(0, count, block, 0)
    widen_table([table_load(t) for t in range(count)], raw, table)

    def put_table(k, row):
        table[pl.ds(2 * dst_s[k], 2), :] = row

    move_rows(events, lambda k: updated[pl.ds(2 * k, 2), :], put_table)
    queries = qry_s.shape[0]
    gather_rows(qry_s, 0, queries, 2, table, stage, query_out, 0)
    total = req_s.shape[0]
    chunk = total // SENDS
    sends = []
    for c in range(SENDS):
        gather_rows(req_s, c * chunk, chunk, 1, table, stage, packed, c * chunk)
        send = pltpu.make_async_copy(
            packed.at[pl.ds(c * chunk, chunk)],
            found_hbm.at[pl.ds(c * chunk, chunk)],
            out_sem.at[c],
        )
        send.start()
        sends.append(send)
    for send in sends:
        send.wait()
    for t in range(count):
        put_new(t).wait()


def update(dst, req2, qry_rows, node_memory, got, dst_row, dst_col, pre, inv, rows, msg_weight):
    events, width = got.shape
    queries = qry_rows.shape[0]
    total = req2.shape[0]
    return run(
        update_kernel,
        [dst, req2, qry_rows, node_memory, got, dst_row, dst_col, pre, inv, rows, msg_weight],
        out_shape=(
            jax.ShapeDtypeStruct((total, width), bf16),
            jax.ShapeDtypeStruct((queries, width), bf16),
            jax.ShapeDtypeStruct((events, width), bf16),
        ),
        in_specs=[SM, SM, SM, HB, VM, VM, VM, HB, HB, HB, HB],
        out_specs=(HB, VM, HB),
        scratch_shapes=[
            pltpu.VMEM(node_memory.shape, bf16),
            pltpu.VMEM((2 * node_memory.shape[0] + 16, LANES), f32),
            pltpu.VMEM((2 * events, LANES), f32),
            pltpu.VMEM((events, width), bf16),
            pltpu.VMEM((2 * max(total // SENDS, queries), LANES), f32),
            pltpu.VMEM((total, width), bf16),
            pltpu.VMEM(pre.shape, bf16),
            pltpu.VMEM(inv.shape, f32),
            pltpu.VMEM(rows.shape, bf16),
            pltpu.VMEM((width, msg_weight.shape[1]), bf16),
            pltpu.SemaphoreType.DMA((1,)),
            pltpu.SemaphoreType.DMA((3, events // min(ROWS, events))),
            pltpu.SemaphoreType.DMA((SENDS,)),
            pltpu.SemaphoreType.DMA((events // min(ROWS, events),)),
            pltpu.SemaphoreType.DMA((events // min(ROWS, events),)),
        ],
        compiler_params=params(44),
        cost_estimate=cost(4e9, 40e6),
        name="update",
    )


def write_back_kernel(dst_s, memory, new_hbm, memory_out, raw, new, table, updated, sem, new_sem):
    loads = start_table(memory, raw, sem)
    new_load = pltpu.make_async_copy(new_hbm, new, new_sem)
    new_load.start()
    widen_table(loads, raw, table)
    new_load.wait()
    events = new.shape[0]

    def spread(t, carry):
        r = pl.multiple_of(t * 64, 64)
        rows = new[pl.ds(r, 64), :].astype(f32)
        for half in range(2):
            updated[pl.ds(2 * r + half, 64, stride=2), :] = rows[:, half * LANES : (half + 1) * LANES]
        return carry

    lax.fori_loop(0, events // 64, spread, 0)

    def put(k, row):
        table[pl.ds(2 * dst_s[k], 2), :] = row

    move_rows(events, lambda k: updated[pl.ds(2 * k, 2), :], put)
    share = raw.shape[0] // CHUNKS
    saves = []
    for c in range(CHUNKS):
        pack_rows(share, table, c * share, raw, c * share)
        save = pltpu.make_async_copy(
            raw.at[pl.ds(c * share, share)], memory_out.at[pl.ds(c * share, share)], sem.at[c]
        )
        save.start()
        saves.append(save)
    for save in saves:
        save.wait()


def write_back(dst, node_memory, new):
    nodes, _ = node_memory.shape
    events = new.shape[0]
    return run(
        write_back_kernel,
        [dst, node_memory, new],
        out_shape=(jax.ShapeDtypeStruct(node_memory.shape, bf16),),
        in_specs=[SM, HB, HB],
        out_specs=(HB,),
        scratch_shapes=[
            pltpu.VMEM(node_memory.shape, bf16),
            pltpu.VMEM(new.shape, bf16),
            pltpu.VMEM((2 * nodes + 16, LANES), f32),
            pltpu.VMEM((2 * events, LANES), f32),
            pltpu.SemaphoreType.DMA((CHUNKS,)),
            pltpu.SemaphoreType.DMA,
        ],
        compiler_params=params(32),
        cost_estimate=cost(0, 20e6),
        name="write_back",
    )[0]


def invert_kernel(slots, values, out):
    total = slots.shape[1]
    high = total // LANES
    where = slots[...]
    rows = lax.broadcasted_iota(i32, (high, total), 0)
    at_row = rows == (where >> 7)
    lanes = lax.broadcasted_iota(i32, (LANES, total), 0)
    at_lane = jnp.where(lanes == (where & 127), 1.0, 0.0).astype(bf16)
    result = jnp.zeros((high, LANES), i32)
    for digit in range(3):
        part = ((values[...] >> (8 * digit)) & 255).astype(f32)
        spread = jnp.where(at_row, part, 0.0).astype(bf16)
        result = result + (dot_nt(spread, at_lane).astype(i32) << (8 * digit))
    out[...] = result


def invert(slots, values):
    total = slots.shape[1]
    return run(
        invert_kernel,
        [slots, values],
        out_shape=(jax.ShapeDtypeStruct((total // LANES, LANES), i32),),
        in_specs=[VM, VM],
        out_specs=(VM,),
        compiler_params=params(24),
        cost_estimate=cost(1e9, 5e6),
        name="invert",
    )[0]


def project_kernel(
    shift,
    query,
    info,
    freq,
    phase,
    query_weight,
    kv_weight,
    qx_hbm,
    et_hbm,
    se_hbm,
    qx,
    et,
    se,
    sem,
):
    width = query_weight.shape[0]
    head_dim = width // HEADS
    queries = query.shape[0]
    step = 256
    slots = info.shape[1]
    who = info[...] & ((1 << shift) - 1)
    delta = ((info[...] >> shift) - (1 << TIME_BITS)).astype(f32)
    for t in range(slots // step):
        part = delta[:, t * step : (t + 1) * step]
        et[:, pl.ds(t * step, step)] = cosine(freq[...] * part + phase[...]).astype(bf16)
    mask = lax.broadcasted_iota(i32, (queries, slots), 0) == who
    vec = dot(query[...], query_weight[...]) * (1.0 / math.sqrt(head_dim))
    for h in range(HEADS):
        high, low = split(vec[:, h * head_dim : (h + 1) * head_dim])
        keys = kv_weight[:, h * head_dim : (h + 1) * head_dim]
        folded = dot_nt(high, keys) + dot_nt(low, keys)
        high, low = split(folded)
        rows = pl.ds(2 * h * queries, queries)
        qx[rows, :] = high[:, :width]
        qx[pl.ds((2 * h + 1) * queries, queries), :] = low[:, :width]
        scores = dot(high[:, width:], et[...]) + dot(low[:, width:], et[...])
        se[pl.ds(h * queries, queries), :] = jnp.where(mask, scores, NEG)
    pairs = ((qx, qx_hbm), (et, et_hbm), (se, se_hbm))
    copies = [pltpu.make_async_copy(a, b, sem.at[k]) for k, (a, b) in enumerate(pairs)]
    for copy in copies:
        copy.start()
    for copy in copies:
        copy.wait()


def project(shift, query, info, freq, phase, query_weight, kv_weight):
    queries, width = query.shape
    slots = info.shape[1]
    outs = (
        jax.ShapeDtypeStruct((2 * HEADS * queries, width), bf16),
        jax.ShapeDtypeStruct((freq.shape[0], slots), bf16),
        jax.ShapeDtypeStruct((HEADS * queries, slots), f32),
    )
    return run(
        functools.partial(project_kernel, shift),
        [query, info, freq, phase, query_weight, kv_weight],
        out_shape=outs,
        in_specs=[VM] * 6,
        out_specs=(HB, HB, HB),
        scratch_shapes=[pltpu.VMEM(o.shape, o.dtype) for o in outs] + [pltpu.SemaphoreType.DMA((3,))],
        compiler_params=params(32),
        cost_estimate=cost(1e9, 10e6),
        name="project",
    )


def attend_kernel(
    sub,
    got,
    qx_hbm,
    et_hbm,
    se_hbm,
    kv_hbm,
    part_out,
    lse_out,
    qx,
    et,
    se,
    kv_weight,
    sem,
    se_sem,
):
    owners, both, width = got.shape
    per_peer = both // 2
    slots = owners * per_peer
    queries = qx.shape[0] // (2 * HEADS)
    head_dim = width // HEADS
    pairs = ((qx_hbm, qx), (et_hbm, et), (kv_hbm, kv_weight))
    copies = [pltpu.make_async_copy(a, b, sem.at[k]) for k, (a, b) in enumerate(pairs)]

    def load_se(h):
        at = pl.ds(h * queries, queries)
        return pltpu.make_async_copy(se_hbm.at[at], se.at[at], se_sem.at[h])

    for copy in copies:
        copy.start()
    for h in range(HEADS):
        load_se(h).start()
    rows = got[:, sub * per_peer : (sub + 1) * per_peer, :].reshape(slots, width)
    logs = []
    for h in range(HEADS):
        if h == 0:
            copies[0].wait()
        both_parts = dot_nt(qx[pl.ds(2 * h * queries, 2 * queries), :], rows)
        load_se(h).wait()
        scores = both_parts[:queries] + both_parts[queries:] + se[pl.ds(h * queries, queries), :]
        top = jnp.maximum(jnp.max(scores, axis=1, keepdims=True), 0.1 * NEG)
        weights = jnp.exp(scores - top).astype(bf16)
        total = jnp.sum(weights.astype(f32), axis=1, keepdims=True)
        some = total > 0.0
        inv = jnp.where(some, 1.0 / jnp.where(some, total, 1.0), 0.0)
        logs.append(jnp.where(some, top + jnp.log(jnp.where(some, total, 1.0)), NEG))
        if h == 0:
            copies[1].wait()
            copies[2].wait()
        mem_high, mem_low = split(dot(weights, rows) * inv)
        code_high, code_low = split(dot_nt(weights, et[...]) * inv)
        lanes = slice(width + h * head_dim, width + (h + 1) * head_dim)
        value_mem = kv_weight[:width, lanes]
        value_code = kv_weight[width:, lanes]
        part = dot(mem_high, value_mem) + dot(mem_low, value_mem)
        part = part + dot(code_high, value_code) + dot(code_low, value_code)
        part_out[:, h * head_dim : (h + 1) * head_dim] = part.astype(part_out.dtype)
    lane = lax.broadcasted_iota(i32, (queries, LANES), 1)
    spread = jnp.where((lane & 7) < 4, logs[0], logs[1])
    lse_out[...] = jnp.transpose(spread)[:8, :]


def attend(sub, got, qx, et, se, kv_weight, kind, name):
    queries = qx.shape[0] // (2 * HEADS)
    width = got.shape[2]
    return run(
        functools.partial(attend_kernel, sub),
        [got, qx, et, se, kv_weight],
        out_shape=(
            jax.ShapeDtypeStruct((queries, width), kind),
            jax.ShapeDtypeStruct((8, queries), f32),
        ),
        in_specs=[VM, HB, HB, HB, HB],
        out_specs=(VM, VM),
        scratch_shapes=[pltpu.VMEM(a.shape, a.dtype) for a in (qx, et, se, kv_weight)]
        + [pltpu.SemaphoreType.DMA((3,)), pltpu.SemaphoreType.DMA((HEADS,))],
        compiler_params=params(40),
        cost_estimate=cost(4e9, 10e6),
        name=name,
    )


def merge_kernel(mine, mine_lse, other, other_lse, query, out_weight, out):
    queries, width = mine.shape
    head_dim = width // HEADS
    pieces = []
    for h in range(HEADS):
        lanes = slice(h * head_dim, (h + 1) * head_dim)
        lse_a = jnp.transpose(jnp.broadcast_to(mine_lse[pl.ds(4 * h, 1), :], (LANES, queries)))
        lse_b = jnp.transpose(jnp.broadcast_to(other_lse[pl.ds(4 * h, 1), :], (LANES, queries)))
        top = jnp.maximum(lse_a, lse_b)
        weight_a = jnp.exp(lse_a - top)
        weight_b = jnp.exp(lse_b - top)
        inv = 1.0 / (weight_a + weight_b)
        pieces.append(
            mine[:, lanes] * (weight_a * inv) + other[:, lanes].astype(f32) * (weight_b * inv)
        )
    attended = jnp.concatenate(pieces, axis=1).astype(bf16)
    result = dot(attended, out_weight[:width, :]) + dot(query[...], out_weight[width:, :])
    out[...] = result.astype(bf16)


def merge(mine, mine_lse, other, other_lse, query, out_weight):
    return pl.pallas_call(
        merge_kernel,
        out_shape=jax.ShapeDtypeStruct(query.shape, bf16),
        in_specs=[VM] * 6,
        out_specs=VM,
        compiler_params=params(8),
        cost_estimate=cost(1e8, 1e6),
        name="merge",
    )(mine, mine_lse, other, other_lse, query, out_weight)


def local(
    group_count,
    mem_count,
    node_memory,
    last_update,
    evt_src,
    evt_dst,
    evt_time,
    evt_counts,
    time_freq,
    time_phase,
    msg_weight,
    mem_weight,
    gru_bias,
    qry_rows,
    qry_time,
    nbr_time,
    nbr_slot,
    req_rows,
    query_weight,
    kv_weight,
    out_weight,
):
    peers = group_count * mem_count
    side_peers = peers // 2
    half_groups = group_count // 2
    nodes, width = node_memory.shape
    events = evt_src.shape[0]
    cap = events // peers
    queries, fan_out = nbr_time.shape
    total_slots = queries * fan_out
    per_peer = total_slots // peers
    side_slots = side_peers * per_peer
    shift = (queries - 1).bit_length()
    side = lax.axis_index("grp") // half_groups
    sides = [list(range(s * side_peers, (s + 1) * side_peers)) for s in range(2)]
    opposite = [(g, (g + half_groups) % group_count) for g in range(group_count)]

    def mine_other(pair):
        return jnp.where(side == 0, pair[0], pair[1]), jnp.where(side == 0, pair[1], pair[0])

    ids = pack_ids(cap, nodes, evt_dst, evt_time, req_rows, evt_counts)
    got_ids = lax.all_to_all(ids, AXES, split_axis=0, concat_axis=0, tiled=True)[:, 0]
    sent_rows = gather_sources(evt_src, node_memory)
    got_rows = lax.all_to_all(
        sent_rows.reshape(peers, cap, width), AXES, split_axis=0, concat_axis=0, tiled=True
    )
    got_rows = got_rows.reshape(events, width)
    qry_time, time_freq, time_phase, gru_bias, got_ids = lax.optimization_barrier(
        (qry_time, time_freq, time_phase, gru_bias, got_ids)
    )

    packed = got_ids[:, :cap].reshape(events)
    dst = packed >> TIME_BITS
    time_row = (packed & ((1 << TIME_BITS) - 1)).reshape(1, events)
    dst_row = jnp.where(dst < nodes, dst, -1).reshape(1, events)
    dst_col = dst.reshape(events, 1)
    mine, other = mine_other(got_ids[:, LANES : LANES + per_peer].reshape(2, side_peers, per_peer))
    req2 = 2 * jnp.concatenate([mine, other], axis=1).reshape(total_slots)
    freq = time_freq.reshape(-1, 1)
    phase = time_phase.reshape(-1, 1)
    bias = gru_bias.reshape(1, -1)
    delta = qry_time[:, None] - nbr_time + (1 << TIME_BITS)
    values = (delta << shift) + jnp.arange(queries, dtype=i32)[:, None]
    info = invert(nbr_slot, values.reshape(1, total_slots))
    info_mine, info_send = mine_other(info.reshape(2, 1, side_slots))
    req2, info_send = lax.optimization_barrier((req2, info_send))
    info_other = lax.ppermute(info_send, "grp", opposite)
    pre, inv, rows = prepare(
        jnp.minimum(dst, nodes - 1),
        last_update.reshape(-1, LANES),
        node_memory,
        dst_row,
        dst_col,
        time_row,
        freq,
        phase,
        msg_weight,
        mem_weight,
        bias,
    )
    found, query_mem, new_rows = update(
        dst, req2, qry_rows, node_memory, got_rows, dst_row, dst_col, pre, inv, rows, msg_weight
    )
    query_other = lax.ppermute(query_mem, "grp", opposite)
    got = lax.all_to_all(
        found.reshape(side_peers, 2 * per_peer, width),
        AXES,
        split_axis=0,
        concat_axis=0,
        tiled=True,
        axis_index_groups=sides,
    )
    new_memory = write_back(dst, node_memory, new_rows)

    args = (freq, phase, query_weight, kv_weight)
    other = project(shift, query_other, info_other, *args)
    own = project(shift, query_mem, info_mine, *args)
    part_b, lse_b = attend(1, got, *other, kv_weight, bf16, "attend_other")
    back, back_lse = lax.ppermute(part_b, "grp", opposite), lax.ppermute(lse_b, "grp", opposite)
    part_a, lse_a = attend(0, got, *own, kv_weight, f32, "attend_mine")
    embeddings = merge(part_a, lse_a, back, back_lse, query_mem, out_weight)
    return new_memory, embeddings


def solution(mesh):
    split_rows = P(AXES, None)
    split_flat = P(AXES)
    in_specs = (
        split_rows,
        split_flat,
        split_flat,
        split_flat,
        split_flat,
        split_rows,
        P(),
        P(),
        P(),
        P(),
        P(),
        split_flat,
        split_flat,
        split_rows,
        split_rows,
        split_flat,
        P(),
        P(),
        P(),
    )
    body = functools.partial(local, mesh.shape["grp"], mesh.shape["mem"])
    return jax.shard_map(
        body, mesh=mesh, in_specs=in_specs, out_specs=(split_rows, split_rows), check_vma=False
    )
```
